128 devices in a mesh: rows: 16 (over x, z_hi, core), cols: 8 (over y, z_lo).
Axes of the slice: x: 4, y: 4, z: 4 (z_hi: 2, z_lo: 2; z = z_hi * 2 + z_lo), core: 2. Of those that a mesh axis runs over, the one named last changes fastest.
Arguments:
- values: float32 [256, 64, 32, 128], P(None, 'rows', 'cols'), may hold values from -6 to 6
- offsets: float32 [2, 64, 32, 128], P(None, 'rows', 'cols'), may hold values from 0 to 1
- nugget: float32 [64, 32, 128], P('rows', 'cols'), may hold values from 0.8 to 2.5
- neighbours: int32 [64, 32, 256], P('rows', 'cols'), may hold values from 0 to 262143, as said below
- length_scale: float32 [1], replicated, may hold values from 2.5 to 5
- target_tile: int32 [65536, 1], P(('rows', 'cols')), may hold values from 0 to 15; in each aligned block of 512 rows (0 to 511, 512 to 1023, ...) at most 64 rows name the same one
- target_spots: float32 [2, 65536], P(None, ('rows', 'cols')), may hold values from 0 to 1
Outputs:
- whitened: float32 [64, 32, 128, 256], P('rows', 'cols')
- cluster_terms: float32 [64, 32], P('rows', 'cols')
- predictions: float32 [65536, 256], P(('rows', 'cols'))
The draws below stay inside these ranges and needn't reach their ends.
Inputs may be any that keep to these rules, and one draw needn't show every extreme that they name: `neighbours`: each cluster's 256 entries are distinct points of other clusters whose two grid coordinates each differ from the cluster's own by at most 2. `target_tile`: at most 64 of the 512 targets of one device name the same tile, and in every draw some tile is named exactly 64 times by the targets of some device.
All inputs are finite; a program needn't handle non-finite values.
Results may differ from the reference program's by a relative error of at most 0.0052.
Values may be sent and summed in bfloat16 or wider, within the bound.
No kernel may reach another device: no remote copies, remote signals or barrier semaphores. Data moves between devices by JAX's collectives and lax.ppermute only.
A program may use at most 256 MiB of HBM per device.

```python
import math
import jax
import jax.numpy as jnp
import numpy as np
from jax import lax

CLX = 4
BLOCK = 128
NEIGH = 256
HALO = 2
REPS = 256
TGT_DEV = 512
GX = 64
GY = 32
POINTS = 262144
ORDER = 384
TILES = 16
CAP = 64
TARGETS = 65536
SLAB = 16384
N_ROWS = 16
N_COLS = 8


def draw_neighbours(key, part):
    offset_pairs = [(along_x, second) for along_x in range(-HALO, HALO + 1) for second in range(-HALO, HALO + 1) if along_x != 0 or second != 0]
    shift_x = jnp.asarray(np.array([offset_pair[0] for offset_pair in offset_pairs], dtype=np.int32))
    shift_y = jnp.asarray(np.array([offset_pair[1] for offset_pair in offset_pairs], dtype=np.int32))
    offset_total = len(offset_pairs)
    grid_rows = jnp.arange(GX, dtype=jnp.int32)[:, None, None]
    grid_cols = jnp.arange(GY, dtype=jnp.int32)[None, :, None]
    cells_x = grid_rows + shift_x[None, None, :]
    cells_y = grid_cols + shift_y[None, None, :]
    inside = (cells_x >= 0) & (cells_x < GX) & (cells_y >= 0) & (cells_y < GY)
    scores = jax.random.randint(key, (GX, GY, offset_total, BLOCK), 0, 2 ** 18, dtype=jnp.int32)
    labels = jnp.arange(offset_total * BLOCK, dtype=jnp.int32).reshape(offset_total, BLOCK)
    scores = scores * 4096 + labels[None, None]
    scores = jnp.where(inside[..., None], scores, -1).reshape(GX, GY, offset_total * BLOCK)
    ignored, chosen = lax.top_k(scores, NEIGH)
    chosen_cell = chosen // BLOCK
    member = chosen % BLOCK
    near_x = grid_rows + jnp.take(shift_x, chosen_cell)
    near_y = grid_cols + jnp.take(shift_y, chosen_cell)
    return ((near_x * GY + near_y) * BLOCK + member).astype(jnp.int32)


def levels(key, dims, shards, least, largest):
    factor_of = 1.0
    for axis_at, shards_of in shards:
        draws = jax.random.uniform(jax.random.fold_in(jax.random.fold_in(key, 6), axis_at), (shards_of,), jnp.float32, least / len(shards), largest / len(shards))
        factor_of = factor_of * jnp.repeat(jnp.exp(draws), dims[axis_at] // shards_of).reshape((-1,) + (1,) * (len(dims) - 1 - axis_at))
    return factor_of


def deal_out(key, own, number, rows, amount, top, reach, lean):
    order = jax.random.permutation(key, amount)
    heavy_load, common = load_shares(amount, rows * top, reach, lean, True), load_shares(amount, rows * top, reach, lean, False)
    places = jnp.arange(amount)

    def named(sizes, offset_by):
        used = int((sizes > 0).sum())
        fixed = max(1, used // 4)
        shifted = fixed + (places - fixed + offset_by * (used - fixed)) % max(1, amount - fixed)
        return jnp.zeros((amount,), jnp.int32).at[order[jnp.where(places < fixed, places, shifted)]].set(jnp.asarray(sizes, jnp.int32))

    sizes = jnp.where(number % 4 == 0, named(heavy_load, number // 4), named(common, number - number // 4 - 1))
    mixed = jax.random.permutation(jax.random.fold_in(own, 3), amount)
    source_of, sink = mixed[0:amount // 2 * 2:2], mixed[1:amount // 2 * 2:2]
    slack = jnp.minimum(sizes[source_of] - 1, reach - sizes[sink]) // 2
    slack = jnp.where((source_of == order[0]) | (sink == order[0]) | (sizes[sink] == 0), 0, jnp.maximum(slack, 0))
    shifted = jax.random.randint(jax.random.fold_in(own, 4), (amount // 2,), 0, 1 << 20) % (slack + 1)
    sizes = sizes.at[source_of].add(-shifted).at[sink].add(shifted)
    items = jnp.searchsorted(jnp.cumsum(sizes), jnp.arange(rows * top), side="right").astype(jnp.int32)
    table = items.reshape(top, rows).T
    table = table[jax.random.permutation(jax.random.fold_in(own, 1), rows)]
    offset_by = jax.random.randint(jax.random.fold_in(own, 2), (rows, 1), 0, top)
    return jnp.take_along_axis(table, (jnp.arange(top)[None, :] + offset_by) % top, axis=1)


def load_shares(count, total, most, slope, full):
    portions = [(1 << 20) // math.isqrt(standing ** slope) + 1 for standing in range(1, count + 1)]
    largest = most if full else min(most, max(-(-total // count), total * portions[0] // sum(portions)))
    least = 1 if total - largest >= count - 1 else 0
    counts, spare = [largest] + [least] * (count - 1), total - largest - least * (count - 1)
    while spare > 0:
        free = [i for i in range(1, count) if counts[i] < largest] or [i for i in range(1, count) if counts[i] < most]
        pool, budget = sum([portions[i] for i in free]), spare
        for i in free:
            addition = min(most - counts[i], max(1, budget * portions[i] // pool), spare)
            counts[i] = counts[i] + addition
            spare = spare - addition
    return np.array(counts)


def scatter_about(stream_key, dims, scale, most, split=(), held_as=jnp.bfloat16):
    level = levels(stream_key, dims, split, -0.22, 0.18) if split else 1.0
    drawn = jax.random.normal(stream_key, dims, jnp.float32) * scale * level
    return jnp.minimum(jnp.maximum(drawn, -most), most).astype(held_as)


def setup_inputs(seed: int = 0) -> dict:
    key_list = jax.random.split(jax.random.key(seed), 8)
    values = scatter_about(key_list[0], (REPS, GX, GY, BLOCK), 1.0, 6.0, ((1, 16), (2, 8)), jnp.float32)
    offsets = jnp.clip(1.0 * jax.random.uniform(key_list[1], (2, GX, GY, BLOCK), jnp.float32) ** levels(key_list[1], (2, GX, GY, BLOCK), ((1, 16), (2, 8)), -0.2, 0.2), 0.0, 1.0)
    nugget = jnp.clip(jnp.exp(math.log(2.5) - 1.13943427 * jax.random.uniform(key_list[2], (GX, GY, BLOCK), jnp.float32) ** levels(key_list[2], (GX, GY, BLOCK), ((0, 16), (1, 8)), -0.2, 0.2)), 0.8, 2.5)
    neighbours = draw_neighbours(jax.random.fold_in(key_list[7], 71), 0)
    length_scale = jnp.clip(jax.random.uniform(key_list[4], (1,), jnp.float32, 2.5, 5.0), 2.5, 5.0)
    target_tile_keys = jax.random.split(jax.random.fold_in(key_list[5], 1), TARGETS // TGT_DEV)
    target_tile_turns = jax.random.permutation(jax.random.fold_in(key_list[5], 3), TARGETS // TGT_DEV)
    target_tile = jax.vmap(lambda own, number: deal_out(jax.random.fold_in(key_list[5], 2), own, number, TGT_DEV, TILES, 1, CAP, 2))(target_tile_keys, target_tile_turns).reshape((TARGETS, 1))
    target_spots = jnp.clip(1.0 * jax.random.uniform(key_list[6], (2, TARGETS), jnp.float32) ** levels(key_list[6], (2, TARGETS), ((1, 128),), -0.2, 0.2), 0.0, 1.0)
    return dict(values=values, offsets=offsets, nugget=nugget, neighbours=neighbours, length_scale=length_scale, target_tile=target_tile, target_spots=target_spots)


root_three = math.sqrt(3.0)

def matern(distances, length):
    scaled = root_three * distances / length
    return (1.0 + scaled) * jnp.exp(-scaled)

def cluster_work(point_data, reps, neigh, length):
    place_x = point_data[reps]
    place_y = point_data[reps + 1]
    noise_row = point_data[reps + 2]
    distances = jnp.sqrt((place_x[:, None] - place_x[None, :]) ** 2 + (place_y[:, None] - place_y[None, :]) ** 2)
    covariance = matern(distances, length) + jnp.diag(noise_row)
    factor = jnp.linalg.cholesky(covariance)
    white_all = jax.scipy.linalg.solve_triangular(factor, point_data[:reps].T, lower=True)
    tail_rows = white_all[neigh:]
    log_diag = jnp.log(jnp.diagonal(factor)[neigh:])
    total_count = tail_rows.shape[0] * reps
    cluster_term = -(0.5 * jnp.sum(tail_rows * tail_rows) + reps * jnp.sum(log_diag)) / total_count - 0.5 * math.log(2.0 * math.pi)
    return (tail_rows, cluster_term)

def cross_exact(target_x, target_y, point_x, point_y, weights, length, factor_scale):
    target_total = target_x.shape[0]
    point_total = point_x.shape[0]
    reps = weights.shape[1]
    target_step = math.gcd(target_total, 512)
    point_step = math.gcd(point_total, 4096)
    blocks_x = point_x.reshape(-1, point_step)
    blocks_y = point_y.reshape(-1, point_step)
    blocks_w = weights.reshape(-1, point_step, reps)

    def one_block(target_pair):
        rows_x, rows_y = target_pair

        def add_points(running, point_set):
            cols_x, cols_y, cols_w = point_set
            distances = jnp.sqrt((rows_x[:, None] - cols_x[None, :]) ** 2 + (rows_y[:, None] - cols_y[None, :]) ** 2)
            kernel_bf = matern(distances, length).astype(jnp.bfloat16)
            product = jnp.dot(kernel_bf.astype(jnp.float32), cols_w.astype(jnp.float32), precision=lax.Precision.HIGHEST)
            return (running + product, None)
        summed, ignored = lax.scan(add_points, jnp.zeros((target_step, reps), jnp.float32), (blocks_x, blocks_y, blocks_w))
        return summed * factor_scale
    mapped = lax.map(one_block, (target_x.reshape(-1, target_step), target_y.reshape(-1, target_step)))
    return mapped.reshape(target_total, reps)

def reference(values, offsets, nugget, neighbours, length_scale, target_tile, target_spots):
    length = length_scale[0]
    cell_x = jnp.arange(GX, dtype=jnp.int32).astype(jnp.float32)
    cell_y = jnp.arange(GY, dtype=jnp.int32).astype(jnp.float32)
    place_x = offsets[0] + cell_x[:, None, None]
    place_y = offsets[1] + cell_y[None, :, None]
    flat_x = place_x.reshape(-1)
    flat_y = place_y.reshape(-1)
    flat_values = values.reshape(REPS, -1)
    flat_nugget = nugget.reshape(-1)
    cluster_ids = jnp.arange(GX * GY, dtype=jnp.int32)
    own_pos = cluster_ids[:, None] * BLOCK + jnp.arange(BLOCK, dtype=jnp.int32)[None, :]
    all_pos = jnp.concatenate([neighbours.reshape(-1, NEIGH).astype(jnp.int32), own_pos], axis=1)
    group_size = 32

    def run_cluster(point_data):
        return cluster_work(point_data, REPS, NEIGH, length)

    def per_group(positions):
        point_data = jnp.concatenate([flat_values[:, positions], flat_x[positions][None], flat_y[positions][None], flat_nugget[positions][None]], axis=0)
        return jax.vmap(run_cluster, in_axes=1)(point_data)
    tails, terms = lax.map(per_group, all_pos.reshape(-1, group_size, ORDER))
    whitened = tails.reshape(GX, GY, BLOCK, REPS)
    cluster_terms = terms.reshape(GX, GY)
    weights = whitened.reshape(POINTS, REPS).astype(jnp.bfloat16)
    device_total = N_ROWS * N_COLS
    tile_ids = target_tile[:, 0].astype(jnp.int32)
    one_hot = (tile_ids[:, None] == jnp.arange(TILES, dtype=jnp.int32)[None, :]).astype(jnp.int32)
    per_device = one_hot.reshape(device_total, TGT_DEV, TILES)
    rank_in_tile = lax.optimization_barrier(jnp.sum((jnp.cumsum(per_device, axis=1) - 1) * per_device, axis=2)).reshape(-1)
    device_ids = jnp.arange(TARGETS, dtype=jnp.int32) // TGT_DEV
    slot_index = tile_ids * (device_total * CAP) + device_ids * CAP + rank_in_tile
    spot_x = (tile_ids.astype(jnp.float32) + target_spots[0]) * CLX
    spot_y = target_spots[1] * GY
    padded_x = jnp.zeros((TILES * device_total * CAP,), jnp.float32).at[slot_index].set(spot_x)
    padded_y = jnp.zeros((TILES * device_total * CAP,), jnp.float32).at[slot_index].set(spot_y)
    inv_root = 1.0 / math.sqrt(SLAB)

    def per_tile(tile_pack):
        tile_number, rows_x, rows_y = tile_pack
        start_point = tile_number * SLAB
        slab_x = lax.dynamic_slice_in_dim(flat_x, start_point, SLAB)
        slab_y = lax.dynamic_slice_in_dim(flat_y, start_point, SLAB)
        slab_w = lax.dynamic_slice_in_dim(weights, start_point, SLAB, 0)
        return cross_exact(rows_x, rows_y, slab_x, slab_y, slab_w, length, inv_root)
    padded = lax.map(per_tile, (jnp.arange(TILES, dtype=jnp.int32), padded_x.reshape(TILES, -1), padded_y.reshape(TILES, -1)))
    predictions = padded.reshape(-1, REPS)[slot_index]
    return (whitened, cluster_terms, predictions)
```

```python
import math

import jax
import jax.numpy as jnp

from jax import lax
from jax.experimental import pallas as pl
from jax.experimental.pallas import tpu as pltpu
from jax.sharding import PartitionSpec as P

F32 = jnp.float32
BF = jnp.bfloat16
NN = (((1,), (0,)), ((), ()))
NT = (((1,), (1,)), ((), ()))
TN = (((0,), (0,)), ((), ()))


def split(x):
    hi = x.astype(BF)
    return hi, (x - hi.astype(F32)).astype(BF)


def dot(a, b, dims):
    return lax.dot_general(a, b, dims, preferred_element_type=F32)


def mm_nt(a, b):
    ah, al = split(a)
    bh, bl = split(b)
    return dot(jnp.concatenate([ah, ah, al], 1), jnp.concatenate([bh, bl, bh], 1), NT)


def mm_nn(a, b):
    ah, al = split(a)
    bh, bl = split(b)
    return dot(jnp.concatenate([ah, ah, al], 1), jnp.concatenate([bh, bl, bh], 0), NN)


def lane_take(x, idx):
    return jnp.take_along_axis(x, idx, axis=1, mode="promise_in_bounds")


def recip(p):
    r = pl.reciprocal(p, approx=True)
    return r * (2.0 - p * r)


def leaf_factor(leaf, lane, sub):
    base = lane & 96
    col = lane & 31
    x = [list(p) for p in leaf]
    piv = [[jnp.ones((8, 128), F32) for _ in range(4)] for _ in range(4)]
    for j in range(32):
        v0, s0 = divmod(j, 8)
        idx = base + j
        unit = jnp.where(col == j, 1.0, 0.0)
        below = sub > s0
        here = sub == s0
        for p in range(4):
            row = jnp.broadcast_to(x[p][v0][s0 : s0 + 1, :], (8, 128))
            d = lane_take(row, idx)
            r = recip(d)
            piv[p][v0] = jnp.where(here, d, piv[p][v0])
            rowp = row + unit
            for v in range(v0, 4):
                if v == v0 and s0 == 7:
                    continue
                c = lane_take(x[p][v], idx)
                if v == v0:
                    c = jnp.where(below, c, 0.0)
                x[p][v] = x[p][v] - (c * rowp) * r
    out = []
    for p in range(4):
        o = []
        for v in range(4):
            q = lax.rsqrt(piv[p][v])
            q = q * (1.5 - 0.5 * piv[p][v] * q * q)
            r_i = sub + 8 * v
            o.append(q * jnp.where(col < r_i, x[p][v], jnp.where(col == r_i, 1.0, 0.0)))
        out.append(o)
    return out


def inv_chol(xw, wp, count):
    lane8 = lax.broadcasted_iota(jnp.int32, (8, 128), 1)
    sub8 = lax.broadcasted_iota(jnp.int32, (8, 128), 0)
    lane = lax.broadcasted_iota(jnp.int32, (32, 128), 1)
    subl = lax.broadcasted_iota(jnp.int32, (32, 128), 0)
    for k in range(4):
        lo = 32 * k
        for base in range(0, count, 16):
            leaf = []
            for p in range(4):
                tiles = []
                for v in range(4):
                    acc = None
                    for g in range(4):
                        t = xw[base + 4 * p + g, lo + 8 * v : lo + 8 * v + 8, :]
                        t = pltpu.roll(t, (32 * (g - k)) % 128, axis=1) if g != k else t
                        acc = t if acc is None else jnp.where(lane8 // 32 == g, t, acc)
                    tiles.append(acc)
                leaf.append(tiles)
            inv = leaf_factor(leaf, lane8, sub8)
            for p in range(4):
                for v in range(4):
                    wp[p, 8 * v : 8 * v + 8, :] = inv[p][v]

            def apply(p, _):
                for g in range(4):
                    c = base + 4 * p + g
                    gi = 32 * g + (lane8 & 31)
                    wr = jnp.concatenate(
                        [lane_take(wp[p, 8 * v : 8 * v + 8, :], gi) for v in range(4)], 0
                    )
                    wh = wr.astype(BF).astype(F32)
                    lhs = jnp.where(lane < 64, wh, wr - wh).astype(BF)
                    r = xw[c, lo : lo + 32, :]
                    r = jnp.where(lane // 32 == k, jnp.where((lane & 31) == subl, 1.0, 0.0), r)
                    rh, rl = split(r)
                    t = dot(lhs, jnp.concatenate([rh, rl, rh, rl], 0), NN)
                    xw[c, lo : lo + 32, :] = jnp.where(lane < lo + 32, t, 0.0)
                    if k < 3:
                        th, tl = split(t)
                        u = dot(
                            jnp.concatenate([th, th, tl, tl], 0),
                            jnp.concatenate([th, tl, th, tl], 0),
                            TN,
                        )
                        n = 96 - lo
                        rest = xw[c, lo + 32 :, :]
                        ln = lax.broadcasted_iota(jnp.int32, (n, 128), 1)
                        xw[c, lo + 32 :, :] = jnp.where(ln // 32 == k, 0.0, rest) - u[lo + 32 :, :]
                return 0

            lax.fori_loop(0, 4, apply, 0)


def factor_kernel(first, length, nb, geo, gs, w3_out, xw, wp, cc, tt, l32s):
    count = 16
    lane8 = lax.broadcasted_iota(jnp.int32, (8, 128), 1)
    sub8 = lax.broadcasted_iota(jnp.int32, (8, 128), 0)
    scale = math.sqrt(3.0) / length[0]
    eye = (
        lax.broadcasted_iota(jnp.int32, (128, 128), 0)
        == lax.broadcasted_iota(jnp.int32, (128, 128), 1)
    )

    def window(c):
        ci, cj = c // 4, c % 4
        idx = nb[ci, pl.ds(cj, 1), :]
        gx = idx >> 12
        gy = (idx >> 7) & 31
        w = (gx - (first[0] + ci) + 2) * 5 + (gy - (first[1] + cj) + 2)
        return ci, cj, w, idx & 127

    def covariance(c, _):
        ci, cj, w, member = window(c)
        parts = []
        for h in range(2):
            wb = jnp.broadcast_to(w[:, 128 * h : 128 * h + 128], (8, 128))
            mb = jnp.broadcast_to(member[:, 128 * h : 128 * h + 128], (8, 128))
            acc = jnp.zeros((8, 128), F32)
            for wi in range(5):
                for wj in range(5):
                    if wi == 2 and wj == 2:
                        continue
                    shift = jnp.where(
                        sub8 == 0, float(wi - 2), jnp.where(sub8 == 1, float(wj - 2), 0.0)
                    )
                    t = lane_take(geo[ci + wi, cj + wj], mb) + shift
                    acc = jnp.where(wb == wi * 5 + wj, t, acc)
            parts.append(acc)
        parts.append(geo[ci + 2, cj + 2])
        pts = jnp.concatenate(parts, 1)
        cols = jnp.transpose(pts * scale)
        rows = pts * scale

        def block(a, b):
            dx = cols[128 * a : 128 * a + 128, 0:1] - rows[0:1, 128 * b : 128 * b + 128]
            dy = cols[128 * a : 128 * a + 128, 1:2] - rows[1:2, 128 * b : 128 * b + 128]
            s2 = dx * dx + dy * dy
            s = s2 * lax.rsqrt(jnp.maximum(s2, 1e-30))
            k = (1.0 + s) * jnp.exp(-s)
            if a == b:
                k = k + jnp.where(eye, pts[2:3, 128 * b : 128 * b + 128], 0.0)
            return k

        xw[c] = block(0, 0)
        cc[c, :128, :] = block(1, 0)
        cc[c, 128:, :] = block(2, 0)
        tt[c, :128, :128] = block(1, 1)
        tt[c, 128:, :128] = block(2, 1)
        tt[c, 128:, 128:] = block(2, 2)
        return 0

    lax.fori_loop(0, count, covariance, 0)
    inv_chol(xw, wp, count)

    def level1(q, _):
        for e in range(2):
            c = 2 * q + e
            w1 = xw[c]
            p = mm_nt(cc[c], w1)
            u = mm_nt(p, p)
            cc[c] = mm_nn(p, w1)
            xw[c] = tt[c, :128, :128] - u[:128, :128]
            tt[c, 128:, :128] = tt[c, 128:, :128] - u[128:, :128]
            tt[c, 128:, 128:] = tt[c, 128:, 128:] - u[128:, 128:]
        return 0

    lax.fori_loop(0, count // 2, level1, 0)
    inv_chol(xw, wp, count)

    def level2(q, _):
        for e in range(4):
            c = 4 * q + e
            w2 = xw[c]
            l32 = mm_nt(tt[c, 128:, :128], w2)
            l32s[c] = mm_nn(l32, w2)
            xw[c] = tt[c, 128:, 128:] - mm_nt(l32, l32)
        return 0

    lax.fori_loop(0, count // 4, level2, 0)
    inv_chol(xw, wp, count)

    def last(c, _):
        ci, cj, w, member = window(c)
        w3 = xw[c]
        w3_out[c] = w3
        q2 = l32s[c]
        q1 = cc[c, 128:, :] - mm_nn(q2, cc[c, :128, :])
        g = mm_nn(w3, jnp.concatenate([q1, q2], 1))
        gb = g.astype(BF).astype(F32)
        mb = jnp.broadcast_to(member, (128, 256))
        pick = jnp.where(lax.broadcasted_iota(jnp.int32, (128, 256), 0) == mb, 1.0, 0.0).astype(BF)
        for wi in range(5):
            lhs = jnp.concatenate(
                [jnp.where(w == wi * 5 + wj, gb, 0.0).astype(BF) for wj in range(5)], 0
            )
            s = dot(lhs, pick, NT).astype(BF)
            for wj in range(5):
                gs[c, wi, :, 128 * wj : 128 * wj + 128] = s[128 * wj : 128 * wj + 128, :]
        return 0

    lax.fori_loop(0, count, last, 0)


def factor(first, length, nb, geo):
    vm = pl.BlockSpec(memory_space=pltpu.VMEM)
    sm = pl.BlockSpec(memory_space=pltpu.SMEM)
    return pl.pallas_call(
        factor_kernel,
        out_shape=(
            jax.ShapeDtypeStruct((16, 5, 128, 640), BF),
            jax.ShapeDtypeStruct((16, 128, 128), F32),
        ),
        in_specs=[sm, sm, vm, vm],
        out_specs=(vm, vm),
        scratch_shapes=[
            pltpu.VMEM((16, 128, 128), F32),
            pltpu.VMEM((4, 32, 128), F32),
            pltpu.VMEM((16, 256, 128), F32),
            pltpu.VMEM((16, 256, 256), F32),
            pltpu.VMEM((16, 128, 128), F32),
        ],
        compiler_params=pltpu.CompilerParams(vmem_limit_bytes=60 << 20),
        name="factor",
    )(first, length, nb, geo)


def whiten_kernel(mid, north, south, west, east, nw, ne, sw, se, gs, w3, own, white, weights, term, tab):
    step = pl.program_id(0)

    @pl.when(step == 0)
    def _():
        tab[0:2, :, 0:256] = nw[...]
        tab[0:2, :, 256:768] = north[...]
        tab[0:2, :, 768:1024] = ne[...]
        tab[2:6, :, 0:256] = west[...]
        tab[2:6, :, 256:768] = mid[...]
        tab[2:6, :, 768:1024] = east[...]
        tab[6:8, :, 0:256] = sw[...]
        tab[6:8, :, 256:768] = south[...]
        tab[6:8, :, 768:1024] = se[...]

    ci, cj = step // 4, step % 4
    start = pl.multiple_of(cj * 128, 128)
    acc = mm_nt(w3[0], own[0])
    for wi in range(5):
        acc = acc - dot(gs[0, wi], tab[ci + wi, :, pl.ds(start, 640)], NT)
    white[0] = acc
    weights[...] = acc.astype(BF)
    eye = (
        lax.broadcasted_iota(jnp.int32, (128, 128), 0)
        == lax.broadcasted_iota(jnp.int32, (128, 128), 1)
    )
    diag = jnp.sum(jnp.where(eye, w3[0], 0.0), axis=0, keepdims=True)
    total = 0.5 * jnp.sum(acc * acc) - 256.0 * jnp.sum(jnp.log(diag))
    term[...] = jnp.full((1, 8, 128), -total / 32768.0 - 0.5 * math.log(2.0 * math.pi), F32)


def whiten(pieces, gs, w3, own):
    def whole(a):
        nd = a.ndim
        return pl.BlockSpec(a.shape, lambda s: (0,) * nd, pipeline_mode=pl.Buffered(1))

    return pl.pallas_call(
        whiten_kernel,
        grid=(16,),
        out_shape=(
            jax.ShapeDtypeStruct((16, 128, 256), F32),
            jax.ShapeDtypeStruct((2048, 256), BF),
            jax.ShapeDtypeStruct((16, 8, 128), F32),
        ),
        in_specs=[whole(p) for p in pieces]
        + [
            pl.BlockSpec((1, 5, 128, 640), lambda s: (s, 0, 0, 0)),
            pl.BlockSpec((1, 128, 128), lambda s: (s, 0, 0)),
            pl.BlockSpec((1, 256, 128), lambda s: (s // 4, 0, s % 4)),
        ],
        out_specs=(
            pl.BlockSpec((1, 128, 256), lambda s: (s, 0, 0)),
            pl.BlockSpec((128, 256), lambda s: (s, 0)),
            pl.BlockSpec((1, 8, 128), lambda s: (s, 0, 0)),
        ),
        scratch_shapes=[pltpu.VMEM((8, 256, 1024), BF)],
        compiler_params=pltpu.CompilerParams(vmem_limit_bytes=40 << 20),
        name="whiten",
    )(*pieces, gs, w3, own)


LN2 = math.log(2.0)
TB = 512


def pieces3(x):
    a = x.astype(BF).astype(F32)
    r = x - a
    b = r.astype(BF).astype(F32)
    return a, b, r - b


def cross_kernel(scale, tgt, pts, w, out, rhs):
    def form(x, y, left):
        q = x * x + y * y
        qs = pieces3(q)
        ones = jnp.ones_like(x)
        xs, ys = pieces3(x), pieces3(y)
        m = -2.0 if left else 1.0
        rows = []
        for a, b in ((0, 0), (0, 1), (1, 0), (0, 2), (1, 1), (2, 0)):
            k = a if left else b
            rows += [xs[k] * m, ys[k] * m]
        rows += (list(qs) + [ones] * 3) if left else ([ones] * 3 + list(qs))
        rows += [jnp.zeros_like(x)] * 14
        return jnp.concatenate(rows, 0).astype(BF)

    @pl.when(pl.program_id(0) == 0)
    def _():
        rhs[...] = form(pts[0:1, :] * scale[0], pts[1:2, :] * scale[0], False)

    lhs = form(tgt[0, 0:1, :] * scale[0], tgt[0, 1:2, :] * scale[0], True)
    acc = jnp.zeros((TB, 256), F32)
    for b in range(4):
        cut = slice(512 * b, 512 * b + 512)
        s2 = jnp.maximum(dot(lhs, rhs[:, cut], TN), 1e-30)
        s = s2 * lax.rsqrt(s2)
        k = (1.0 + s * LN2) * jnp.exp2(-s)
        acc = acc + dot(k.astype(BF), w[cut, :], NN)
    out[...] = (acc * scale[1]).astype(out.dtype)


def cross(scale, tgt, pts, w, dtype):
    n = tgt.shape[0]
    return pl.pallas_call(
        cross_kernel,
        grid=(n,),
        out_shape=jax.ShapeDtypeStruct((n * TB, 256), dtype),
        in_specs=[
            pl.BlockSpec(memory_space=pltpu.SMEM),
            pl.BlockSpec((1, 2, TB), lambda s: (s, 0, 0)),
            pl.BlockSpec((2, 2048), lambda s: (0, 0)),
            pl.BlockSpec((2048, 256), lambda s: (0, 0)),
        ],
        out_specs=pl.BlockSpec((TB, 256), lambda s: (s, 0)),
        scratch_shapes=[pltpu.VMEM((32, 2048), BF)],
        compiler_params=pltpu.CompilerParams(vmem_limit_bytes=40 << 20),
        name="cross",
    )(scale, tgt, pts, w)


def sum_kernel(parts, out):
    acc = parts[0].astype(F32)
    for i in range(1, 8):
        acc = acc + parts[i].astype(F32)
    out[...] = acc


def sum_parts(parts):
    n = parts.shape[1]
    return pl.pallas_call(
        sum_kernel,
        grid=(n // 256,),
        out_shape=jax.ShapeDtypeStruct((n, 256), F32),
        in_specs=[pl.BlockSpec((8, 256, 256), lambda s: (0, s, 0))],
        out_specs=pl.BlockSpec((256, 256), lambda s: (s, 0)),
        name="sum_parts",
    )(parts)


def shifted(x, dr, dc):
    pairs = [
        (r * 8 + c, (r + dr) * 8 + c + dc)
        for r in range(16)
        for c in range(8)
        if 0 <= r + dr < 16 and 0 <= c + dc < 8
    ]
    return lax.ppermute(x, ("rows", "cols"), pairs)


def surround(x, cut_r, cut_c):
    n = shifted(cut_r(x, 1), 1, 0)
    s = shifted(cut_r(x, 0), -1, 0)
    w = shifted(cut_c(x, 1), 0, 1)
    e = shifted(cut_c(x, 0), 0, -1)
    nw = shifted(cut_c(cut_r(x, 1), 1), 1, 1)
    ne = shifted(cut_c(cut_r(x, 1), 0), 1, -1)
    sw = shifted(cut_c(cut_r(x, 0), 1), -1, 1)
    se = shifted(cut_c(cut_r(x, 0), 0), -1, -1)
    return n, s, w, e, nw, ne, sw, se


def spread(x):
    return [x] + [
        lax.ppermute(x, "cols", [(i, (i + k) % 8) for i in range(8)]) for k in range(1, 8)
    ]


def body(values, offsets, nugget, neighbours, length_scale, target_tile, target_spots):
    row = lax.axis_index("rows")
    col = lax.axis_index("cols")
    length = length_scale[0]
    first = jnp.stack([row * 4, col * 4]).astype(jnp.int32)

    geo = jnp.concatenate(
        [offsets.transpose(1, 2, 0, 3), nugget[:, :, None, :], jnp.zeros((4, 4, 5, 128), F32)], 2
    )
    n, s, w, e, nw, ne, sw, se = surround(
        geo, lambda a, h: a[2 * h : 2 * h + 2], lambda a, h: a[:, 2 * h : 2 * h + 2]
    )
    geo_all = jnp.concatenate(
        [
            jnp.concatenate([nw, n, ne], 1),
            jnp.concatenate([w, geo, e], 1),
            jnp.concatenate([sw, s, se], 1),
        ],
        0,
    )

    own = values.transpose(1, 0, 2, 3).reshape(4, 256, 512)
    mid = own.astype(BF)
    around = surround(
        mid, lambda a, h: a[2 * h : 2 * h + 2], lambda a, h: a[:, :, 256 * h : 256 * h + 256]
    )

    tile_ids = target_tile[:, 0]
    one_hot = (tile_ids[:, None] == jnp.arange(16, dtype=jnp.int32)[None, :]).astype(jnp.int32)
    rank = jnp.sum((jnp.cumsum(one_hot, axis=0) - 1) * one_hot, axis=1)
    slot = tile_ids * 64 + rank
    send_x = jnp.zeros((1024,), F32).at[slot].set(target_spots[0])
    send_y = jnp.zeros((1024,), F32).at[slot].set(target_spots[1])
    outgoing = jnp.concatenate([send_x.reshape(16, 64), send_y.reshape(16, 64)], axis=1)
    incoming = lax.all_to_all(outgoing, "rows", split_axis=0, concat_axis=0, tiled=True)
    tx = incoming[:, :64].reshape(1024) * 4.0 - 2.0
    ty = incoming[:, 64:].reshape(1024) * 32.0
    spots = spread(jnp.stack([tx, ty]))
    spots = jnp.stack(spots)
    order = (col - jnp.arange(8, dtype=jnp.int32)) % 8
    spots = jnp.take(spots, order, axis=0)
    mid_y = (col * 4 + 2).astype(F32)
    tgt = jnp.stack([spots[:, 0], spots[:, 1] - mid_y], 1)
    tgt = tgt.reshape(8, 2, 1024 // TB, TB).transpose(0, 2, 1, 3).reshape(-1, 2, TB)

    gs, w3 = factor(first, length_scale, neighbours, geo_all)
    white, weights, term = whiten([mid, *around], gs, w3, own)

    px = offsets[0] + (jnp.arange(4, dtype=F32) - 2.0)[:, None, None]
    py = offsets[1] + (jnp.arange(4, dtype=F32) - 2.0)[None, :, None]
    pts = jnp.stack([px.reshape(-1), py.reshape(-1)])
    scale = jnp.stack([math.sqrt(3.0) / LN2 / length, jnp.float32(1.0 / 128.0)])
    partial = cross(scale, tgt, pts, weights, BF)
    shared = lax.all_to_all(
        partial.reshape(8, 1024, 256), "cols", split_axis=0, concat_axis=0, tiled=True
    )
    predicted = sum_parts(shared)
    returned = lax.all_to_all(
        predicted.reshape(16, 64, 256), "rows", split_axis=0, concat_axis=0, tiled=True
    )
    predictions = returned.reshape(-1, 256)[slot]
    return (white.reshape(4, 4, 128, 256), term[:, 0, 0].reshape(4, 4), predictions)


def solution(mesh):
    return jax.shard_map(
        body,
        mesh=mesh,
        in_specs=(
            P(None, "rows", "cols", None),
            P(None, "rows", "cols", None),
            P("rows", "cols", None),
            P("rows", "cols", None),
            P(),
            P(("rows", "cols"), None),
            P(None, ("rows", "cols")),
        ),
        out_specs=(P("rows", "cols", None, None), P("rows", "cols"), P(("rows", "cols"), None)),
        check_vma=False,
    )
```

```python
import math

import jax
import jax.numpy as jnp

from jax import lax
from jax.experimental import pallas as pl
from jax.experimental.pallas import tpu as pltpu
from jax.sharding import PartitionSpec as P

F32 = jnp.float32
BF = jnp.bfloat16
NN = (((1,), (0,)), ((), ()))
NT = (((1,), (1,)), ((), ()))
TN = (((0,), (0,)), ((), ()))


def split(x):
    hi = x.astype(BF)
    return hi, (x - hi.astype(F32)).astype(BF)


def dot(a, b, dims):
    return lax.dot_general(a, b, dims, preferred_element_type=F32)


def mm_nt(a, b):
    ah, al = split(a)
    bh, bl = split(b)
    return dot(jnp.concatenate([ah, ah, al], 1), jnp.concatenate([bh, bl, bh], 1), NT)


def mm_nn(a, b):
    ah, al = split(a)
    bh, bl = split(b)
    return dot(jnp.concatenate([ah, ah, al], 1), jnp.concatenate([bh, bl, bh], 0), NN)


def lane_take(x, idx):
    return jnp.take_along_axis(x, idx, axis=1, mode="promise_in_bounds")


def recip(p):
    r = pl.reciprocal(p, approx=True)
    return r * (2.0 - p * r)


def leaf_factor(leaf, lane, sub):
    base = lane & 96
    col = lane & 31
    x = [list(p) for p in leaf]
    ones = jnp.ones((8, 128), F32)
    piv = [[[ones, jnp.zeros((8, 128), F32), ones] for _ in range(4)] for _ in range(4)]

    def spread_row(t, s):
        return jnp.broadcast_to(t[s : s + 1, :], (8, 128))

    for j in range(0, 32, 2):
        v0, s0 = divmod(j, 8)
        first, second = base + j, base + j + 1
        unit0 = jnp.where(col == j, 1.0, 0.0)
        unit1 = jnp.where(col == j + 1, 1.0, 0.0)
        below = sub > s0 + 1
        here = (sub == s0) | (sub == s0 + 1)
        for p in range(4):
            c0 = [lane_take(x[p][v], first) for v in range(v0, 4)]
            c1 = [lane_take(x[p][v], second) for v in range(v0, 4)]
            a, b, d = spread_row(c0[0], s0), spread_row(c0[0], s0 + 1), spread_row(c1[0], s0 + 1)
            r = recip(a * d - b * b)
            r0 = spread_row(x[p][v0], s0) + unit0
            r1 = spread_row(x[p][v0], s0 + 1) + unit1
            w0 = d * r0 - b * r1
            w1 = a * r1 - b * r0
            for i, new in enumerate((a, b, d)):
                piv[p][v0][i] = jnp.where(here, new, piv[p][v0][i])
            for v in range(v0, 4):
                if v == v0 and s0 == 6:
                    continue
                t = c0[v - v0] * w0 + c1[v - v0] * w1
                if v == v0:
                    t = jnp.where(below, t, 0.0)
                x[p][v] = x[p][v] - t * r
    odd = (sub & 1) == 1
    out = []
    for p in range(4):
        o = []
        for v in range(4):
            a, b, d = piv[p][v]
            f = jnp.where(odd, b * recip(a), 0.0)
            e = jnp.where(odd, d - b * f, a)
            q = lax.rsqrt(e)
            q = q * (1.5 - 0.5 * e * q * q)
            r_i = sub + 8 * v
            n = jnp.where(col < (r_i & 30), x[p][v], jnp.where(col == r_i, 1.0, 0.0))
            o.append(q * (n - f * pltpu.roll(n, 1, axis=0)))
        out.append(o)
    return out


def inv_chol(xw, wp, count):
    lane8 = lax.broadcasted_iota(jnp.int32, (8, 128), 1)
    sub8 = lax.broadcasted_iota(jnp.int32, (8, 128), 0)
    lane = lax.broadcasted_iota(jnp.int32, (32, 128), 1)
    subl = lax.broadcasted_iota(jnp.int32, (32, 128), 0)
    for k in range(4):
        lo = 32 * k
        for base in range(0, count, 16):
            leaf = []
            for p in range(4):
                tiles = []
                for v in range(4):
                    acc = None
                    for g in range(4):
                        t = xw[base + 4 * p + g, lo + 8 * v : lo + 8 * v + 8, :]
                        t = pltpu.roll(t, (32 * (g - k)) % 128, axis=1) if g != k else t
                        acc = t if acc is None else jnp.where(lane8 // 32 == g, t, acc)
                    tiles.append(acc)
                leaf.append(tiles)
            inv = leaf_factor(leaf, lane8, sub8)
            for p in range(4):
                for v in range(4):
                    wp[p, 8 * v : 8 * v + 8, :] = inv[p][v]

            def apply(q, _):
                cs = [base + 8 * q + e for e in range(8)]
                xs = [xw[c] for c in cs]
                ws = []
                for h in range(2):
                    ws.append(wp[2 * q + h])
                ts = []
                for e in range(8):
                    g = e % 4
                    gi = 32 * g + (lane8 & 31)
                    w = ws[e // 4]
                    wr = jnp.concatenate(
                        [lane_take(w[8 * v : 8 * v + 8], gi) for v in range(4)], 0
                    )
                    wh = wr.astype(BF).astype(F32)
                    lhs = jnp.where(lane < 64, wh, wr - wh).astype(BF)
                    r = xs[e][lo : lo + 32, :]
                    r = jnp.where(lane // 32 == k, jnp.where((lane & 31) == subl, 1.0, 0.0), r)
                    rh, rl = split(r)
                    ts.append(dot(lhs, jnp.concatenate([rh, rl, rh, rl], 0), NN))
                if k < 3:
                    n = 96 - lo
                    ln = lax.broadcasted_iota(jnp.int32, (n, 128), 1)
                    ls = []
                    for e in range(8):
                        g = e % 4
                        w = ws[e // 4]
                        w = pltpu.roll(w, (32 * (k - g)) % 128, axis=1) if g != k else w
                        w = jnp.where(lane // 32 == k, w, 0.0)
                        wh, wl = split(w)
                        wh = jnp.concatenate([wh] * 4, 0)
                        wl = jnp.concatenate([wl] * 4, 0)
                        xh, xl = split(xs[e][lo + 32 :, :])
                        ls.append(
                            dot(
                                jnp.concatenate([xh, xl, xh], 1),
                                jnp.concatenate([wh, wh, wl], 1),
                                NT,
                            )
                        )
                    us = []
                    for e in range(8):
                        lh = ls[e].astype(BF).astype(F32)
                        lhs = jnp.where(ln < 64, lh, ls[e] - lh).astype(BF)
                        th, tl = split(ts[e])
                        us.append(dot(lhs, jnp.concatenate([th, tl, th, tl], 0), NN))
                for e in range(8):
                    c = cs[e]
                    xw[c, lo : lo + 32, :] = jnp.where(lane < lo + 32, ts[e], 0.0)
                    if k < 3:
                        rest = xs[e][lo + 32 :, :]
                        xw[c, lo + 32 :, :] = jnp.where(ln // 32 == k, 0.0, rest) - us[e]
                return 0

            lax.fori_loop(0, 2, apply, 0)


def window(first, nb, c):
    ci, cj = c // 4, c % 4
    idx = nb[ci, pl.ds(cj, 1), :]
    gx = idx >> 12
    gy = (idx >> 7) & 31
    w = (gx - (first[0] + ci) + 2) * 5 + (gy - (first[1] + cj) + 2)
    return ci, cj, w, idx & 127


def first_kernel(first, length, nb, geo, xw, cc, tt, wp, mid):
    count = 16
    lane8 = lax.broadcasted_iota(jnp.int32, (8, 128), 1)
    sub8 = lax.broadcasted_iota(jnp.int32, (8, 128), 0)
    scale = math.sqrt(3.0) / length[0]
    eye = (
        lax.broadcasted_iota(jnp.int32, (128, 128), 0)
        == lax.broadcasted_iota(jnp.int32, (128, 128), 1)
    )

    def covariance(c, _):
        ci, cj, w, member = window(first, nb, c)
        parts = []
        for h in range(2):
            wb = jnp.broadcast_to(w[:, 128 * h : 128 * h + 128], (8, 128))
            mb = jnp.broadcast_to(member[:, 128 * h : 128 * h + 128], (8, 128))
            acc = jnp.zeros((8, 128), F32)
            for wi in range(5):
                for wj in range(5):
                    if wi == 2 and wj == 2:
                        continue
                    shift = jnp.where(
                        sub8 == 0, float(wi - 2), jnp.where(sub8 == 1, float(wj - 2), 0.0)
                    )
                    t = lane_take(geo[ci + wi, cj + wj], mb) + shift
                    acc = jnp.where(wb == wi * 5 + wj, t, acc)
            parts.append(acc)
        parts.append(geo[ci + 2, cj + 2])
        pts = jnp.concatenate(parts, 1)
        cols = jnp.transpose(pts * scale)
        rows = pts * scale

        def block(a, b):
            dx = cols[128 * a : 128 * a + 128, 0:1] - rows[0:1, 128 * b : 128 * b + 128]
            dy = cols[128 * a : 128 * a + 128, 1:2] - rows[1:2, 128 * b : 128 * b + 128]
            s2 = dx * dx + dy * dy
            s = s2 * lax.rsqrt(jnp.maximum(s2, 1e-30))
            k = (1.0 + s) * jnp.exp(-s)
            if a == b:
                k = k + jnp.where(eye, pts[2:3, 128 * b : 128 * b + 128], 0.0)
            return k

        xw[c] = block(0, 0)
        cc[c, :128, :] = block(1, 0)
        cc[c, 128:, :] = block(2, 0)
        mid[c] = block(1, 1)
        tt[c, :, :128] = block(2, 1)
        tt[c, :, 128:] = block(2, 2)
        return 0

    lax.fori_loop(0, count, covariance, 0)
    inv_chol(xw, wp, count)

    def level1(q, _):
        cs = [4 * q + e for e in range(4)]
        w1 = [xw[c] for c in cs]
        p = [mm_nt(cc[c], w) for c, w in zip(cs, w1)]
        u = [mm_nt(a, a) for a in p]
        v = [mm_nn(a, w) for a, w in zip(p, w1)]
        for e, c in enumerate(cs):
            cc[c] = v[e]
            xw[c] = mid[c] - u[e][:128, :128]
            tt[c] = tt[c] - u[e][128:, :]
        return 0

    lax.fori_loop(0, count // 4, level1, 0)

def rest_kernel(first, nb, x_in, cc, tt, gs, w3_out, xw, wp, l32s):
    count = 16
    xw[...] = x_in[...]
    inv_chol(xw, wp, count)

    def level2(q, _):
        cs = [4 * q + e for e in range(4)]
        w2 = [xw[c] for c in cs]
        l32 = [mm_nt(tt[c, :, :128], w) for c, w in zip(cs, w2)]
        u = [mm_nt(a, a) for a in l32]
        v = [mm_nn(a, w) for a, w in zip(l32, w2)]
        for e, c in enumerate(cs):
            l32s[c] = v[e]
            xw[c] = tt[c, :, 128:] - u[e]
        return 0

    lax.fori_loop(0, count // 4, level2, 0)
    inv_chol(xw, wp, count)

    def last(q, _):
        cs = [2 * q + e for e in range(2)]
        w3 = [xw[c] for c in cs]
        q2 = [l32s[c] for c in cs]
        q1 = [cc[c, 128:, :] - mm_nn(b, cc[c, :128, :]) for c, b in zip(cs, q2)]
        gb = [
            mm_nn(w, jnp.concatenate([a, b], 1)).astype(BF).astype(F32)
            for w, a, b in zip(w3, q1, q2)
        ]
        for e, c in enumerate(cs):
            ci, cj, w, member = window(first, nb, c)
            w3_out[c] = w3[e]
            mb = jnp.broadcast_to(member, (128, 256))
            point = lax.broadcasted_iota(jnp.int32, (128, 256), 0)
            pick = jnp.where(point == mb, 1.0, 0.0).astype(BF)
            for wi in range(5):
                lhs = jnp.concatenate(
                    [jnp.where(w == wi * 5 + wj, gb[e], 0.0).astype(BF) for wj in range(5)], 0
                )
                s = dot(lhs, pick, NT).astype(BF)
                for wj in range(5):
                    gs[c, wi, :, 128 * wj : 128 * wj + 128] = s[128 * wj : 128 * wj + 128, :]
        return 0

    lax.fori_loop(0, count // 2, last, 0)


VM = pl.BlockSpec(memory_space=pltpu.VMEM)
SM = pl.BlockSpec(memory_space=pltpu.SMEM)


def factor_first(first, length, nb, geo):
    return pl.pallas_call(
        first_kernel,
        out_shape=(
            jax.ShapeDtypeStruct((16, 128, 128), F32),
            jax.ShapeDtypeStruct((16, 256, 128), F32),
            jax.ShapeDtypeStruct((16, 128, 256), F32),
        ),
        in_specs=[SM, SM, VM, VM],
        out_specs=(VM, VM, VM),
        scratch_shapes=[pltpu.VMEM((4, 32, 128), F32), pltpu.VMEM((16, 128, 128), F32)],
        compiler_params=pltpu.CompilerParams(vmem_limit_bytes=32 << 20),
        name="factor_first",
    )(first, length, nb, geo)


def factor_rest(first, nb, x, c, t):
    return pl.pallas_call(
        rest_kernel,
        out_shape=(
            jax.ShapeDtypeStruct((16, 5, 128, 640), BF),
            jax.ShapeDtypeStruct((16, 128, 128), F32),
        ),
        in_specs=[SM, VM, VM, VM, VM],
        out_specs=(VM, VM),
        scratch_shapes=[
            pltpu.VMEM((16, 128, 128), F32),
            pltpu.VMEM((4, 32, 128), F32),
            pltpu.VMEM((16, 128, 128), F32),
        ],
        compiler_params=pltpu.CompilerParams(vmem_limit_bytes=40 << 20),
        name="factor_rest",
    )(first, nb, x, c, t)


def whiten_kernel(north, mid, south, gs, w3, own, white, weights, term, tab):
    step = pl.program_id(0)

    @pl.when(step == 0)
    def _():
        tab[0:2] = north[...]
        tab[2:6] = mid[...]
        tab[6:8] = south[...]

    ci, cj = step // 4, step % 4
    start = pl.multiple_of(cj * 128, 128)
    acc = mm_nt(w3[0], own[0])
    for wi in range(5):
        acc = acc - dot(gs[0, wi], tab[ci + wi, :, pl.ds(start, 640)], NT)
    white[0] = acc
    weights[...] = acc.astype(BF)
    eye = (
        lax.broadcasted_iota(jnp.int32, (128, 128), 0)
        == lax.broadcasted_iota(jnp.int32, (128, 128), 1)
    )
    diag = jnp.sum(jnp.where(eye, w3[0], 0.0), axis=0, keepdims=True)
    total = 0.5 * jnp.sum(acc * acc) - 256.0 * jnp.sum(jnp.log(diag))
    term[...] = jnp.full((1, 8, 128), -total / 32768.0 - 0.5 * math.log(2.0 * math.pi), F32)


def whiten(pieces, gs, w3, own):
    def whole(a):
        nd = a.ndim
        return pl.BlockSpec(a.shape, lambda s: (0,) * nd, pipeline_mode=pl.Buffered(1))

    return pl.pallas_call(
        whiten_kernel,
        grid=(16,),
        out_shape=(
            jax.ShapeDtypeStruct((16, 128, 256), F32),
            jax.ShapeDtypeStruct((2048, 256), BF),
            jax.ShapeDtypeStruct((16, 8, 128), F32),
        ),
        in_specs=[whole(p) for p in pieces]
        + [
            pl.BlockSpec((1, 5, 128, 640), lambda s: (s, 0, 0, 0)),
            pl.BlockSpec((1, 128, 128), lambda s: (s, 0, 0)),
            pl.BlockSpec((1, 256, 128), lambda s: (s // 4, 0, s % 4)),
        ],
        out_specs=(
            pl.BlockSpec((1, 128, 256), lambda s: (s, 0, 0)),
            pl.BlockSpec((128, 256), lambda s: (s, 0)),
            pl.BlockSpec((1, 8, 128), lambda s: (s, 0, 0)),
        ),
        scratch_shapes=[pltpu.VMEM((8, 256, 1024), BF)],
        compiler_params=pltpu.CompilerParams(vmem_limit_bytes=40 << 20),
        name="whiten",
    )(*pieces, gs, w3, own)


LN2 = math.log(2.0)
TB = 1024


def pieces3(x):
    a = x.astype(BF).astype(F32)
    r = x - a
    b = r.astype(BF).astype(F32)
    return a, b, r - b


def cross_kernel(scale, tgt, pts, w, acc_in, out, rhs):
    def form(x, y, left):
        q = x * x + y * y
        qs = pieces3(q)
        ones = jnp.ones_like(x)
        xs, ys = pieces3(x), pieces3(y)
        m = -2.0 if left else 1.0
        rows = []
        for a, b in ((0, 0), (0, 1), (1, 0), (0, 2), (1, 1), (2, 0)):
            k = a if left else b
            rows += [xs[k] * m, ys[k] * m]
        rows += (list(qs) + [ones] * 3) if left else ([ones] * 3 + list(qs))
        rows += [jnp.zeros_like(x)] * 14
        return jnp.concatenate(rows, 0).astype(BF)

    @pl.when(pl.program_id(0) == 0)
    def _():
        rhs[...] = form(pts[0:1, :] * scale[0], pts[1:2, :] * scale[0], False)

    lhs = form(tgt[0, 0:1, :] * scale[0], tgt[0, 1:2, :] * scale[0], True)
    acc = acc_in[...] if acc_in is not None else jnp.zeros((TB, 256), F32)
    for b in range(8):
        cut = slice(256 * b, 256 * b + 256)
        s2 = jnp.maximum(dot(lhs, rhs[:, cut], TN), 1e-30)
        s = s2 * lax.rsqrt(s2)
        k = (1.0 + s * LN2) * jnp.exp2(-s)
        acc = acc + dot(k.astype(BF), w[cut, :], NN)
    out[...] = acc.astype(out.dtype)


def cross(scale, tgt, pts, w, dtype, acc=None, skip=0, name="cross"):
    n = tgt.shape[0]
    kernel = cross_kernel
    if acc is None:
        kernel = lambda s, t, p, w, o, r: cross_kernel(s, t, p, w, None, o, r)
    return pl.pallas_call(
        kernel,
        grid=(n,),
        out_shape=jax.ShapeDtypeStruct((n * TB, 256), dtype),
        in_specs=[
            pl.BlockSpec(memory_space=pltpu.SMEM),
            pl.BlockSpec((1, 2, TB), lambda s: (s, 0, 0)),
            pl.BlockSpec((2, 2048), lambda s: (0, 0)),
            pl.BlockSpec((2048, 256), lambda s: (0, 0)),
        ]
        + ([] if acc is None else [pl.BlockSpec((TB, 256), lambda s: (skip + s, 0))]),
        out_specs=pl.BlockSpec((TB, 256), lambda s: (s, 0)),
        scratch_shapes=[pltpu.VMEM((32, 2048), BF)],
        compiler_params=pltpu.CompilerParams(vmem_limit_bytes=32 << 20),
        name=name,
    )(scale, tgt, pts, w, *([] if acc is None else [acc]))


def sum_kernel(here, a, b, c, out):
    total = here[...] + (a[...].astype(F32) + b[...].astype(F32) + c[...].astype(F32))
    out[...] = total * (1.0 / 128.0)


def sum_parts(here, parts):
    spec = pl.BlockSpec((256, 256), lambda s: (s, 0))
    return pl.pallas_call(
        sum_kernel,
        grid=(4,),
        out_shape=jax.ShapeDtypeStruct((1024, 256), F32),
        in_specs=[spec] * 4,
        out_specs=spec,
        name="sum_parts",
    )(here, *parts)


def sides(low, high, axis):
    count = lax.axis_size(axis)
    forward = [(i, i + 1) for i in range(count - 1)]
    backward = [(b, a) for a, b in forward]
    return lax.ppermute(high, axis, forward), lax.ppermute(low, axis, backward)


def body(values, offsets, nugget, neighbours, length_scale, target_tile, target_spots):
    row = lax.axis_index("rows")
    col = lax.axis_index("cols")
    length = length_scale[0]
    first = jnp.stack([row * 4, col * 4]).astype(jnp.int32)

    geo = jnp.concatenate(
        [offsets.transpose(1, 2, 0, 3), nugget[:, :, None, :], jnp.zeros((4, 4, 5, 128), F32)], 2
    )
    w, e = sides(geo[:, :2], geo[:, 2:], "cols")
    geo = jnp.concatenate([w, geo, e], 1)
    n, s = sides(geo[:2], geo[2:], "rows")
    geo = jnp.concatenate([n, geo, s], 0)

    own = values.transpose(1, 0, 2, 3).reshape(4, 256, 512)
    mid = own.astype(BF)
    w, e = sides(mid[:, :, :256], mid[:, :, 256:], "cols")

    tile_ids = target_tile[:, 0]
    one_hot = (tile_ids[:, None] == jnp.arange(16, dtype=jnp.int32)[None, :]).astype(jnp.int32)
    rank = jnp.sum((jnp.cumsum(one_hot, axis=0) - 1) * one_hot, axis=1)
    slot = tile_ids * 64 + rank
    send_x = jnp.zeros((1024,), F32).at[slot].set(target_spots[0])
    send_y = jnp.zeros((1024,), F32).at[slot].set(target_spots[1])
    outgoing = jnp.concatenate([send_x.reshape(16, 64), send_y.reshape(16, 64)], axis=1)
    everyone = jnp.broadcast_to(outgoing[:, None, :], (16, 8, 128)).reshape(128, 1, 128)
    spots = lax.all_to_all(everyone, ("rows", "cols"), split_axis=0, concat_axis=0, tiled=True)
    spots = spots.reshape(16, 8, 2, 64).transpose(1, 2, 0, 3).reshape(4, 2, 2, 1024)
    band, half = col // 2, col % 2
    spots = lax.dynamic_index_in_dim(spots, half, 1, keepdims=False)
    spots = jnp.take(spots, (band + jnp.array([2, 1, 3, 0], jnp.int32)) % 4, axis=0)
    mid_y = (band * 8 + 4).astype(F32)
    tgt = jnp.stack([spots[:, 0] * 4.0 - 2.0, spots[:, 1] * 32.0 - mid_y], 1)
    tgt = tgt.reshape(4, 2, 1024 // TB, TB).transpose(0, 2, 1, 3).reshape(-1, 2, TB)
    px = offsets[0] + (jnp.arange(4, dtype=F32) - 2.0)[:, None, None]
    py = offsets[1] + (jnp.arange(4, dtype=F32) - 4.0 + 4.0 * half.astype(F32))[None, :, None]
    pts = jnp.stack([px.reshape(-1), py.reshape(-1)])
    partner = [(c, c ^ 1) for c in range(8)]
    pts2 = lax.ppermute(pts, "cols", partner)

    state = factor_first(first, length_scale, neighbours, geo)
    mid = jnp.concatenate([w, mid, e], 2)
    *state, mid = lax.optimization_barrier((*state, mid))
    n, s = sides(mid[:2], mid[2:], "rows")
    around = [n, mid, s]
    gs, w3 = factor_rest(first, neighbours, *state)
    white, weights, term = whiten(around, gs, w3, own)

    scale = jnp.stack([math.sqrt(3.0) / LN2 / length])
    weights2 = lax.ppermute(weights, "cols", partner)
    near = cross(scale, tgt, pts, weights, F32, name="cross_near")
    per = 1024 // TB
    parts = []
    for i, k in enumerate((2, 1, 3)):
        part = cross(
            scale, tgt[per * i : per * i + per], pts2, weights2, BF, near, per * i, "cross_far"
        )
        parts.append(lax.ppermute(part, "cols", [(c, (c + 2 * k) % 8) for c in range(8)]))
    here = cross(scale, tgt[3 * per :], pts2, weights2, F32, near, 3 * per, "cross_here")
    predicted = sum_parts(here, parts)
    returned = lax.all_to_all(
        predicted.reshape(16, 64, 256), "rows", split_axis=0, concat_axis=0, tiled=True
    )
    predictions = returned.reshape(-1, 256)[slot]
    return (white.reshape(4, 4, 128, 256), term[:, 0, 0].reshape(4, 4), predictions)


def solution(mesh):
    return jax.shard_map(
        body,
        mesh=mesh,
        in_specs=(
            P(None, "rows", "cols", None),
            P(None, "rows", "cols", None),
            P("rows", "cols", None),
            P("rows", "cols", None),
            P(),
            P(("rows", "cols"), None),
            P(None, ("rows", "cols")),
        ),
        out_specs=(P("rows", "cols", None, None), P("rows", "cols"), P(("rows", "cols"), None)),
        check_vma=False,
    )
```

```python
import math

import jax
import jax.numpy as jnp

from jax import lax
from jax.experimental import pallas as pl
from jax.experimental.pallas import tpu as pltpu
from jax.sharding import PartitionSpec as P

F32 = jnp.float32
BF = jnp.bfloat16
NN = (((1,), (0,)), ((), ()))
NT = (((1,), (1,)), ((), ()))
TN = (((0,), (0,)), ((), ()))


def split(x):
    hi = x.astype(BF)
    return hi, (x - hi.astype(F32)).astype(BF)


def dot(a, b, dims):
    return lax.dot_general(a, b, dims, preferred_element_type=F32)


def mm_nt(a, b):
    ah, al = split(a)
    bh, bl = split(b)
    return dot(jnp.concatenate([ah, ah, al], 1), jnp.concatenate([bh, bl, bh], 1), NT)


def mm_nn(a, b):
    ah, al = split(a)
    bh, bl = split(b)
    return dot(jnp.concatenate([ah, ah, al], 1), jnp.concatenate([bh, bl, bh], 0), NN)


def lane_take(x, idx):
    return jnp.take_along_axis(x, idx, axis=1, mode="promise_in_bounds")


def recip(p):
    r = pl.reciprocal(p, approx=True)
    return r * (2.0 - p * r)


def leaf_factor(leaf, lane, sub):
    base = lane & 96
    col = lane & 31
    x = [list(p) for p in leaf]
    ones = jnp.ones((8, 128), F32)
    piv = [[[ones, jnp.zeros((8, 128), F32), ones] for _ in range(4)] for _ in range(4)]

    def spread_row(t, s):
        return jnp.broadcast_to(t[s : s + 1, :], (8, 128))

    for j in range(0, 32, 2):
        v0, s0 = divmod(j, 8)
        first, second = base + j, base + j + 1
        unit0 = jnp.where(col == j, 1.0, 0.0)
        unit1 = jnp.where(col == j + 1, 1.0, 0.0)
        below = sub > s0 + 1
        here = (sub == s0) | (sub == s0 + 1)
        for p in range(4):
            c0 = [lane_take(x[p][v], first) for v in range(v0, 4)]
            c1 = [lane_take(x[p][v], second) for v in range(v0, 4)]
            a, b, d = spread_row(c0[0], s0), spread_row(c0[0], s0 + 1), spread_row(c1[0], s0 + 1)
            r = recip(a * d - b * b)
            r0 = spread_row(x[p][v0], s0) + unit0
            r1 = spread_row(x[p][v0], s0 + 1) + unit1
            w0 = d * r0 - b * r1
            w1 = a * r1 - b * r0
            for i, new in enumerate((a, b, d)):
                piv[p][v0][i] = jnp.where(here, new, piv[p][v0][i])
            for v in range(v0, 4):
                if v == v0 and s0 == 6:
                    continue
                t = c0[v - v0] * w0 + c1[v - v0] * w1
                if v == v0:
                    t = jnp.where(below, t, 0.0)
                x[p][v] = x[p][v] - t * r
    odd = (sub & 1) == 1
    out = []
    for p in range(4):
        o = []
        for v in range(4):
            a, b, d = piv[p][v]
            f = jnp.where(odd, b * recip(a), 0.0)
            e = jnp.where(odd, d - b * f, a)
            q = lax.rsqrt(e)
            q = q * (1.5 - 0.5 * e * q * q)
            r_i = sub + 8 * v
            n = jnp.where(col < (r_i & 30), x[p][v], jnp.where(col == r_i, 1.0, 0.0))
            o.append(q * (n - f * pltpu.roll(n, 1, axis=0)))
        out.append(o)
    return out


def inv_chol(xw, wp, count):
    lane8 = lax.broadcasted_iota(jnp.int32, (8, 128), 1)
    sub8 = lax.broadcasted_iota(jnp.int32, (8, 128), 0)
    lane = lax.broadcasted_iota(jnp.int32, (32, 128), 1)
    subl = lax.broadcasted_iota(jnp.int32, (32, 128), 0)
    for k in range(4):
        lo = 32 * k
        for base in range(0, count, 16):
            leaf = []
            for p in range(4):
                tiles = []
                for v in range(4):
                    acc = None
                    for g in range(4):
                        t = xw[base + 4 * p + g, lo + 8 * v : lo + 8 * v + 8, :]
                        t = pltpu.roll(t, (32 * (g - k)) % 128, axis=1) if g != k else t
                        acc = t if acc is None else jnp.where(lane8 // 32 == g, t, acc)
                    tiles.append(acc)
                leaf.append(tiles)
            inv = leaf_factor(leaf, lane8, sub8)
            for p in range(4):
                for v in range(4):
                    wp[p, 8 * v : 8 * v + 8, :] = inv[p][v]

            def apply(q, _):
                cs = [base + 8 * q + e for e in range(8)]
                xs = [xw[c] for c in cs]
                ws = [wp[2 * q], wp[2 * q + 1]]
                ts = []
                for e in range(8):
                    g = e % 4
                    gi = 32 * g + (lane8 & 31)
                    w = ws[e // 4]
                    wr = jnp.concatenate(
                        [lane_take(w[8 * v : 8 * v + 8], gi) for v in range(4)], 0
                    )
                    wh = wr.astype(BF).astype(F32)
                    lhs = jnp.where(lane < 64, wh, wr - wh).astype(BF)
                    r = xs[e][lo : lo + 32, :]
                    r = jnp.where(lane // 32 == k, jnp.where((lane & 31) == subl, 1.0, 0.0), r)
                    rh, rl = split(r)
                    ts.append(dot(lhs, jnp.concatenate([rh, rl, rh, rl], 0), NN))
                if k < 3:
                    n = 96 - lo
                    ln = lax.broadcasted_iota(jnp.int32, (n, 128), 1)
                    ls = []
                    for e in range(8):
                        g = e % 4
                        w = ws[e // 4]
                        w = pltpu.roll(w, (32 * (k - g)) % 128, axis=1) if g != k else w
                        w = jnp.where(lane // 32 == k, w, 0.0)
                        wh, wl = split(w)
                        wh = jnp.concatenate([wh] * 4, 0)
                        wl = jnp.concatenate([wl] * 4, 0)
                        xh, xl = split(xs[e][lo + 32 :, :])
                        ls.append(
                            dot(
                                jnp.concatenate([xh, xl, xh], 1),
                                jnp.concatenate([wh, wh, wl], 1),
                                NT,
                            )
                        )
                    us = []
                    for e in range(8):
                        lh = ls[e].astype(BF).astype(F32)
                        lhs = jnp.where(ln < 64, lh, ls[e] - lh).astype(BF)
                        th, tl = split(ts[e])
                        us.append(dot(lhs, jnp.concatenate([th, tl, th, tl], 0), NN))
                for e in range(8):
                    c = cs[e]
                    xw[c, lo : lo + 32, :] = jnp.where(lane < lo + 32, ts[e], 0.0)
                    if k < 3:
                        rest = xs[e][lo + 32 :, :]
                        xw[c, lo + 32 :, :] = jnp.where(ln // 32 == k, 0.0, rest) - us[e]
                return 0

            lax.fori_loop(0, 2, apply, 0)


def window(first, nb, c):
    ci, cj = c // 4, c % 4
    idx = nb[ci, pl.ds(cj, 1), :]
    gx = idx >> 12
    gy = (idx >> 7) & 31
    w = (gx - (first[0] + ci) + 2) * 5 + (gy - (first[1] + cj) + 2)
    return ci, cj, w, idx & 127


def first_kernel(first, length, nb, geo, xw, cc, tt, wp, mid):
    count = 16
    lane8 = lax.broadcasted_iota(jnp.int32, (8, 128), 1)
    sub8 = lax.broadcasted_iota(jnp.int32, (8, 128), 0)
    scale = math.sqrt(3.0) / length[0]
    eye = (
        lax.broadcasted_iota(jnp.int32, (128, 128), 0)
        == lax.broadcasted_iota(jnp.int32, (128, 128), 1)
    )

    def covariance(c, _):
        ci, cj, w, member = window(first, nb, c)
        parts = []
        for h in range(2):
            wb = jnp.broadcast_to(w[:, 128 * h : 128 * h + 128], (8, 128))
            mb = jnp.broadcast_to(member[:, 128 * h : 128 * h + 128], (8, 128))
            acc = jnp.zeros((8, 128), F32)
            for wi in range(5):
                for wj in range(5):
                    if wi == 2 and wj == 2:
                        continue
                    shift = jnp.where(
                        sub8 == 0, float(wi - 2), jnp.where(sub8 == 1, float(wj - 2), 0.0)
                    )
                    t = lane_take(geo[ci + wi, cj + wj], mb) + shift
                    acc = jnp.where(wb == wi * 5 + wj, t, acc)
            parts.append(acc)
        parts.append(geo[ci + 2, cj + 2])
        pts = jnp.concatenate(parts, 1)
        cols = jnp.transpose(pts * scale)
        rows = pts * scale

        def block(a, b):
            dx = cols[128 * a : 128 * a + 128, 0:1] - rows[0:1, 128 * b : 128 * b + 128]
            dy = cols[128 * a : 128 * a + 128, 1:2] - rows[1:2, 128 * b : 128 * b + 128]
            s2 = dx * dx + dy * dy
            s = s2 * lax.rsqrt(jnp.maximum(s2, 1e-30))
            k = (1.0 + s) * jnp.exp(-s)
            if a == b:
                k = k + jnp.where(eye, pts[2:3, 128 * b : 128 * b + 128], 0.0)
            return k

        xw[c] = block(0, 0)
        cc[c, :128, :] = block(1, 0)
        cc[c, 128:, :] = block(2, 0)
        mid[c] = block(1, 1)
        tt[c, :, :128] = block(2, 1)
        tt[c, :, 128:] = block(2, 2)
        return 0

    lax.fori_loop(0, count, covariance, 0)
    inv_chol(xw, wp, count)

    def level1(q, _):
        cs = [4 * q + e for e in range(4)]
        w1 = [xw[c] for c in cs]
        p = [mm_nt(cc[c], w) for c, w in zip(cs, w1)]
        u = [mm_nt(a, a) for a in p]
        v = [mm_nn(a, w) for a, w in zip(p, w1)]
        for e, c in enumerate(cs):
            cc[c] = v[e]
            xw[c] = mid[c] - u[e][:128, :128]
            tt[c] = tt[c] - u[e][128:, :]
        return 0

    lax.fori_loop(0, count // 4, level1, 0)

def rest_kernel(x_in, cc, tt, g_out, w3_out, xw, wp, l32s):
    count = 16
    xw[...] = x_in[...]

    def level2(q, _):
        cs = [4 * q + e for e in range(4)]
        w2 = [xw[c] for c in cs]
        l32 = [mm_nt(tt[c, :, :128], w) for c, w in zip(cs, w2)]
        u = [mm_nt(a, a) for a in l32]
        v = [mm_nn(a, w) for a, w in zip(l32, w2)]
        for e, c in enumerate(cs):
            l32s[c] = v[e]
            xw[c] = tt[c, :, 128:] - u[e]
        return 0

    def level(b, _):
        inv_chol(xw, wp, count)

        @pl.when(b == 0)
        def _():
            lax.fori_loop(0, count // 4, level2, 0)

        return 0

    lax.fori_loop(0, 2, level, 0)

    def last(q, _):
        cs = [4 * q + e for e in range(4)]
        w3 = [xw[c] for c in cs]
        q2 = [l32s[c] for c in cs]
        q1 = [cc[c, 128:, :] - mm_nn(b, cc[c, :128, :]) for c, b in zip(cs, q2)]
        gb = [
            mm_nn(w, jnp.concatenate([a, b], 1)).astype(BF)
            for w, a, b in zip(w3, q1, q2)
        ]
        for e, c in enumerate(cs):
            w3_out[c] = w3[e]
            g_out[c] = gb[e]
        return 0

    lax.fori_loop(0, count // 4, last, 0)


VM = pl.BlockSpec(memory_space=pltpu.VMEM)
SM = pl.BlockSpec(memory_space=pltpu.SMEM)


def factor_first(first, length, nb, geo):
    return pl.pallas_call(
        first_kernel,
        out_shape=(
            jax.ShapeDtypeStruct((16, 128, 128), F32),
            jax.ShapeDtypeStruct((16, 256, 128), F32),
            jax.ShapeDtypeStruct((16, 128, 256), F32),
        ),
        in_specs=[SM, SM, VM, VM],
        out_specs=(VM, VM, VM),
        scratch_shapes=[pltpu.VMEM((4, 32, 128), F32), pltpu.VMEM((16, 128, 128), F32)],
        compiler_params=pltpu.CompilerParams(vmem_limit_bytes=20 << 20),
        name="factor_first",
    )(first, length, nb, geo)


def factor_rest(x, c, t):
    return pl.pallas_call(
        rest_kernel,
        out_shape=(
            jax.ShapeDtypeStruct((16, 128, 256), BF),
            jax.ShapeDtypeStruct((16, 128, 128), F32),
        ),
        in_specs=[VM, VM, VM],
        out_specs=(VM, VM),
        scratch_shapes=[
            pltpu.VMEM((16, 128, 128), F32),
            pltpu.VMEM((4, 32, 128), F32),
            pltpu.VMEM((16, 128, 128), F32),
        ],
        compiler_params=pltpu.CompilerParams(vmem_limit_bytes=20 << 20),
        name="factor_rest",
    )(x, c, t)


def whiten_kernel(base, first, nb, north, mid, south, g, w3, own, white, weights, term, tab):
    step = pl.program_id(0) + base

    @pl.when(step == base)
    def _():
        tab[0:2] = north[...]
        tab[2:6] = mid[...]
        tab[6:8] = south[...]

    ci, cj, w, member = window(first, nb, step)
    start = pl.multiple_of(cj * 128, 128)
    acc = mm_nt(w3[0], own[0])
    gf = g[0].astype(F32)
    point = lax.broadcasted_iota(jnp.int32, (128, 256), 0)
    pick = jnp.where(point == jnp.broadcast_to(member, (128, 256)), 1.0, 0.0).astype(BF)
    for wi in range(5):
        lhs = jnp.concatenate(
            [jnp.where(w == wi * 5 + wj, gf, 0.0).astype(BF) for wj in range(5)], 0
        )
        gs = dot(lhs, pick, NT).astype(BF)
        gs = jnp.concatenate([gs[128 * wj : 128 * wj + 128, :] for wj in range(5)], 1)
        acc = acc - dot(gs, tab[ci + wi, :, pl.ds(start, 640)], NT)
    white[0] = acc
    weights[...] = acc.astype(BF)
    eye = (
        lax.broadcasted_iota(jnp.int32, (128, 128), 0)
        == lax.broadcasted_iota(jnp.int32, (128, 128), 1)
    )
    diag = jnp.sum(jnp.where(eye, w3[0], 0.0), axis=0, keepdims=True)
    total = 0.5 * jnp.sum(acc * acc) - 256.0 * jnp.sum(jnp.log(diag))
    term[...] = jnp.full((1, 8, 128), -total / 32768.0 - 0.5 * math.log(2.0 * math.pi), F32)


def whiten(first, nb, pieces, g, w3, own, base, white=None):
    def whole(a):
        nd = a.ndim
        return pl.BlockSpec(a.shape, lambda s: (0,) * nd, pipeline_mode=pl.Buffered(1))

    if white is None:
        kernel = lambda *refs: whiten_kernel(base, *refs)
    else:
        kernel = lambda *refs: whiten_kernel(base, *refs[:8], *refs[9:])
    extra = [] if white is None else [white]
    return pl.pallas_call(
        kernel,
        grid=(8,),
        out_shape=(
            jax.ShapeDtypeStruct((16, 128, 256), F32),
            jax.ShapeDtypeStruct((1024, 256), BF),
            jax.ShapeDtypeStruct((8, 8, 128), F32),
        ),
        in_specs=[SM, whole(nb)]
        + [whole(p) for p in pieces]
        + [
            pl.BlockSpec((1, 128, 256), lambda s: (s + base, 0, 0)),
            pl.BlockSpec((1, 128, 128), lambda s: (s + base, 0, 0)),
            pl.BlockSpec((1, 256, 128), lambda s: ((s + base) // 4, 0, (s + base) % 4)),
        ]
        + [pl.BlockSpec(memory_space=pl.ANY) for _ in extra],
        out_specs=(
            pl.BlockSpec((1, 128, 256), lambda s: (s + base, 0, 0)),
            pl.BlockSpec((128, 256), lambda s: (s, 0)),
            pl.BlockSpec((1, 8, 128), lambda s: (s, 0, 0)),
        ),
        input_output_aliases={} if white is None else {8: 0},
        scratch_shapes=[pltpu.VMEM((8, 256, 1024), BF)],
        compiler_params=pltpu.CompilerParams(vmem_limit_bytes=24 << 20),
        name="whiten",
    )(first, nb, *pieces, g, w3, own, *extra)


LN2 = math.log(2.0)
TB = 1024


def pieces3(x):
    a = x.astype(BF).astype(F32)
    r = x - a
    b = r.astype(BF).astype(F32)
    return a, b, r - b


def cross_kernel(scale, tgt, pts, wa, wb, acc_in, out, rhs, total):
    def form(x, y, left):
        q = x * x + y * y
        qs = pieces3(q)
        ones = jnp.ones_like(x)
        xs, ys = pieces3(x), pieces3(y)
        m = -2.0 if left else 1.0
        rows = []
        for a, b in ((0, 0), (0, 1), (1, 0), (0, 2), (1, 1), (2, 0)):
            k = a if left else b
            rows += [xs[k] * m, ys[k] * m]
        rows += (list(qs) + [ones] * 3) if left else ([ones] * 3 + list(qs))
        rows += [jnp.zeros_like(x)] * 14
        return jnp.concatenate(rows, 0).astype(BF)

    @pl.when(pl.program_id(0) == 0)
    def _():
        rhs[...] = form(pts[0:1, :] * scale[0], pts[1:2, :] * scale[0], False)

    lhs = form(tgt[0, 0:1, :] * scale[0], tgt[0, 1:2, :] * scale[0], True)
    total[...] = acc_in[...] if acc_in is not None else jnp.zeros((TB, 256), F32)

    def chunk(b, _):
        acc = total[...]
        for w in (wa, wb):
            at = b * 256 + (1024 if w is wb else 0)
            s2 = jnp.maximum(dot(lhs, rhs[:, pl.ds(pl.multiple_of(at, 256), 256)], TN), 1e-30)
            s = s2 * lax.rsqrt(s2)
            k = (1.0 + s * LN2) * jnp.exp2(-s)
            acc = acc + dot(k.astype(BF), w[pl.ds(pl.multiple_of(b * 256, 256), 256), :], NN)
        total[...] = acc
        return 0

    lax.fori_loop(0, 4, chunk, 0)
    out[...] = total[...].astype(out.dtype)


def cross(scale, tgt, pts, w, dtype, acc=None, skip=0, name="cross"):
    n = tgt.shape[0]
    kernel = cross_kernel
    if acc is None:
        kernel = lambda s, t, p, a, b, o, r, m: cross_kernel(s, t, p, a, b, None, o, r, m)
    return pl.pallas_call(
        kernel,
        grid=(n,),
        out_shape=jax.ShapeDtypeStruct((n * TB, 256), dtype),
        in_specs=[
            pl.BlockSpec(memory_space=pltpu.SMEM),
            pl.BlockSpec((1, 2, TB), lambda s: (s, 0, 0)),
            pl.BlockSpec((2, 2048), lambda s: (0, 0)),
            pl.BlockSpec((1024, 256), lambda s: (0, 0)),
            pl.BlockSpec((1024, 256), lambda s: (0, 0)),
        ]
        + ([] if acc is None else [pl.BlockSpec((TB, 256), lambda s: (skip + s, 0))]),
        out_specs=pl.BlockSpec((TB, 256), lambda s: (s, 0)),
        scratch_shapes=[pltpu.VMEM((32, 2048), BF), pltpu.VMEM((TB, 256), F32)],
        compiler_params=pltpu.CompilerParams(vmem_limit_bytes=24 << 20),
        name=name,
    )(scale, tgt, pts, *w, *([] if acc is None else [acc]))


def sides(low, high, axis):
    count = lax.axis_size(axis)
    forward = [(i, i + 1) for i in range(count - 1)]
    backward = [(b, a) for a, b in forward]
    return lax.ppermute(high, axis, forward), lax.ppermute(low, axis, backward)


def body(values, offsets, nugget, neighbours, length_scale, target_tile, target_spots):
    row = lax.axis_index("rows")
    col = lax.axis_index("cols")
    length = length_scale[0]
    first = jnp.stack([row * 4, col * 4]).astype(jnp.int32)

    geo = jnp.concatenate(
        [offsets.transpose(1, 2, 0, 3), nugget[:, :, None, :], jnp.zeros((4, 4, 5, 128), F32)], 2
    )
    w, e = sides(geo[:, :2], geo[:, 2:], "cols")
    geo = jnp.concatenate([w, geo, e], 1)
    n, s = sides(geo[:2], geo[2:], "rows")
    geo = jnp.concatenate([n, geo, s], 0)

    own = values.transpose(1, 0, 2, 3).reshape(4, 256, 512)
    mid = own.astype(BF)
    w, e = sides(mid[:, :, :256], mid[:, :, 256:], "cols")

    tile_ids = target_tile[:, 0]
    one_hot = (tile_ids[:, None] == jnp.arange(16, dtype=jnp.int32)[None, :]).astype(jnp.int32)
    rank = jnp.sum((jnp.cumsum(one_hot, axis=0) - 1) * one_hot, axis=1)
    slot = tile_ids * 64 + rank
    send_x = jnp.zeros((1024,), F32).at[slot].set(target_spots[0])
    send_y = jnp.zeros((1024,), F32).at[slot].set(target_spots[1])
    outgoing = jnp.concatenate([send_x.reshape(16, 64), send_y.reshape(16, 64)], axis=1)
    everyone = jnp.broadcast_to(outgoing[:, None, :], (16, 8, 128)).reshape(128, 1, 128)
    spots = lax.all_to_all(everyone, ("rows", "cols"), split_axis=0, concat_axis=0, tiled=True)
    spots = spots.reshape(16, 8, 2, 64).transpose(1, 2, 0, 3).reshape(4, 2, 2, 1024)
    band, half = col // 2, col % 2
    spots = lax.dynamic_index_in_dim(spots, half, 1, keepdims=False)
    spots = jnp.take(spots, (band + jnp.array([2, 1, 3, 0], jnp.int32)) % 4, axis=0)
    mid_y = (band * 8 + 4).astype(F32)
    tgt = jnp.stack([spots[:, 0] * 4.0 - 2.0, spots[:, 1] * 32.0 - mid_y], 1)
    tgt = tgt.reshape(4, 2, 1024 // TB, TB).transpose(0, 2, 1, 3).reshape(-1, 2, TB)
    px = offsets[0] + (jnp.arange(4, dtype=F32) - 2.0)[:, None, None]
    py = offsets[1] + (jnp.arange(4, dtype=F32) - 4.0 + 4.0 * half.astype(F32))[None, :, None]
    pts = jnp.stack([px.reshape(-1), py.reshape(-1)])
    partner = [(c, c ^ 1) for c in range(8)]
    pts2 = lax.ppermute(pts, "cols", partner)

    state = factor_first(first, length_scale, neighbours, geo)
    mid = jnp.concatenate([w, mid, e], 2)
    *state, mid = lax.optimization_barrier((*state, mid))
    n, s = sides(mid[:2], mid[2:], "rows")
    around = [n, mid, s]
    g, w3 = factor_rest(*state)
    white, w_a, term_a = whiten(first, neighbours, around, g, w3, own, 0)
    far_a = lax.ppermute(w_a, "cols", partner)
    white, w_b, term_b = whiten(first, neighbours, around, g, w3, own, 8, white)
    far_b = lax.ppermute(w_b, "cols", partner)
    term = jnp.concatenate([term_a[:, 0, 0], term_b[:, 0, 0]])

    scale = jnp.stack([math.sqrt(3.0) / LN2 / length])
    near = cross(scale, tgt, pts, (w_a, w_b), F32, name="cross_near")
    per = 1024 // TB
    parts = []
    for i, k in enumerate((2, 1, 3)):
        part = cross(
            scale, tgt[per * i : per * i + per], pts2, (far_a, far_b), BF, near, per * i, "cross_far"
        )
        parts.append(lax.ppermute(part, "cols", [(c, (c + 2 * k) % 8) for c in range(8)]))
    here = cross(scale, tgt[3 * per :], pts2, (far_a, far_b), F32, near, 3 * per, "cross_here")
    predicted = here + (parts[0].astype(F32) + parts[1].astype(F32) + parts[2].astype(F32))
    predicted = (predicted * (1.0 / 128.0)).astype(BF)
    returned = lax.all_to_all(
        predicted.reshape(16, 64, 256), "rows", split_axis=0, concat_axis=0, tiled=True
    )
    predictions = returned.reshape(-1, 256)[slot].astype(F32)
    return (white.reshape(4, 4, 128, 256), term.reshape(4, 4), predictions)


def solution(mesh):
    return jax.shard_map(
        body,
        mesh=mesh,
        in_specs=(
            P(None, "rows", "cols", None),
            P(None, "rows", "cols", None),
            P("rows", "cols", None),
            P("rows", "cols", None),
            P(),
            P(("rows", "cols"), None),
            P(None, ("rows", "cols")),
        ),
        out_specs=(P("rows", "cols", None, None), P("rows", "cols"), P(("rows", "cols"), None)),
        check_vma=False,
    )
```

```python
import math

import jax
import jax.numpy as jnp

from jax import lax
from jax.experimental import pallas as pl
from jax.experimental.pallas import tpu as pltpu
from jax.sharding import PartitionSpec as P

F32 = jnp.float32
BF = jnp.bfloat16
NN = (((1,), (0,)), ((), ()))
NT = (((1,), (1,)), ((), ()))
TN = (((0,), (0,)), ((), ()))


def split(x):
    hi = x.astype(BF)
    return hi, (x - hi.astype(F32)).astype(BF)


def dot(a, b, dims):
    return lax.dot_general(a, b, dims, preferred_element_type=F32)


def mm_nt(a, b):
    ah, al = split(a)
    bh, bl = split(b)
    return dot(jnp.concatenate([ah, ah, al], 1), jnp.concatenate([bh, bl, bh], 1), NT)


def mm_nn(a, b):
    ah, al = split(a)
    bh, bl = split(b)
    return dot(jnp.concatenate([ah, ah, al], 1), jnp.concatenate([bh, bl, bh], 0), NN)


def lane_take(x, idx):
    return jnp.take_along_axis(x, idx, axis=1, mode="promise_in_bounds")


def recip(p):
    r = pl.reciprocal(p, approx=True)
    return r * (2.0 - p * r)


def leaf_factor(leaf, lane, sub):
    base = lane & 96
    col = lane & 31
    x = [list(p) for p in leaf]
    ones = jnp.ones((8, 128), F32)
    piv = [[[ones, jnp.zeros((8, 128), F32), ones] for _ in range(4)] for _ in range(4)]

    def spread_row(t, s):
        return jnp.broadcast_to(t[s : s + 1, :], (8, 128))

    for j in range(0, 32, 2):
        v0, s0 = divmod(j, 8)
        first, second = base + j, base + j + 1
        unit0 = jnp.where(col == j, 1.0, 0.0)
        unit1 = jnp.where(col == j + 1, 1.0, 0.0)
        below = sub > s0 + 1
        here = (sub == s0) | (sub == s0 + 1)
        for p in range(4):
            c0 = [lane_take(x[p][v], first) for v in range(v0, 4)]
            c1 = [lane_take(x[p][v], second) for v in range(v0, 4)]
            a, b, d = spread_row(c0[0], s0), spread_row(c0[0], s0 + 1), spread_row(c1[0], s0 + 1)
            r = recip(a * d - b * b)
            r0 = spread_row(x[p][v0], s0) + unit0
            r1 = spread_row(x[p][v0], s0 + 1) + unit1
            w0 = d * r0 - b * r1
            w1 = a * r1 - b * r0
            for i, new in enumerate((a, b, d)):
                piv[p][v0][i] = jnp.where(here, new, piv[p][v0][i])
            for v in range(v0, 4):
                if v == v0 and s0 == 6:
                    continue
                t = c0[v - v0] * w0 + c1[v - v0] * w1
                if v == v0:
                    t = jnp.where(below, t, 0.0)
                x[p][v] = x[p][v] - t * r
    odd = (sub & 1) == 1
    out = []
    for p in range(4):
        o = []
        for v in range(4):
            a, b, d = piv[p][v]
            f = jnp.where(odd, b * recip(a), 0.0)
            e = jnp.where(odd, d - b * f, a)
            q = lax.rsqrt(e)
            q = q * (1.5 - 0.5 * e * q * q)
            r_i = sub + 8 * v
            n = jnp.where(col < (r_i & 30), x[p][v], jnp.where(col == r_i, 1.0, 0.0))
            o.append(q * (n - f * pltpu.roll(n, 1, axis=0)))
        out.append(o)
    return out


def inv_chol(xw, wp, count):
    lane8 = lax.broadcasted_iota(jnp.int32, (8, 128), 1)
    sub8 = lax.broadcasted_iota(jnp.int32, (8, 128), 0)
    lane = lax.broadcasted_iota(jnp.int32, (32, 128), 1)
    subl = lax.broadcasted_iota(jnp.int32, (32, 128), 0)
    for k in range(4):
        lo = 32 * k
        for base in range(0, count, 16):
            leaf = []
            for p in range(4):
                tiles = []
                for v in range(4):
                    acc = None
                    for g in range(4):
                        t = xw[base + 4 * p + g, lo + 8 * v : lo + 8 * v + 8, :]
                        t = pltpu.roll(t, (32 * (g - k)) % 128, axis=1) if g != k else t
                        acc = t if acc is None else jnp.where(lane8 // 32 == g, t, acc)
                    tiles.append(acc)
                leaf.append(tiles)
            inv = leaf_factor(leaf, lane8, sub8)
            for p in range(4):
                for v in range(4):
                    wp[p, 8 * v : 8 * v + 8, :] = inv[p][v]

            def apply(q, _):
                cs = [base + 8 * q + e for e in range(8)]
                xs = [xw[c] for c in cs]
                ws = [wp[2 * q], wp[2 * q + 1]]
                ts = []
                for e in range(8):
                    g = e % 4
                    gi = 32 * g + (lane8 & 31)
                    w = ws[e // 4]
                    wr = jnp.concatenate(
                        [lane_take(w[8 * v : 8 * v + 8], gi) for v in range(4)], 0
                    )
                    wh = wr.astype(BF).astype(F32)
                    lhs = jnp.where(lane < 64, wh, wr - wh).astype(BF)
                    r = xs[e][lo : lo + 32, :]
                    r = jnp.where(lane // 32 == k, jnp.where((lane & 31) == subl, 1.0, 0.0), r)
                    rh, rl = split(r)
                    ts.append(dot(lhs, jnp.concatenate([rh, rl, rh, rl], 0), NN))
                if k < 3:
                    n = 96 - lo
                    ln = lax.broadcasted_iota(jnp.int32, (n, 128), 1)
                    ls = []
                    for e in range(8):
                        g = e % 4
                        w = ws[e // 4]
                        w = pltpu.roll(w, (32 * (k - g)) % 128, axis=1) if g != k else w
                        w = jnp.where(lane // 32 == k, w, 0.0)
                        wh, wl = split(w)
                        wh = jnp.concatenate([wh] * 4, 0)
                        wl = jnp.concatenate([wl] * 4, 0)
                        xh, xl = split(xs[e][lo + 32 :, :])
                        ls.append(
                            dot(
                                jnp.concatenate([xh, xl, xh], 1),
                                jnp.concatenate([wh, wh, wl], 1),
                                NT,
                            )
                        )
                    us = []
                    for e in range(8):
                        lh = ls[e].astype(BF).astype(F32)
                        lhs = jnp.where(ln < 64, lh, ls[e] - lh).astype(BF)
                        th, tl = split(ts[e])
                        us.append(dot(lhs, jnp.concatenate([th, tl, th, tl], 0), NN))
                for e in range(8):
                    c = cs[e]
                    xw[c, lo : lo + 32, :] = jnp.where(lane < lo + 32, ts[e], 0.0)
                    if k < 3:
                        rest = xs[e][lo + 32 :, :]
                        xw[c, lo + 32 :, :] = jnp.where(ln // 32 == k, 0.0, rest) - us[e]
                return 0

            lax.fori_loop(0, 2, apply, 0)


def window(first, nb, c):
    ci, cj = c // 4, c % 4
    idx = nb[ci, pl.ds(cj, 1), :]
    gx = idx >> 12
    gy = (idx >> 7) & 31
    w = (gx - (first[0] + ci) + 2) * 5 + (gy - (first[1] + cj) + 2)
    return ci, cj, w, idx & 127


def factor_kernel(first, length, nb, geo, g_out, w3_out, xw, wp, mid, cc, tt, l32s):
    count = 16
    lane8 = lax.broadcasted_iota(jnp.int32, (8, 128), 1)
    sub8 = lax.broadcasted_iota(jnp.int32, (8, 128), 0)
    scale = math.sqrt(3.0) / length[0]
    eye = (
        lax.broadcasted_iota(jnp.int32, (128, 128), 0)
        == lax.broadcasted_iota(jnp.int32, (128, 128), 1)
    )

    def covariance(c, _):
        ci, cj, w, member = window(first, nb, c)
        parts = []
        for h in range(2):
            wb = jnp.broadcast_to(w[:, 128 * h : 128 * h + 128], (8, 128))
            mb = jnp.broadcast_to(member[:, 128 * h : 128 * h + 128], (8, 128))
            acc = jnp.zeros((8, 128), F32)
            for wi in range(5):
                for wj in range(5):
                    if wi == 2 and wj == 2:
                        continue
                    shift = jnp.where(
                        sub8 == 0, float(wi - 2), jnp.where(sub8 == 1, float(wj - 2), 0.0)
                    )
                    t = lane_take(geo[ci + wi, cj + wj], mb) + shift
                    acc = jnp.where(wb == wi * 5 + wj, t, acc)
            parts.append(acc)
        parts.append(geo[ci + 2, cj + 2])
        pts = jnp.concatenate(parts, 1)
        cols = jnp.transpose(pts * scale)
        rows = pts * scale

        def block(a, b):
            dx = cols[128 * a : 128 * a + 128, 0:1] - rows[0:1, 128 * b : 128 * b + 128]
            dy = cols[128 * a : 128 * a + 128, 1:2] - rows[1:2, 128 * b : 128 * b + 128]
            s2 = dx * dx + dy * dy
            s = s2 * lax.rsqrt(jnp.maximum(s2, 1e-30))
            k = (1.0 + s) * jnp.exp(-s)
            if a == b:
                k = k + jnp.where(eye, pts[2:3, 128 * b : 128 * b + 128], 0.0)
            return k

        xw[c] = block(0, 0)
        cc[c, :128, :] = block(1, 0)
        cc[c, 128:, :] = block(2, 0)
        mid[c] = block(1, 1)
        tt[c, :, :128] = block(2, 1)
        tt[c, :, 128:] = block(2, 2)
        return 0

    lax.fori_loop(0, count, covariance, 0)
    def level1(q, _):
        cs = [4 * q + e for e in range(4)]
        w1 = [xw[c] for c in cs]
        p = [mm_nt(cc[c], w) for c, w in zip(cs, w1)]
        u = [mm_nt(a, a) for a in p]
        v = [mm_nn(a, w) for a, w in zip(p, w1)]
        for e, c in enumerate(cs):
            cc[c] = v[e]
            xw[c] = mid[c] - u[e][:128, :128]
            tt[c] = tt[c] - u[e][128:, :]
        return 0

    def level2(q, _):
        cs = [4 * q + e for e in range(4)]
        w2 = [xw[c] for c in cs]
        l32 = [mm_nt(tt[c, :, :128], w) for c, w in zip(cs, w2)]
        u = [mm_nt(a, a) for a in l32]
        v = [mm_nn(a, w) for a, w in zip(l32, w2)]
        for e, c in enumerate(cs):
            l32s[c] = v[e]
            xw[c] = tt[c, :, 128:] - u[e]
        return 0

    def level(b, _):
        inv_chol(xw, wp, count)

        @pl.when(b == 0)
        def _():
            lax.fori_loop(0, count // 4, level1, 0)

        @pl.when(b == 1)
        def _():
            lax.fori_loop(0, count // 4, level2, 0)

        return 0

    lax.fori_loop(0, 3, level, 0)

    def last(q, _):
        cs = [4 * q + e for e in range(4)]
        w3 = [xw[c] for c in cs]
        q2 = [l32s[c] for c in cs]
        q1 = [cc[c, 128:, :] - mm_nn(b, cc[c, :128, :]) for c, b in zip(cs, q2)]
        gb = [
            mm_nn(w, jnp.concatenate([a, b], 1)).astype(BF)
            for w, a, b in zip(w3, q1, q2)
        ]
        for e, c in enumerate(cs):
            w3_out[c] = w3[e]
            g_out[c] = gb[e]
        return 0

    lax.fori_loop(0, count // 4, last, 0)


VM = pl.BlockSpec(memory_space=pltpu.VMEM)
SM = pl.BlockSpec(memory_space=pltpu.SMEM)


def factor(first, length, nb, geo):
    return pl.pallas_call(
        factor_kernel,
        out_shape=(
            jax.ShapeDtypeStruct((16, 128, 256), BF),
            jax.ShapeDtypeStruct((16, 128, 128), F32),
        ),
        in_specs=[SM, SM, VM, VM],
        out_specs=(VM, VM),
        scratch_shapes=[
            pltpu.VMEM((16, 128, 128), F32),
            pltpu.VMEM((4, 32, 128), F32),
            pltpu.VMEM((16, 128, 128), F32),
            pltpu.VMEM((16, 256, 128), F32),
            pltpu.VMEM((16, 128, 256), F32),
            pltpu.VMEM((16, 128, 128), F32),
        ],
        compiler_params=pltpu.CompilerParams(vmem_limit_bytes=20 << 20),
        name="factor",
    )(first, length, nb, geo)


def whiten_kernel(first, nb, north, mid, south, g, w3, own, white, weights, term, tab, acc):
    ci = pl.program_id(0)

    @pl.when(ci == 0)
    def _():
        tab[0:2] = north[...]
        tab[2:6] = mid[...]
        tab[6:8] = south[...]

    point = lax.broadcasted_iota(jnp.int32, (128, 256), 0)
    near = []
    for cj in range(4):
        _, _, w, member = window(first, nb, 4 * ci + cj)
        pick = jnp.where(point == jnp.broadcast_to(member, (128, 256)), 1.0, 0.0).astype(BF)
        near.append((w, pick, g[cj].astype(F32)))
        acc[128 * cj : 128 * cj + 128, :] = mm_nt(w3[cj], own[0, :, 128 * cj : 128 * cj + 128])
    blank = [jnp.zeros((128, 128), BF)] * 4

    def one_row(wi, _):
        rows = []
        for cj in range(4):
            w, pick, gf = near[cj]
            lhs = jnp.concatenate(
                [jnp.where(w == wi * 5 + wj, gf, 0.0).astype(BF) for wj in range(5)], 0
            )
            gs = dot(lhs, pick, NT).astype(BF)
            blocks = [gs[128 * wj : 128 * wj + 128, :] for wj in range(5)]
            rows.append(jnp.concatenate(blank[:cj] + blocks + blank[cj + 1 :], 1))
        acc[...] = acc[...] - dot(jnp.concatenate(rows, 0), tab[ci + wi], NT)
        return 0

    lax.fori_loop(0, 5, one_row, 0)
    weights[...] = acc[...].astype(BF)
    eye = (
        lax.broadcasted_iota(jnp.int32, (128, 128), 0)
        == lax.broadcasted_iota(jnp.int32, (128, 128), 1)
    )
    for cj in range(4):
        out = acc[128 * cj : 128 * cj + 128, :]
        white[cj] = out
        diag = jnp.sum(jnp.where(eye, w3[cj], 0.0), axis=0, keepdims=True)
        total = 0.5 * jnp.sum(out * out) - 256.0 * jnp.sum(jnp.log(diag))
        value = -total / 32768.0 - 0.5 * math.log(2.0 * math.pi)
        term[0, cj : cj + 1, :] = jnp.full((1, 128), value, F32)


def whiten(first, nb, pieces, g, w3, own):
    def whole(a):
        nd = a.ndim
        return pl.BlockSpec(a.shape, lambda s: (0,) * nd, pipeline_mode=pl.Buffered(1))

    return pl.pallas_call(
        whiten_kernel,
        grid=(4,),
        out_shape=(
            jax.ShapeDtypeStruct((16, 128, 256), F32),
            jax.ShapeDtypeStruct((2048, 256), BF),
            jax.ShapeDtypeStruct((4, 8, 128), F32),
        ),
        in_specs=[SM, whole(nb)]
        + [whole(p) for p in pieces]
        + [
            pl.BlockSpec((4, 128, 256), lambda s: (s, 0, 0)),
            pl.BlockSpec((4, 128, 128), lambda s: (s, 0, 0)),
            pl.BlockSpec((1, 256, 512), lambda s: (s, 0, 0)),
        ],
        out_specs=(
            pl.BlockSpec((4, 128, 256), lambda s: (s, 0, 0)),
            pl.BlockSpec((512, 256), lambda s: (s, 0)),
            pl.BlockSpec((1, 8, 128), lambda s: (s, 0, 0)),
        ),
        scratch_shapes=[pltpu.VMEM((8, 256, 1024), BF), pltpu.VMEM((512, 256), F32)],
        compiler_params=pltpu.CompilerParams(vmem_limit_bytes=24 << 20),
        name="whiten",
    )(first, nb, *pieces, g, w3, own)


LN2 = math.log(2.0)
TB = 1024
FAR = 1


def pieces3(x):
    a = x.astype(BF).astype(F32)
    r = x - a
    b = r.astype(BF).astype(F32)
    return a, b, r - b


def cross_kernel(loops, scale, tgt, pts, w, acc_in, out, rhs, total):
    def form(x, y, left):
        q = x * x + y * y
        qs = pieces3(q)
        ones = jnp.ones_like(x)
        xs, ys = pieces3(x), pieces3(y)
        m = -2.0 if left else 1.0
        rows = []
        for a, b in ((0, 0), (0, 1), (1, 0), (0, 2), (1, 1), (2, 0)):
            k = a if left else b
            rows += [xs[k] * m, ys[k] * m]
        rows += (list(qs) + [ones] * 3) if left else ([ones] * 3 + list(qs))
        rows += [jnp.zeros_like(x)] * 14
        return jnp.concatenate(rows, 0).astype(BF)

    @pl.when(pl.program_id(0) == 0)
    def _():
        rhs[...] = form(pts[0:1, :] * scale[0], pts[1:2, :] * scale[0], False)

    lhs = form(tgt[0, 0:1, :] * scale[0], tgt[0, 1:2, :] * scale[0], True)
    def chunk(at, acc):
        s2 = jnp.maximum(dot(lhs, rhs[:, pl.ds(at, 256)], TN), 1e-30)
        s = s2 * lax.rsqrt(s2)
        k = (1.0 + s * LN2) * jnp.exp2(-s)
        return acc + dot(k.astype(BF), w[pl.ds(at, 256), :], NN)

    acc = acc_in[...] if acc_in is not None else jnp.zeros((TB, 256), F32)
    per = 8 // loops
    if loops == 1:
        for e in range(8):
            acc = chunk(256 * e, acc)
        out[...] = acc.astype(out.dtype)
        return
    total[...] = acc

    def some(b, _):
        acc = total[...]
        for e in range(per):
            acc = chunk(pl.multiple_of((b * per + e) * 256, 256), acc)
        total[...] = acc
        return 0

    lax.fori_loop(0, loops, some, 0)
    out[...] = total[...].astype(out.dtype)


def cross(scale, tgt, pts, w, dtype, acc=None, skip=0, name="cross", loops=1):
    n = tgt.shape[0]
    if acc is None:
        kernel = lambda s, t, p, w, o, r, m: cross_kernel(loops, s, t, p, w, None, o, r, m)
    else:
        kernel = lambda *refs: cross_kernel(loops, *refs)
    return pl.pallas_call(
        kernel,
        grid=(n,),
        out_shape=jax.ShapeDtypeStruct((n * TB, 256), dtype),
        in_specs=[
            pl.BlockSpec(memory_space=pltpu.SMEM),
            pl.BlockSpec((1, 2, TB), lambda s: (s, 0, 0)),
            pl.BlockSpec((2, 2048), lambda s: (0, 0)),
            pl.BlockSpec((2048, 256), lambda s: (0, 0)),
        ]
        + ([] if acc is None else [pl.BlockSpec((TB, 256), lambda s: (skip + s, 0))]),
        out_specs=pl.BlockSpec((TB, 256), lambda s: (s, 0)),
        scratch_shapes=[pltpu.VMEM((32, 2048), BF), pltpu.VMEM((TB, 256), F32)],
        compiler_params=pltpu.CompilerParams(vmem_limit_bytes=24 << 20),
        name=name,
    )(scale, tgt, pts, w, *([] if acc is None else [acc]))


def sort_kernel(tile, spots, out, slot):
    t = tile[...]
    named = lax.broadcasted_iota(jnp.int32, (16, 512), 0) == jnp.broadcast_to(t, (16, 512))
    hot = jnp.where(named, 1.0, 0.0)
    before = lax.broadcasted_iota(jnp.int32, (512, 512), 0) < lax.broadcasted_iota(
        jnp.int32, (512, 512), 1
    )
    counts = dot(hot.astype(BF), jnp.where(before, 1.0, 0.0).astype(BF), NN)
    rank = jnp.sum(counts * hot, axis=0, keepdims=True).astype(jnp.int32)
    slot[...] = t * 64 + rank
    at = lax.broadcasted_iota(jnp.int32, (128, 512), 0) & 63
    place = jnp.where(at == jnp.broadcast_to(rank, (128, 512)), 1.0, 0.0).astype(BF)
    moved = []
    for i in range(2):
        parts = [hot * p for p in pieces3(spots[i : i + 1, :])]
        m = dot(jnp.concatenate(parts, 0).astype(BF), place, NT)
        moved.append(m[:16] + m[16:32] + m[32:48])
    lane = lax.broadcasted_iota(jnp.int32, (16, 128), 1)
    row = jnp.where(lane < 64, moved[0], moved[1])
    for g in range(16):
        out[g] = jnp.broadcast_to(row[g : g + 1, :], (8, 128))


def sort_targets(tile, spots):
    return pl.pallas_call(
        sort_kernel,
        out_shape=(
            jax.ShapeDtypeStruct((16, 8, 128), F32),
            jax.ShapeDtypeStruct((1, 512), jnp.int32),
        ),
        in_specs=[VM, VM],
        out_specs=(VM, VM),
        compiler_params=pltpu.CompilerParams(vmem_limit_bytes=8 << 20),
        name="sort_targets",
    )(tile, spots)


def sides(low, high, axis):
    count = lax.axis_size(axis)
    forward = [(i, i + 1) for i in range(count - 1)]
    backward = [(b, a) for a, b in forward]
    return lax.ppermute(high, axis, forward), lax.ppermute(low, axis, backward)


def body(values, offsets, nugget, neighbours, length_scale, target_tile, target_spots):
    row = lax.axis_index("rows")
    col = lax.axis_index("cols")
    length = length_scale[0]
    first = jnp.stack([row * 4, col * 4]).astype(jnp.int32)

    geo = jnp.concatenate(
        [offsets.transpose(1, 2, 0, 3), nugget[:, :, None, :], jnp.zeros((4, 4, 5, 128), F32)], 2
    )
    w, e = sides(geo[:, :2], geo[:, 2:], "cols")
    geo = jnp.concatenate([w, geo, e], 1)
    n, s = sides(geo[:2], geo[2:], "rows")
    geo = jnp.concatenate([n, geo, s], 0)

    own = values.transpose(1, 0, 2, 3).reshape(4, 256, 512)
    mid = own.astype(BF)
    w, e = sides(mid[:, :, :256], mid[:, :, 256:], "cols")

    everyone, slot = sort_targets(target_tile.reshape(1, 512), target_spots)
    everyone = everyone.reshape(128, 1, 128)
    spots = lax.all_to_all(everyone, ("rows", "cols"), split_axis=0, concat_axis=0, tiled=True)
    spots = spots.reshape(16, 8, 2, 64).transpose(1, 2, 0, 3).reshape(4, 2, 2, 1024)
    band, half = col // 2, col % 2
    spots = lax.dynamic_index_in_dim(spots, half, 1, keepdims=False)
    spots = jnp.take(spots, (band + jnp.array([2, 1, 3, 0], jnp.int32)) % 4, axis=0)
    mid_y = (band * 8 + 4).astype(F32)
    tgt = jnp.stack([spots[:, 0] * 4.0 - 2.0, spots[:, 1] * 32.0 - mid_y], 1)
    tgt = tgt.reshape(4, 2, 1024 // TB, TB).transpose(0, 2, 1, 3).reshape(-1, 2, TB)
    px = offsets[0] + (jnp.arange(4, dtype=F32) - 2.0)[:, None, None]
    py = offsets[1] + (jnp.arange(4, dtype=F32) - 4.0 + 4.0 * half.astype(F32))[None, :, None]
    pts = jnp.stack([px.reshape(-1), py.reshape(-1)])
    partner = [(c, c ^ 1) for c in range(8)]
    pts2 = lax.ppermute(pts, "cols", partner)

    first, w, e = lax.optimization_barrier((first, w, e))
    mid = jnp.concatenate([w, mid, e], 2)
    n, s = sides(mid[:2], mid[2:], "rows")
    around = [n, mid, s]
    g, w3 = factor(first, length_scale, neighbours, geo)
    white, weights, term = whiten(first, neighbours, around, g, w3, own)
    scale = jnp.stack([math.sqrt(3.0) / LN2 / length])
    weights2 = lax.ppermute(weights, "cols", partner)
    near = cross(scale, tgt, pts, weights, F32, name="cross_near")
    per = 1024 // TB
    parts = []
    for i, k in enumerate((2, 1, 3)):
        part = cross(
            scale, tgt[per * i : per * i + per], pts2, weights2, BF, near, per * i, "cross_far", FAR
        )
        parts.append(lax.ppermute(part, "cols", [(c, (c + 2 * k) % 8) for c in range(8)]))
    here = cross(scale, tgt[3 * per :], pts2, weights2, F32, near, 3 * per, "cross_here", FAR)
    predicted = here + (parts[0].astype(F32) + parts[1].astype(F32) + parts[2].astype(F32))
    predicted = (predicted * (1.0 / 128.0)).astype(BF)
    returned = lax.all_to_all(
        predicted.reshape(16, 64, 256), "rows", split_axis=0, concat_axis=0, tiled=True
    )
    predictions = returned.reshape(-1, 256)[slot.reshape(512)].astype(F32)
    return (white.reshape(4, 4, 128, 256), term[:, :4, 0], predictions)


def solution(mesh):
    return jax.shard_map(
        body,
        mesh=mesh,
        in_specs=(
            P(None, "rows", "cols", None),
            P(None, "rows", "cols", None),
            P("rows", "cols", None),
            P("rows", "cols", None),
            P(),
            P(("rows", "cols"), None),
            P(None, ("rows", "cols")),
        ),
        out_specs=(P("rows", "cols", None, None), P("rows", "cols"), P(("rows", "cols"), None)),
        check_vma=False,
    )
```

```python
import math

import jax
import jax.numpy as jnp

from jax import lax
from jax.experimental import pallas as pl
from jax.experimental.pallas import tpu as pltpu
from jax.sharding import PartitionSpec as P

F32 = jnp.float32
BF = jnp.bfloat16
NN = (((1,), (0,)), ((), ()))
NT = (((1,), (1,)), ((), ()))
TN = (((0,), (0,)), ((), ()))


def split(x):
    hi = x.astype(BF)
    return hi, (x - hi.astype(F32)).astype(BF)


def dot(a, b, dims):
    return lax.dot_general(a, b, dims, preferred_element_type=F32)


def mm_nt(a, b):
    ah, al = split(a)
    bh, bl = split(b)
    return dot(jnp.concatenate([ah, ah, al], 1), jnp.concatenate([bh, bl, bh], 1), NT)


def mm_nn(a, b):
    ah, al = split(a)
    bh, bl = split(b)
    return dot(jnp.concatenate([ah, ah, al], 1), jnp.concatenate([bh, bl, bh], 0), NN)


def lane_take(x, idx):
    return jnp.take_along_axis(x, idx, axis=1, mode="promise_in_bounds")


def recip(p):
    r = pl.reciprocal(p, approx=True)
    return r * (2.0 - p * r)


def leaf_factor(leaf, lane, sub):
    base = lane & 96
    col = lane & 31
    x = [list(p) for p in leaf]
    ones = jnp.ones((8, 128), F32)
    piv = [[[ones, jnp.zeros((8, 128), F32), ones] for _ in range(4)] for _ in range(4)]

    def spread_row(t, s):
        return jnp.broadcast_to(t[s : s + 1, :], (8, 128))

    for j in range(0, 32, 2):
        v0, s0 = divmod(j, 8)
        first, second = base + j, base + j + 1
        unit0 = jnp.where(col == j, 1.0, 0.0)
        unit1 = jnp.where(col == j + 1, 1.0, 0.0)
        below = sub > s0 + 1
        here = (sub == s0) | (sub == s0 + 1)
        for p in range(4):
            c0 = [lane_take(x[p][v], first) for v in range(v0, 4)]
            c1 = [lane_take(x[p][v], second) for v in range(v0, 4)]
            a, b, d = spread_row(c0[0], s0), spread_row(c0[0], s0 + 1), spread_row(c1[0], s0 + 1)
            r = recip(a * d - b * b)
            r0 = spread_row(x[p][v0], s0) + unit0
            r1 = spread_row(x[p][v0], s0 + 1) + unit1
            w0 = d * r0 - b * r1
            w1 = a * r1 - b * r0
            for i, new in enumerate((a, b, d)):
                piv[p][v0][i] = jnp.where(here, new, piv[p][v0][i])
            for v in range(v0, 4):
                if v == v0 and s0 == 6:
                    continue
                t = c0[v - v0] * w0 + c1[v - v0] * w1
                if v == v0:
                    t = jnp.where(below, t, 0.0)
                x[p][v] = x[p][v] - t * r
    odd = (sub & 1) == 1
    out = []
    for p in range(4):
        o = []
        for v in range(4):
            a, b, d = piv[p][v]
            f = jnp.where(odd, b * recip(a), 0.0)
            e = jnp.where(odd, d - b * f, a)
            q = lax.rsqrt(e)
            q = q * (1.5 - 0.5 * e * q * q)
            r_i = sub + 8 * v
            n = jnp.where(col < (r_i & 30), x[p][v], jnp.where(col == r_i, 1.0, 0.0))
            o.append(q * (n - f * pltpu.roll(n, 1, axis=0)))
        out.append(o)
    return out


def inv_chol(xw, wp, count):
    lane8 = lax.broadcasted_iota(jnp.int32, (8, 128), 1)
    sub8 = lax.broadcasted_iota(jnp.int32, (8, 128), 0)
    lane = lax.broadcasted_iota(jnp.int32, (32, 128), 1)
    subl = lax.broadcasted_iota(jnp.int32, (32, 128), 0)
    for k in range(4):
        lo = 32 * k
        for base in range(0, count, 16):
            leaf = []
            for p in range(4):
                tiles = []
                for v in range(4):
                    acc = None
                    for g in range(4):
                        t = xw[base + 4 * p + g, lo + 8 * v : lo + 8 * v + 8, :]
                        t = pltpu.roll(t, (32 * (g - k)) % 128, axis=1) if g != k else t
                        acc = t if acc is None else jnp.where(lane8 // 32 == g, t, acc)
                    tiles.append(acc)
                leaf.append(tiles)
            inv = leaf_factor(leaf, lane8, sub8)
            for p in range(4):
                for v in range(4):
                    wp[p, 8 * v : 8 * v + 8, :] = inv[p][v]

            def apply(q, _):
                cs = [base + 8 * q + e for e in range(8)]
                xs = [xw[c] for c in cs]
                ws = [wp[2 * q], wp[2 * q + 1]]
                ts = []
                for e in range(8):
                    g = e % 4
                    gi = 32 * g + (lane8 & 31)
                    w = ws[e // 4]
                    wr = jnp.concatenate(
                        [lane_take(w[8 * v : 8 * v + 8], gi) for v in range(4)], 0
                    )
                    wh = wr.astype(BF).astype(F32)
                    lhs = jnp.where(lane < 64, wh, wr - wh).astype(BF)
                    r = xs[e][lo : lo + 32, :]
                    r = jnp.where(lane // 32 == k, jnp.where((lane & 31) == subl, 1.0, 0.0), r)
                    rh, rl = split(r)
                    ts.append(dot(lhs, jnp.concatenate([rh, rl, rh, rl], 0), NN))
                if k < 3:
                    n = 96 - lo
                    ln = lax.broadcasted_iota(jnp.int32, (n, 128), 1)
                    ls = []
                    for e in range(8):
                        g = e % 4
                        w = ws[e // 4]
                        w = pltpu.roll(w, (32 * (k - g)) % 128, axis=1) if g != k else w
                        w = jnp.where(lane // 32 == k, w, 0.0)
                        wh, wl = split(w)
                        wh = jnp.concatenate([wh] * 4, 0)
                        wl = jnp.concatenate([wl] * 4, 0)
                        xh, xl = split(xs[e][lo + 32 :, :])
                        ls.append(
                            dot(
                                jnp.concatenate([xh, xl, xh], 1),
                                jnp.concatenate([wh, wh, wl], 1),
                                NT,
                            )
                        )
                    us = []
                    for e in range(8):
                        lh = ls[e].astype(BF).astype(F32)
                        lhs = jnp.where(ln < 64, lh, ls[e] - lh).astype(BF)
                        th, tl = split(ts[e])
                        us.append(dot(lhs, jnp.concatenate([th, tl, th, tl], 0), NN))
                for e in range(8):
                    c = cs[e]
                    xw[c, lo : lo + 32, :] = jnp.where(lane < lo + 32, ts[e], 0.0)
                    if k < 3:
                        rest = xs[e][lo + 32 :, :]
                        xw[c, lo + 32 :, :] = jnp.where(ln // 32 == k, 0.0, rest) - us[e]
                return 0

            lax.fori_loop(0, 2, apply, 0)


def window(first, nb, c):
    ci, cj = c // 4, c % 4
    idx = nb[ci, pl.ds(cj, 1), :]
    gx = idx >> 12
    gy = (idx >> 7) & 31
    w = (gx - (first[0] + ci) + 2) * 5 + (gy - (first[1] + cj) + 2)
    return ci, cj, w, idx & 127


def factor_kernel(first, length, nb, geo, g_out, w3_out, xw, wp, mid, cc, tt, l32s):
    count = 16
    lane8 = lax.broadcasted_iota(jnp.int32, (8, 128), 1)
    sub8 = lax.broadcasted_iota(jnp.int32, (8, 128), 0)
    scale = math.sqrt(3.0) / length[0]
    eye = (
        lax.broadcasted_iota(jnp.int32, (128, 128), 0)
        == lax.broadcasted_iota(jnp.int32, (128, 128), 1)
    )

    def covariance(c, _):
        ci, cj, w, member = window(first, nb, c)
        parts = []
        for h in range(2):
            wb = jnp.broadcast_to(w[:, 128 * h : 128 * h + 128], (8, 128))
            mb = jnp.broadcast_to(member[:, 128 * h : 128 * h + 128], (8, 128))
            acc = jnp.zeros((8, 128), F32)
            for wi in range(5):
                for wj in range(5):
                    if wi == 2 and wj == 2:
                        continue
                    shift = jnp.where(
                        sub8 == 0, float(wi - 2), jnp.where(sub8 == 1, float(wj - 2), 0.0)
                    )
                    t = lane_take(geo[ci + wi, cj + wj], mb) + shift
                    acc = jnp.where(wb == wi * 5 + wj, t, acc)
            parts.append(acc)
        parts.append(geo[ci + 2, cj + 2])
        pts = jnp.concatenate(parts, 1)
        cols = jnp.transpose(pts * scale)
        rows = pts * scale

        def block(a, b):
            dx = cols[128 * a : 128 * a + 128, 0:1] - rows[0:1, 128 * b : 128 * b + 128]
            dy = cols[128 * a : 128 * a + 128, 1:2] - rows[1:2, 128 * b : 128 * b + 128]
            s2 = dx * dx + dy * dy
            s = s2 * lax.rsqrt(jnp.maximum(s2, 1e-30))
            k = (1.0 + s) * jnp.exp(-s)
            if a == b:
                k = k + jnp.where(eye, pts[2:3, 128 * b : 128 * b + 128], 0.0)
            return k

        xw[c] = block(0, 0)
        cc[c, :128, :] = block(1, 0)
        cc[c, 128:, :] = block(2, 0)
        mid[c] = block(1, 1)
        tt[c, :, :128] = block(2, 1)
        tt[c, :, 128:] = block(2, 2)
        return 0

    lax.fori_loop(0, count, covariance, 0)
    def level1(q, _):
        cs = [4 * q + e for e in range(4)]
        w1 = [xw[c] for c in cs]
        p = [mm_nt(cc[c], w) for c, w in zip(cs, w1)]
        u = [mm_nt(a, a) for a in p]
        v = [mm_nn(a, w) for a, w in zip(p, w1)]
        for e, c in enumerate(cs):
            cc[c] = v[e]
            xw[c] = mid[c] - u[e][:128, :128]
            tt[c] = tt[c] - u[e][128:, :]
        return 0

    def level2(q, _):
        cs = [4 * q + e for e in range(4)]
        w2 = [xw[c] for c in cs]
        l32 = [mm_nt(tt[c, :, :128], w) for c, w in zip(cs, w2)]
        u = [mm_nt(a, a) for a in l32]
        v = [mm_nn(a, w) for a, w in zip(l32, w2)]
        for e, c in enumerate(cs):
            l32s[c] = v[e]
            xw[c] = tt[c, :, 128:] - u[e]
        return 0

    def level(b, _):
        inv_chol(xw, wp, count)

        @pl.when(b == 0)
        def _():
            lax.fori_loop(0, count // 4, level1, 0)

        @pl.when(b == 1)
        def _():
            lax.fori_loop(0, count // 4, level2, 0)

        return 0

    lax.fori_loop(0, 3, level, 0)

    def last(q, _):
        cs = [4 * q + e for e in range(4)]
        w3 = [xw[c] for c in cs]
        q2 = [l32s[c] for c in cs]
        q1 = [cc[c, 128:, :] - mm_nn(b, cc[c, :128, :]) for c, b in zip(cs, q2)]
        gb = [
            mm_nn(w, jnp.concatenate([a, b], 1)).astype(BF)
            for w, a, b in zip(w3, q1, q2)
        ]
        for e, c in enumerate(cs):
            w3_out[c] = w3[e]
            g_out[c] = gb[e]
        return 0

    lax.fori_loop(0, count // 4, last, 0)


VM = pl.BlockSpec(memory_space=pltpu.VMEM)
SM = pl.BlockSpec(memory_space=pltpu.SMEM)


def factor(first, length, nb, geo):
    return pl.pallas_call(
        factor_kernel,
        out_shape=(
            jax.ShapeDtypeStruct((16, 128, 256), BF),
            jax.ShapeDtypeStruct((16, 128, 128), F32),
        ),
        in_specs=[SM, SM, VM, VM],
        out_specs=(VM, VM),
        scratch_shapes=[
            pltpu.VMEM((16, 128, 128), F32),
            pltpu.VMEM((4, 32, 128), F32),
            pltpu.VMEM((16, 128, 128), F32),
            pltpu.VMEM((16, 256, 128), F32),
            pltpu.VMEM((16, 128, 256), F32),
            pltpu.VMEM((16, 128, 128), F32),
        ],
        compiler_params=pltpu.CompilerParams(vmem_limit_bytes=20 << 20),
        name="factor",
    )(first, length, nb, geo)


def whiten_kernel(first, nb, north, mid, south, g, w3, own, white, weights, term, tab, acc, lhs):
    ci = pl.program_id(0)

    @pl.when(ci == 0)
    def _():
        tab[0:2] = north[...]
        tab[2:6] = mid[...]
        tab[6:8] = south[...]
        for wi in range(5):
            for cj, q in ((0, 5), (1, 0), (2, 7), (3, 2)):
                lhs[wi, 128 * cj : 128 * cj + 128, 128 * q : 128 * q + 128] = jnp.zeros((128, 128), BF)

    point = lax.broadcasted_iota(jnp.int32, (128, 256), 0)
    for cj in range(4):
        _, _, w, member = window(first, nb, 4 * ci + cj)
        here = point == jnp.broadcast_to(member, (128, 256))
        odd = jnp.broadcast_to(w & 1, (128, 256)) == 1
        pick = jnp.concatenate(
            [
                jnp.where(here & ~odd, 1.0, 0.0).astype(BF),
                jnp.where(here & odd, 1.0, 0.0).astype(BF),
            ],
            0,
        )
        gf = g[cj].astype(F32)
        pair = w >> 1
        for p in range(13):
            s = dot(jnp.where(pair == p, gf, 0.0).astype(BF), pick, NT).astype(BF)
            for h in range(2):
                wi, wj = divmod(2 * p + h, 5)
                if wi < 5:
                    at = 128 * (cj + wj)
                    lhs[wi, 128 * cj : 128 * cj + 128, at : at + 128] = s[:, 128 * h : 128 * h + 128]
        acc[128 * cj : 128 * cj + 128, :] = mm_nt(w3[cj], own[0, :, 128 * cj : 128 * cj + 128])

    for wi in range(5):
        row = tab.at[ci + wi]
        both = dot(lhs[wi, :, 256:768], row[:, 256:768], NT)
        left = dot(lhs[wi, :256, :256], row[:, :256], NT)
        right = dot(lhs[wi, 256:, 768:], row[:, 768:], NT)
        acc[...] = acc[...] - both - jnp.concatenate([left, right], 0)
    weights[...] = acc[...].astype(BF)
    eye = (
        lax.broadcasted_iota(jnp.int32, (128, 128), 0)
        == lax.broadcasted_iota(jnp.int32, (128, 128), 1)
    )
    for cj in range(4):
        out = acc[128 * cj : 128 * cj + 128, :]
        white[cj] = out
        diag = jnp.sum(jnp.where(eye, w3[cj], 0.0), axis=0, keepdims=True)
        total = 0.5 * jnp.sum(out * out) - 256.0 * jnp.sum(jnp.log(diag))
        value = -total / 32768.0 - 0.5 * math.log(2.0 * math.pi)
        term[0, cj : cj + 1, :] = jnp.full((1, 128), value, F32)


def whiten(first, nb, pieces, g, w3, own):
    def whole(a):
        nd = a.ndim
        return pl.BlockSpec(a.shape, lambda s: (0,) * nd, pipeline_mode=pl.Buffered(1))

    return pl.pallas_call(
        whiten_kernel,
        grid=(4,),
        out_shape=(
            jax.ShapeDtypeStruct((16, 128, 256), F32),
            jax.ShapeDtypeStruct((2048, 256), BF),
            jax.ShapeDtypeStruct((4, 8, 128), F32),
        ),
        in_specs=[SM, whole(nb)]
        + [whole(p) for p in pieces]
        + [
            pl.BlockSpec((4, 128, 256), lambda s: (s, 0, 0)),
            pl.BlockSpec((4, 128, 128), lambda s: (s, 0, 0)),
            pl.BlockSpec((1, 256, 512), lambda s: (s, 0, 0)),
        ],
        out_specs=(
            pl.BlockSpec((4, 128, 256), lambda s: (s, 0, 0)),
            pl.BlockSpec((512, 256), lambda s: (s, 0)),
            pl.BlockSpec((1, 8, 128), lambda s: (s, 0, 0)),
        ),
        scratch_shapes=[pltpu.VMEM((8, 256, 1024), BF), pltpu.VMEM((512, 256), F32),
            pltpu.VMEM((5, 512, 1024), BF)],
        compiler_params=pltpu.CompilerParams(vmem_limit_bytes=24 << 20),
        name="whiten",
    )(first, nb, *pieces, g, w3, own)


LN2 = math.log(2.0)
TB = 1024
FAR = 1


def pieces3(x):
    a = x.astype(BF).astype(F32)
    r = x - a
    b = r.astype(BF).astype(F32)
    return a, b, r - b


def cross_kernel(loops, scale, tgt, pts, w, acc_in, out, rhs, total):
    def form(x, y, left):
        q = x * x + y * y
        qs = pieces3(q)
        ones = jnp.ones_like(x)
        xs, ys = pieces3(x), pieces3(y)
        m = -2.0 if left else 1.0
        rows = []
        for a, b in ((0, 0), (0, 1), (1, 0), (0, 2), (1, 1), (2, 0)):
            k = a if left else b
            rows += [xs[k] * m, ys[k] * m]
        rows += (list(qs) + [ones] * 3) if left else ([ones] * 3 + list(qs))
        rows += [jnp.zeros_like(x)] * 14
        return jnp.concatenate(rows, 0).astype(BF)

    @pl.when(pl.program_id(0) == 0)
    def _():
        rhs[...] = form(pts[0:1, :] * scale[0], pts[1:2, :] * scale[0], False)

    lhs = form(tgt[0, 0:1, :] * scale[0], tgt[0, 1:2, :] * scale[0], True)
    def chunk(at, acc):
        s2 = jnp.maximum(dot(lhs, rhs[:, pl.ds(at, 256)], TN), 1e-30)
        s = s2 * lax.rsqrt(s2)
        k = (1.0 + s * LN2) * jnp.exp2(-s)
        return acc + dot(k.astype(BF), w[pl.ds(at, 256), :], NN)

    acc = acc_in[...] if acc_in is not None else jnp.zeros((TB, 256), F32)
    per = 8 // loops
    if loops == 1:
        for e in range(8):
            acc = chunk(256 * e, acc)
        out[...] = acc.astype(out.dtype)
        return
    total[...] = acc

    def some(b, _):
        acc = total[...]
        for e in range(per):
            acc = chunk(pl.multiple_of((b * per + e) * 256, 256), acc)
        total[...] = acc
        return 0

    lax.fori_loop(0, loops, some, 0)
    out[...] = total[...].astype(out.dtype)


def cross(scale, tgt, pts, w, dtype, acc=None, skip=0, name="cross", loops=1):
    n = tgt.shape[0]
    if acc is None:
        kernel = lambda s, t, p, w, o, r, m: cross_kernel(loops, s, t, p, w, None, o, r, m)
    else:
        kernel = lambda *refs: cross_kernel(loops, *refs)
    return pl.pallas_call(
        kernel,
        grid=(n,),
        out_shape=jax.ShapeDtypeStruct((n * TB, 256), dtype),
        in_specs=[
            pl.BlockSpec(memory_space=pltpu.SMEM),
            pl.BlockSpec((1, 2, TB), lambda s: (s, 0, 0)),
            pl.BlockSpec((2, 2048), lambda s: (0, 0)),
            pl.BlockSpec((2048, 256), lambda s: (0, 0)),
        ]
        + ([] if acc is None else [pl.BlockSpec((TB, 256), lambda s: (skip + s, 0))]),
        out_specs=pl.BlockSpec((TB, 256), lambda s: (s, 0)),
        scratch_shapes=[pltpu.VMEM((32, 2048), BF), pltpu.VMEM((TB, 256), F32)],
        compiler_params=pltpu.CompilerParams(vmem_limit_bytes=24 << 20),
        name=name,
    )(scale, tgt, pts, w, *([] if acc is None else [acc]))


def sort_kernel(tile, spots, out, slot):
    t = tile[...]
    named = lax.broadcasted_iota(jnp.int32, (16, 512), 0) == jnp.broadcast_to(t, (16, 512))
    hot = jnp.where(named, 1.0, 0.0)
    before = lax.broadcasted_iota(jnp.int32, (512, 512), 0) < lax.broadcasted_iota(
        jnp.int32, (512, 512), 1
    )
    counts = dot(hot.astype(BF), jnp.where(before, 1.0, 0.0).astype(BF), NN)
    rank = jnp.sum(counts * hot, axis=0, keepdims=True).astype(jnp.int32)
    slot[...] = t * 64 + rank
    at = lax.broadcasted_iota(jnp.int32, (128, 512), 0) & 63
    place = jnp.where(at == jnp.broadcast_to(rank, (128, 512)), 1.0, 0.0).astype(BF)
    moved = []
    for i in range(2):
        parts = [hot * p for p in pieces3(spots[i : i + 1, :])]
        m = dot(jnp.concatenate(parts, 0).astype(BF), place, NT)
        moved.append(m[:16] + m[16:32] + m[32:48])
    lane = lax.broadcasted_iota(jnp.int32, (16, 128), 1)
    row = jnp.where(lane < 64, moved[0], moved[1])
    for g in range(16):
        out[g] = jnp.broadcast_to(row[g : g + 1, :], (8, 128))


def sort_targets(tile, spots):
    return pl.pallas_call(
        sort_kernel,
        out_shape=(
            jax.ShapeDtypeStruct((16, 8, 128), F32),
            jax.ShapeDtypeStruct((1, 512), jnp.int32),
        ),
        in_specs=[VM, VM],
        out_specs=(VM, VM),
        compiler_params=pltpu.CompilerParams(vmem_limit_bytes=8 << 20),
        name="sort_targets",
    )(tile, spots)


def sides(low, high, axis):
    count = lax.axis_size(axis)
    forward = [(i, i + 1) for i in range(count - 1)]
    backward = [(b, a) for a, b in forward]
    return lax.ppermute(high, axis, forward), lax.ppermute(low, axis, backward)


def body(values, offsets, nugget, neighbours, length_scale, target_tile, target_spots):
    row = lax.axis_index("rows")
    col = lax.axis_index("cols")
    length = length_scale[0]
    first = jnp.stack([row * 4, col * 4]).astype(jnp.int32)

    geo = jnp.concatenate(
        [offsets.transpose(1, 2, 0, 3), nugget[:, :, None, :], jnp.zeros((4, 4, 5, 128), F32)], 2
    )
    w, e = sides(geo, geo, "cols")
    partner_geo = jnp.where(col % 2 == 0, e, w)
    geo = jnp.concatenate([w[:, 2:], geo, e[:, :2]], 1)
    n, s = sides(geo[:2], geo[2:], "rows")
    geo = jnp.concatenate([n, geo, s], 0)

    own = values.transpose(1, 0, 2, 3).reshape(4, 256, 512)
    mid = own.astype(BF)
    w, e = sides(mid[:, :, :256], mid[:, :, 256:], "cols")

    everyone, slot = sort_targets(target_tile.reshape(1, 512), target_spots)
    everyone = everyone.reshape(128, 1, 128)
    spots = lax.all_to_all(everyone, ("rows", "cols"), split_axis=0, concat_axis=0, tiled=True)
    spots = spots.reshape(16, 8, 2, 64).transpose(1, 2, 0, 3).reshape(4, 2, 2, 1024)
    band, half = col // 2, col % 2
    spots = lax.dynamic_index_in_dim(spots, half, 1, keepdims=False)
    spots = jnp.take(spots, (band + jnp.array([2, 1, 3, 0], jnp.int32)) % 4, axis=0)
    mid_y = (band * 8 + 4).astype(F32)
    tgt = jnp.stack([spots[:, 0] * 4.0 - 2.0, spots[:, 1] * 32.0 - mid_y], 1)
    tgt = tgt.reshape(4, 2, 1024 // TB, TB).transpose(0, 2, 1, 3).reshape(-1, 2, TB)
    px = offsets[0] + (jnp.arange(4, dtype=F32) - 2.0)[:, None, None]
    py = offsets[1] + (jnp.arange(4, dtype=F32) - 4.0 + 4.0 * half.astype(F32))[None, :, None]
    pts = jnp.stack([px.reshape(-1), py.reshape(-1)])
    partner = [(c, c ^ 1) for c in range(8)]
    px = partner_geo[:, :, 0] + (jnp.arange(4, dtype=F32) - 2.0)[:, None, None]
    py = partner_geo[:, :, 1] + (jnp.arange(4, dtype=F32) - 4.0 * half.astype(F32))[None, :, None]
    pts2 = jnp.stack([px.reshape(-1), py.reshape(-1)])

    first, w, e = lax.optimization_barrier((first, w, e))
    mid = jnp.concatenate([w, mid, e], 2)
    n, s = sides(mid[:2], mid[2:], "rows")
    around = [n, mid, s]
    g, w3 = factor(first, length_scale, neighbours, geo)
    white, weights, term = whiten(first, neighbours, around, g, w3, own)
    scale = jnp.stack([math.sqrt(3.0) / LN2 / length])
    weights2 = lax.ppermute(weights, "cols", partner)
    near = cross(scale, tgt, pts, weights, F32, name="cross_near")
    per = 1024 // TB
    parts = []
    for i, k in enumerate((2, 1, 3)):
        part = cross(
            scale, tgt[per * i : per * i + per], pts2, weights2, BF, near, per * i, "cross_far", FAR
        )
        parts.append(lax.ppermute(part, "cols", [(c, (c + 2 * k) % 8) for c in range(8)]))
    here = cross(scale, tgt[3 * per :], pts2, weights2, F32, near, 3 * per, "cross_here", 2)
    predicted = here + (parts[0].astype(F32) + parts[1].astype(F32) + parts[2].astype(F32))
    predicted = (predicted * (1.0 / 128.0)).astype(BF)
    returned = lax.all_to_all(
        predicted.reshape(16, 64, 256), "rows", split_axis=0, concat_axis=0, tiled=True
    )
    predictions = returned.reshape(-1, 256)[slot.reshape(512)].astype(F32)
    return (white.reshape(4, 4, 128, 256), term[:, :4, 0], predictions)


def solution(mesh):
    return jax.shard_map(
        body,
        mesh=mesh,
        in_specs=(
            P(None, "rows", "cols", None),
            P(None, "rows", "cols", None),
            P("rows", "cols", None),
            P("rows", "cols", None),
            P(),
            P(("rows", "cols"), None),
            P(None, ("rows", "cols")),
        ),
        out_specs=(P("rows", "cols", None, None), P("rows", "cols"), P(("rows", "cols"), None)),
        check_vma=False,
    )
```

```python
import math

import jax
import jax.numpy as jnp

from jax import lax
from jax.experimental import pallas as pl
from jax.experimental.pallas import tpu as pltpu
from jax.sharding import PartitionSpec as P

F32 = jnp.float32
BF = jnp.bfloat16
NN = (((1,), (0,)), ((), ()))
NT = (((1,), (1,)), ((), ()))
TN = (((0,), (0,)), ((), ()))


def split(x):
    hi = x.astype(BF)
    return hi, (x - hi.astype(F32)).astype(BF)


def dot(a, b, dims):
    return lax.dot_general(a, b, dims, preferred_element_type=F32)


def mm_nt(a, b):
    ah, al = split(a)
    bh, bl = split(b)
    return dot(jnp.concatenate([ah, ah, al], 1), jnp.concatenate([bh, bl, bh], 1), NT)


def mm_nn(a, b):
    ah, al = split(a)
    bh, bl = split(b)
    return dot(jnp.concatenate([ah, ah, al], 1), jnp.concatenate([bh, bl, bh], 0), NN)


def lane_take(x, idx):
    return jnp.take_along_axis(x, idx, axis=1, mode="promise_in_bounds")


def recip(p):
    r = pl.reciprocal(p, approx=True)
    return r * (2.0 - p * r)


def leaf_factor(leaf, lane, sub):
    base = lane & 96
    col = lane & 31
    x = [list(p) for p in leaf]
    ones = jnp.ones((8, 128), F32)
    piv = [[[ones, jnp.zeros((8, 128), F32), ones] for _ in range(4)] for _ in range(4)]

    def spread_row(t, s):
        return jnp.broadcast_to(t[s : s + 1, :], (8, 128))

    for j in range(0, 32, 2):
        v0, s0 = divmod(j, 8)
        first, second = base + j, base + j + 1
        unit0 = jnp.where(col == j, 1.0, 0.0)
        unit1 = jnp.where(col == j + 1, 1.0, 0.0)
        below = sub > s0 + 1
        here = (sub == s0) | (sub == s0 + 1)
        for p in range(4):
            c0 = [lane_take(x[p][v], first) for v in range(v0, 4)]
            c1 = [lane_take(x[p][v], second) for v in range(v0, 4)]
            a, b, d = spread_row(c0[0], s0), spread_row(c0[0], s0 + 1), spread_row(c1[0], s0 + 1)
            r = recip(a * d - b * b)
            r0 = spread_row(x[p][v0], s0) + unit0
            r1 = spread_row(x[p][v0], s0 + 1) + unit1
            w0 = d * r0 - b * r1
            w1 = a * r1 - b * r0
            for i, new in enumerate((a, b, d)):
                piv[p][v0][i] = jnp.where(here, new, piv[p][v0][i])
            for v in range(v0, 4):
                if v == v0 and s0 == 6:
                    continue
                t = c0[v - v0] * w0 + c1[v - v0] * w1
                if v == v0:
                    t = jnp.where(below, t, 0.0)
                x[p][v] = x[p][v] - t * r
    odd = (sub & 1) == 1
    out = []
    for p in range(4):
        o = []
        for v in range(4):
            a, b, d = piv[p][v]
            f = jnp.where(odd, b * recip(a), 0.0)
            e = jnp.where(odd, d - b * f, a)
            q = lax.rsqrt(e)
            q = q * (1.5 - 0.5 * e * q * q)
            r_i = sub + 8 * v
            n = jnp.where(col < (r_i & 30), x[p][v], jnp.where(col == r_i, 1.0, 0.0))
            o.append(q * (n - f * pltpu.roll(n, 1, axis=0)))
        out.append(o)
    return out


def inv_chol(xw, wp, count):
    lane8 = lax.broadcasted_iota(jnp.int32, (8, 128), 1)
    sub8 = lax.broadcasted_iota(jnp.int32, (8, 128), 0)
    lane = lax.broadcasted_iota(jnp.int32, (32, 128), 1)
    subl = lax.broadcasted_iota(jnp.int32, (32, 128), 0)
    for k in range(4):
        lo = 32 * k
        for base in range(0, count, 16):
            leaf = []
            for p in range(4):
                tiles = []
                for v in range(4):
                    acc = None
                    for g in range(4):
                        t = xw[base + 4 * p + g, lo + 8 * v : lo + 8 * v + 8, :]
                        t = pltpu.roll(t, (32 * (g - k)) % 128, axis=1) if g != k else t
                        acc = t if acc is None else jnp.where(lane8 // 32 == g, t, acc)
                    tiles.append(acc)
                leaf.append(tiles)
            inv = leaf_factor(leaf, lane8, sub8)
            for p in range(4):
                for v in range(4):
                    wp[p, 8 * v : 8 * v + 8, :] = inv[p][v]

            def apply(q, _):
                cs = [base + 8 * q + e for e in range(8)]
                xs = [xw[c] for c in cs]
                ws = [wp[2 * q], wp[2 * q + 1]]
                ts = []
                for e in range(8):
                    g = e % 4
                    gi = 32 * g + (lane8 & 31)
                    w = ws[e // 4]
                    wr = jnp.concatenate(
                        [lane_take(w[8 * v : 8 * v + 8], gi) for v in range(4)], 0
                    )
                    wh = wr.astype(BF).astype(F32)
                    lhs = jnp.where(lane < 64, wh, wr - wh).astype(BF)
                    r = xs[e][lo : lo + 32, :]
                    r = jnp.where(lane // 32 == k, jnp.where((lane & 31) == subl, 1.0, 0.0), r)
                    rh, rl = split(r)
                    ts.append(dot(lhs, jnp.concatenate([rh, rl, rh, rl], 0), NN))
                if k < 3:
                    n = 96 - lo
                    ln = lax.broadcasted_iota(jnp.int32, (n, 128), 1)
                    ls = []
                    for e in range(8):
                        g = e % 4
                        w = ws[e // 4]
                        w = pltpu.roll(w, (32 * (k - g)) % 128, axis=1) if g != k else w
                        w = jnp.where(lane // 32 == k, w, 0.0)
                        wh, wl = split(w)
                        wh = jnp.concatenate([wh] * 4, 0)
                        wl = jnp.concatenate([wl] * 4, 0)
                        xh, xl = split(xs[e][lo + 32 :, :])
                        ls.append(
                            dot(
                                jnp.concatenate([xh, xl, xh], 1),
                                jnp.concatenate([wh, wh, wl], 1),
                                NT,
                            )
                        )
                    us = []
                    for e in range(8):
                        lh = ls[e].astype(BF).astype(F32)
                        lhs = jnp.where(ln < 64, lh, ls[e] - lh).astype(BF)
                        th, tl = split(ts[e])
                        us.append(dot(lhs, jnp.concatenate([th, tl, th, tl], 0), NN))
                for e in range(8):
                    c = cs[e]
                    xw[c, lo : lo + 32, :] = jnp.where(lane < lo + 32, ts[e], 0.0)
                    if k < 3:
                        rest = xs[e][lo + 32 :, :]
                        xw[c, lo + 32 :, :] = jnp.where(ln // 32 == k, 0.0, rest) - us[e]
                return 0

            lax.fori_loop(0, 2, apply, 0)


def window(first, nb, c):
    ci, cj = c // 4, c % 4
    idx = nb[ci, pl.ds(cj, 1), :]
    gx = idx >> 12
    gy = (idx >> 7) & 31
    w = (gx - (first[0] + ci) + 2) * 5 + (gy - (first[1] + cj) + 2)
    return ci, cj, w, idx & 127


def factor_kernel(first, length, nb, geo, g_out, w3_out, xw, wp, mid, cc, tt, l32s):
    count = 16
    lane8 = lax.broadcasted_iota(jnp.int32, (8, 128), 1)
    sub8 = lax.broadcasted_iota(jnp.int32, (8, 128), 0)
    scale = math.sqrt(3.0) / length[0]
    eye = (
        lax.broadcasted_iota(jnp.int32, (128, 128), 0)
        == lax.broadcasted_iota(jnp.int32, (128, 128), 1)
    )

    def covariance(c, _):
        ci, cj, w, member = window(first, nb, c)
        parts = []
        for h in range(2):
            wb = jnp.broadcast_to(w[:, 128 * h : 128 * h + 128], (8, 128))
            mb = jnp.broadcast_to(member[:, 128 * h : 128 * h + 128], (8, 128))
            acc = jnp.zeros((8, 128), F32)
            for wi in range(5):
                for wj in range(5):
                    if wi == 2 and wj == 2:
                        continue
                    shift = jnp.where(
                        sub8 == 0, float(wi - 2), jnp.where(sub8 == 1, float(wj - 2), 0.0)
                    )
                    t = lane_take(geo[ci + wi, cj + wj], mb) + shift
                    acc = jnp.where(wb == wi * 5 + wj, t, acc)
            parts.append(acc)
        parts.append(geo[ci + 2, cj + 2])
        pts = jnp.concatenate(parts, 1)
        cols = jnp.transpose(pts * scale)
        rows = pts * scale

        def block(a, b):
            dx = cols[128 * a : 128 * a + 128, 0:1] - rows[0:1, 128 * b : 128 * b + 128]
            dy = cols[128 * a : 128 * a + 128, 1:2] - rows[1:2, 128 * b : 128 * b + 128]
            s2 = dx * dx + dy * dy
            s = s2 * lax.rsqrt(jnp.maximum(s2, 1e-30))
            k = (1.0 + s) * jnp.exp(-s)
            if a == b:
                k = k + jnp.where(eye, pts[2:3, 128 * b : 128 * b + 128], 0.0)
            return k

        xw[c] = block(0, 0)
        cc[c, :128, :] = block(1, 0)
        cc[c, 128:, :] = block(2, 0)
        mid[c] = block(1, 1)
        tt[c, :, :128] = block(2, 1)
        tt[c, :, 128:] = block(2, 2)
        return 0

    lax.fori_loop(0, count, covariance, 0)
    def level1(q, _):
        cs = [4 * q + e for e in range(4)]
        w1 = [xw[c] for c in cs]
        p = [mm_nt(cc[c], w) for c, w in zip(cs, w1)]
        u = [mm_nt(a, a) for a in p]
        v = [mm_nn(a, w) for a, w in zip(p, w1)]
        for e, c in enumerate(cs):
            cc[c] = v[e]
            xw[c] = mid[c] - u[e][:128, :128]
            tt[c] = tt[c] - u[e][128:, :]
        return 0

    def level2(q, _):
        cs = [4 * q + e for e in range(4)]
        w2 = [xw[c] for c in cs]
        l32 = [mm_nt(tt[c, :, :128], w) for c, w in zip(cs, w2)]
        u = [mm_nt(a, a) for a in l32]
        v = [mm_nn(a, w) for a, w in zip(l32, w2)]
        for e, c in enumerate(cs):
            l32s[c] = v[e]
            xw[c] = tt[c, :, 128:] - u[e]
        return 0

    def level(b, _):
        inv_chol(xw, wp, count)

        @pl.when(b == 0)
        def _():
            lax.fori_loop(0, count // 4, level1, 0)

        @pl.when(b == 1)
        def _():
            lax.fori_loop(0, count // 4, level2, 0)

        return 0

    lax.fori_loop(0, 3, level, 0)

    def last(q, _):
        cs = [4 * q + e for e in range(4)]
        w3 = [xw[c] for c in cs]
        q2 = [l32s[c] for c in cs]
        q1 = [cc[c, 128:, :] - mm_nn(b, cc[c, :128, :]) for c, b in zip(cs, q2)]
        gb = [
            mm_nn(w, jnp.concatenate([a, b], 1)).astype(BF)
            for w, a, b in zip(w3, q1, q2)
        ]
        for e, c in enumerate(cs):
            w3_out[c] = w3[e]
            g_out[c] = gb[e]
        return 0

    lax.fori_loop(0, count // 4, last, 0)


VM = pl.BlockSpec(memory_space=pltpu.VMEM)
SM = pl.BlockSpec(memory_space=pltpu.SMEM)


def factor(first, length, nb, geo):
    return pl.pallas_call(
        factor_kernel,
        out_shape=(
            jax.ShapeDtypeStruct((16, 128, 256), BF),
            jax.ShapeDtypeStruct((16, 128, 128), F32),
        ),
        in_specs=[SM, SM, VM, VM],
        out_specs=(VM, VM),
        scratch_shapes=[
            pltpu.VMEM((16, 128, 128), F32),
            pltpu.VMEM((4, 32, 128), F32),
            pltpu.VMEM((16, 128, 128), F32),
            pltpu.VMEM((16, 256, 128), F32),
            pltpu.VMEM((16, 128, 256), F32),
            pltpu.VMEM((16, 128, 128), F32),
        ],
        compiler_params=pltpu.CompilerParams(vmem_limit_bytes=20 << 20),
        name="factor",
    )(first, length, nb, geo)


def whiten_kernel(first, nb, north, mid, south, g, w3, own, white, weights, term, tab, acc, lhs):
    ci = pl.program_id(0)

    @pl.when(ci == 0)
    def _():
        tab[0:2] = north[...]
        tab[2:6] = mid[...]
        tab[6:8] = south[...]
        for wi in range(5):
            for cj, q in ((0, 5), (1, 0), (2, 7), (3, 2)):
                lhs[wi, 128 * cj : 128 * cj + 128, 128 * q : 128 * q + 128] = jnp.zeros((128, 128), BF)

    point = lax.broadcasted_iota(jnp.int32, (128, 256), 0)
    for cj in range(4):
        _, _, w, member = window(first, nb, 4 * ci + cj)
        here = point == jnp.broadcast_to(member, (128, 256))
        odd = jnp.broadcast_to(w & 1, (128, 256)) == 1
        pick = jnp.concatenate(
            [
                jnp.where(here & ~odd, 1.0, 0.0).astype(BF),
                jnp.where(here & odd, 1.0, 0.0).astype(BF),
            ],
            0,
        )
        gf = g[cj].astype(F32)
        pair = w >> 1
        for p in range(13):
            s = dot(jnp.where(pair == p, gf, 0.0).astype(BF), pick, NT).astype(BF)
            for h in range(2):
                wi, wj = divmod(2 * p + h, 5)
                if wi < 5:
                    at = 128 * (cj + wj)
                    lhs[wi, 128 * cj : 128 * cj + 128, at : at + 128] = s[:, 128 * h : 128 * h + 128]
        acc[128 * cj : 128 * cj + 128, :] = mm_nt(w3[cj], own[0, :, 128 * cj : 128 * cj + 128])

    for wi in range(5):
        row = tab.at[ci + wi]
        both = dot(lhs[wi, :, 256:768], row[:, 256:768], NT)
        left = dot(lhs[wi, :256, :256], row[:, :256], NT)
        right = dot(lhs[wi, 256:, 768:], row[:, 768:], NT)
        acc[...] = acc[...] - both - jnp.concatenate([left, right], 0)
    weights[...] = acc[...].astype(BF)
    eye = (
        lax.broadcasted_iota(jnp.int32, (128, 128), 0)
        == lax.broadcasted_iota(jnp.int32, (128, 128), 1)
    )
    for cj in range(4):
        out = acc[128 * cj : 128 * cj + 128, :]
        white[cj] = out
        diag = jnp.sum(jnp.where(eye, w3[cj], 0.0), axis=0, keepdims=True)
        total = 0.5 * jnp.sum(out * out) - 256.0 * jnp.sum(jnp.log(diag))
        value = -total / 32768.0 - 0.5 * math.log(2.0 * math.pi)
        term[0, cj : cj + 1, :] = jnp.full((1, 128), value, F32)


def whiten(first, nb, pieces, g, w3, own):
    def whole(a):
        nd = a.ndim
        return pl.BlockSpec(a.shape, lambda s: (0,) * nd, pipeline_mode=pl.Buffered(1))

    return pl.pallas_call(
        whiten_kernel,
        grid=(4,),
        out_shape=(
            jax.ShapeDtypeStruct((16, 128, 256), F32),
            jax.ShapeDtypeStruct((2048, 256), BF),
            jax.ShapeDtypeStruct((4, 8, 128), F32),
        ),
        in_specs=[SM, whole(nb)]
        + [whole(p) for p in pieces]
        + [
            pl.BlockSpec((4, 128, 256), lambda s: (s, 0, 0)),
            pl.BlockSpec((4, 128, 128), lambda s: (s, 0, 0)),
            pl.BlockSpec((1, 256, 512), lambda s: (s, 0, 0)),
        ],
        out_specs=(
            pl.BlockSpec((4, 128, 256), lambda s: (s, 0, 0)),
            pl.BlockSpec((512, 256), lambda s: (s, 0)),
            pl.BlockSpec((1, 8, 128), lambda s: (s, 0, 0)),
        ),
        scratch_shapes=[pltpu.VMEM((8, 256, 1024), BF), pltpu.VMEM((512, 256), F32),
            pltpu.VMEM((5, 512, 1024), BF)],
        compiler_params=pltpu.CompilerParams(vmem_limit_bytes=24 << 20),
        name="whiten",
    )(first, nb, *pieces, g, w3, own)


LN2 = math.log(2.0)
TB = 1024
FAR = 1


def pieces3(x):
    a = x.astype(BF).astype(F32)
    r = x - a
    b = r.astype(BF).astype(F32)
    return a, b, r - b


def cross_kernel(loops, scale, tgt, pts, w, acc_in, out, rhs, total):
    def form(x, y, left):
        q = x * x + y * y
        qs = pieces3(q)
        ones = jnp.ones_like(x)
        xs, ys = pieces3(x), pieces3(y)
        m = -2.0 if left else 1.0
        rows = []
        for a, b in ((0, 0), (0, 1), (1, 0), (0, 2), (1, 1), (2, 0)):
            k = a if left else b
            rows += [xs[k] * m, ys[k] * m]
        rows += (list(qs) + [ones] * 3) if left else ([ones] * 3 + list(qs))
        rows += [jnp.zeros_like(x)] * 14
        return jnp.concatenate(rows, 0).astype(BF)

    @pl.when(pl.program_id(0) == 0)
    def _():
        rhs[...] = form(pts[0:1, :] * scale[0], pts[1:2, :] * scale[0], False)

    lhs = form(tgt[0, 0:1, :] * scale[0], tgt[0, 1:2, :] * scale[0], True)
    def chunk(at, acc):
        s2 = jnp.maximum(dot(lhs, rhs[:, pl.ds(at, 256)], TN), 1e-30)
        s = s2 * lax.rsqrt(s2)
        k = (1.0 + s * LN2) * jnp.exp2(-s)
        return acc + dot(k.astype(BF), w[pl.ds(at, 256), :], NN)

    acc = acc_in[...] if acc_in is not None else jnp.zeros((TB, 256), F32)
    per = 8 // loops
    if loops == 1:
        for e in range(8):
            acc = chunk(256 * e, acc)
        out[...] = acc.astype(out.dtype)
        return
    total[...] = acc

    def some(b, _):
        acc = total[...]
        for e in range(per):
            acc = chunk(pl.multiple_of((b * per + e) * 256, 256), acc)
        total[...] = acc
        return 0

    lax.fori_loop(0, loops, some, 0)
    out[...] = total[...].astype(out.dtype)


def cross(scale, tgt, pts, w, dtype, acc=None, skip=0, name="cross", loops=1):
    n = tgt.shape[0]
    if acc is None:
        kernel = lambda s, t, p, w, o, r, m: cross_kernel(loops, s, t, p, w, None, o, r, m)
    else:
        kernel = lambda *refs: cross_kernel(loops, *refs)
    return pl.pallas_call(
        kernel,
        grid=(n,),
        out_shape=jax.ShapeDtypeStruct((n * TB, 256), dtype),
        in_specs=[
            pl.BlockSpec(memory_space=pltpu.SMEM),
            pl.BlockSpec((1, 2, TB), lambda s: (s, 0, 0)),
            pl.BlockSpec((2, 2048), lambda s: (0, 0)),
            pl.BlockSpec((2048, 256), lambda s: (0, 0)),
        ]
        + ([] if acc is None else [pl.BlockSpec((TB, 256), lambda s: (skip + s, 0))]),
        out_specs=pl.BlockSpec((TB, 256), lambda s: (s, 0)),
        scratch_shapes=[pltpu.VMEM((32, 2048), BF), pltpu.VMEM((TB, 256), F32)],
        compiler_params=pltpu.CompilerParams(vmem_limit_bytes=24 << 20),
        name=name,
    )(scale, tgt, pts, w, *([] if acc is None else [acc]))


def sort_kernel(tile, spots, out, slot):
    t = tile[...]
    named = lax.broadcasted_iota(jnp.int32, (16, 512), 0) == jnp.broadcast_to(t, (16, 512))
    hot = jnp.where(named, 1.0, 0.0)
    before = lax.broadcasted_iota(jnp.int32, (512, 512), 0) < lax.broadcasted_iota(
        jnp.int32, (512, 512), 1
    )
    counts = dot(hot.astype(BF), jnp.where(before, 1.0, 0.0).astype(BF), NN)
    rank = jnp.sum(counts * hot, axis=0, keepdims=True).astype(jnp.int32)
    slot[...] = t * 64 + rank
    at = lax.broadcasted_iota(jnp.int32, (128, 512), 0) & 63
    place = jnp.where(at == jnp.broadcast_to(rank, (128, 512)), 1.0, 0.0).astype(BF)
    moved = []
    for i in range(2):
        parts = [hot * p for p in pieces3(spots[i : i + 1, :])]
        m = dot(jnp.concatenate(parts, 0).astype(BF), place, NT)
        moved.append(m[:16] + m[16:32] + m[32:48])
    lane = lax.broadcasted_iota(jnp.int32, (16, 128), 1)
    row = jnp.where(lane < 64, moved[0], moved[1])
    for g in range(16):
        out[g] = jnp.broadcast_to(row[g : g + 1, :], (8, 128))


def sort_targets(tile, spots):
    return pl.pallas_call(
        sort_kernel,
        out_shape=(
            jax.ShapeDtypeStruct((16, 8, 128), F32),
            jax.ShapeDtypeStruct((1, 512), jnp.int32),
        ),
        in_specs=[VM, VM],
        out_specs=(VM, VM),
        compiler_params=pltpu.CompilerParams(vmem_limit_bytes=8 << 20),
        name="sort_targets",
    )(tile, spots)


def sides(low, high, axis):
    count = lax.axis_size(axis)
    forward = [(i, i + 1) for i in range(count - 1)]
    backward = [(b, a) for a, b in forward]
    return lax.ppermute(high, axis, forward), lax.ppermute(low, axis, backward)


def body(values, offsets, nugget, neighbours, length_scale, target_tile, target_spots):
    row = lax.axis_index("rows")
    col = lax.axis_index("cols")
    length = length_scale[0]
    first = jnp.stack([row * 4, col * 4]).astype(jnp.int32)

    geo = jnp.concatenate(
        [offsets.transpose(1, 2, 0, 3), nugget[:, :, None, :], jnp.zeros((4, 4, 5, 128), F32)], 2
    )
    w, e = sides(geo, geo, "cols")
    partner_geo = jnp.where(col % 2 == 0, e, w)
    geo = jnp.concatenate([w[:, 2:], geo, e[:, :2]], 1)
    upper, lower = geo[:2], geo[2:]
    target_spots, upper, lower = lax.optimization_barrier((target_spots, upper, lower))
    north, south = sides(upper, lower, "rows")

    own = values.transpose(1, 0, 2, 3).reshape(4, 256, 512)
    mid = own.astype(BF)
    w, e = sides(mid[:, :, :256], mid[:, :, 256:], "cols")

    everyone, slot = sort_targets(target_tile.reshape(1, 512), target_spots)
    everyone = everyone.reshape(128, 1, 128)
    spots = lax.all_to_all(everyone, ("rows", "cols"), split_axis=0, concat_axis=0, tiled=True)
    first, w, e, north, south, spots = lax.optimization_barrier((first, w, e, north, south, spots))
    spots = spots.reshape(16, 8, 2, 64).transpose(1, 2, 0, 3).reshape(4, 2, 2, 1024)
    band, half = col // 2, col % 2
    spots = lax.dynamic_index_in_dim(spots, half, 1, keepdims=False)
    spots = jnp.take(spots, (band + jnp.array([2, 1, 3, 0], jnp.int32)) % 4, axis=0)
    mid_y = (band * 8 + 4).astype(F32)
    tgt = jnp.stack([spots[:, 0] * 4.0 - 2.0, spots[:, 1] * 32.0 - mid_y], 1)
    tgt = tgt.reshape(4, 2, 1024 // TB, TB).transpose(0, 2, 1, 3).reshape(-1, 2, TB)
    px = offsets[0] + (jnp.arange(4, dtype=F32) - 2.0)[:, None, None]
    py = offsets[1] + (jnp.arange(4, dtype=F32) - 4.0 + 4.0 * half.astype(F32))[None, :, None]
    pts = jnp.stack([px.reshape(-1), py.reshape(-1)])
    partner = [(c, c ^ 1) for c in range(8)]
    px = partner_geo[:, :, 0] + (jnp.arange(4, dtype=F32) - 2.0)[:, None, None]
    py = partner_geo[:, :, 1] + (jnp.arange(4, dtype=F32) - 4.0 * half.astype(F32))[None, :, None]
    pts2 = jnp.stack([px.reshape(-1), py.reshape(-1)])

    geo = jnp.concatenate([north, geo, south], 0)
    mid = jnp.concatenate([w, mid, e], 2)
    n, s = sides(mid[:2], mid[2:], "rows")
    around = [n, mid, s]
    g, w3 = factor(first, length_scale, neighbours, geo)
    white, weights, term = whiten(first, neighbours, around, g, w3, own)
    scale = jnp.stack([math.sqrt(3.0) / LN2 / length])
    weights2 = lax.ppermute(weights, "cols", partner)
    near = cross(scale, tgt, pts, weights, F32, name="cross_near")
    per = 1024 // TB
    parts = []
    for i, k in enumerate((2, 1, 3)):
        part = cross(
            scale, tgt[per * i : per * i + per], pts2, weights2, BF, near, per * i, "cross_far", FAR
        )
        parts.append(lax.ppermute(part, "cols", [(c, (c + 2 * k) % 8) for c in range(8)]))
    here = cross(scale, tgt[3 * per :], pts2, weights2, F32, near, 3 * per, "cross_here", 2)
    predicted = here + (parts[0].astype(F32) + parts[1].astype(F32) + parts[2].astype(F32))
    predicted = (predicted * (1.0 / 128.0)).astype(BF)
    returned = lax.all_to_all(
        predicted.reshape(16, 64, 256), "rows", split_axis=0, concat_axis=0, tiled=True
    )
    predictions = returned.reshape(-1, 256)[slot.reshape(512)].astype(F32)
    return (white.reshape(4, 4, 128, 256), term[:, :4, 0], predictions)


def solution(mesh):
    return jax.shard_map(
        body,
        mesh=mesh,
        in_specs=(
            P(None, "rows", "cols", None),
            P(None, "rows", "cols", None),
            P("rows", "cols", None),
            P("rows", "cols", None),
            P(),
            P(("rows", "cols"), None),
            P(None, ("rows", "cols")),
        ),
        out_specs=(P("rows", "cols", None, None), P("rows", "cols"), P(("rows", "cols"), None)),
        check_vma=False,
    )
```

```python
import math

import jax
import jax.numpy as jnp

from jax import lax
from jax.experimental import pallas as pl
from jax.experimental.pallas import tpu as pltpu
from jax.sharding import PartitionSpec as P

F32 = jnp.float32
BF = jnp.bfloat16
NN = (((1,), (0,)), ((), ()))
NT = (((1,), (1,)), ((), ()))
TN = (((0,), (0,)), ((), ()))


def split(x):
    hi = x.astype(BF)
    return hi, (x - hi.astype(F32)).astype(BF)


def dot(a, b, dims):
    return lax.dot_general(a, b, dims, preferred_element_type=F32)


def mm_nt(a, b):
    ah, al = split(a)
    bh, bl = split(b)
    return dot(jnp.concatenate([ah, ah, al], 1), jnp.concatenate([bh, bl, bh], 1), NT)


def mm_nn(a, b):
    ah, al = split(a)
    bh, bl = split(b)
    return dot(jnp.concatenate([ah, ah, al], 1), jnp.concatenate([bh, bl, bh], 0), NN)


def lane_take(x, idx):
    return jnp.take_along_axis(x, idx, axis=1, mode="promise_in_bounds")


def recip(p):
    r = pl.reciprocal(p, approx=True)
    return r * (2.0 - p * r)


def leaf_factor(leaf, lane, sub):
    base = lane & 96
    col = lane & 31
    x = [list(p) for p in leaf]
    ones = jnp.ones((8, 128), F32)
    piv = [[[ones, jnp.zeros((8, 128), F32), ones] for _ in range(4)] for _ in range(4)]

    def spread_row(t, s):
        return jnp.broadcast_to(t[s : s + 1, :], (8, 128))

    for j in range(0, 32, 2):
        v0, s0 = divmod(j, 8)
        first, second = base + j, base + j + 1
        unit0 = jnp.where(col == j, 1.0, 0.0)
        unit1 = jnp.where(col == j + 1, 1.0, 0.0)
        below = sub > s0 + 1
        here = (sub == s0) | (sub == s0 + 1)
        for p in range(4):
            c0 = [lane_take(x[p][v], first) for v in range(v0, 4)]
            c1 = [lane_take(x[p][v], second) for v in range(v0, 4)]
            a, b, d = spread_row(c0[0], s0), spread_row(c0[0], s0 + 1), spread_row(c1[0], s0 + 1)
            r = recip(a * d - b * b)
            r0 = spread_row(x[p][v0], s0) + unit0
            r1 = spread_row(x[p][v0], s0 + 1) + unit1
            w0 = d * r0 - b * r1
            w1 = a * r1 - b * r0
            for i, new in enumerate((a, b, d)):
                piv[p][v0][i] = jnp.where(here, new, piv[p][v0][i])
            for v in range(v0, 4):
                if v == v0 and s0 == 6:
                    continue
                t = c0[v - v0] * w0 + c1[v - v0] * w1
                if v == v0:
                    t = jnp.where(below, t, 0.0)
                x[p][v] = x[p][v] - t * r
    odd = (sub & 1) == 1
    out = []
    for p in range(4):
        o = []
        for v in range(4):
            a, b, d = piv[p][v]
            f = jnp.where(odd, b * recip(a), 0.0)
            e = jnp.where(odd, d - b * f, a)
            q = lax.rsqrt(e)
            q = q * (1.5 - 0.5 * e * q * q)
            r_i = sub + 8 * v
            n = jnp.where(col < (r_i & 30), x[p][v], jnp.where(col == r_i, 1.0, 0.0))
            o.append(q * (n - f * pltpu.roll(n, 1, axis=0)))
        out.append(o)
    return out


def inv_chol(xw, wp, count):
    lane8 = lax.broadcasted_iota(jnp.int32, (8, 128), 1)
    sub8 = lax.broadcasted_iota(jnp.int32, (8, 128), 0)
    lane = lax.broadcasted_iota(jnp.int32, (32, 128), 1)
    subl = lax.broadcasted_iota(jnp.int32, (32, 128), 0)
    for k in range(4):
        lo = 32 * k
        for base in range(0, count, 16):
            leaf = []
            for p in range(4):
                tiles = []
                for v in range(4):
                    acc = None
                    for g in range(4):
                        t = xw[base + 4 * p + g, lo + 8 * v : lo + 8 * v + 8, :]
                        t = pltpu.roll(t, (32 * (g - k)) % 128, axis=1) if g != k else t
                        acc = t if acc is None else jnp.where(lane8 // 32 == g, t, acc)
                    tiles.append(acc)
                leaf.append(tiles)
            inv = leaf_factor(leaf, lane8, sub8)
            for p in range(4):
                for v in range(4):
                    wp[p, 8 * v : 8 * v + 8, :] = inv[p][v]

            def apply(q, _):
                cs = [base + 8 * q + e for e in range(8)]
                xs = [xw[c] for c in cs]
                ws = [wp[2 * q], wp[2 * q + 1]]
                ts = []
                for e in range(8):
                    g = e % 4
                    gi = 32 * g + (lane8 & 31)
                    w = ws[e // 4]
                    wr = jnp.concatenate(
                        [lane_take(w[8 * v : 8 * v + 8], gi) for v in range(4)], 0
                    )
                    wh = wr.astype(BF).astype(F32)
                    lhs = jnp.where(lane < 64, wh, wr - wh).astype(BF)
                    r = xs[e][lo : lo + 32, :]
                    r = jnp.where(lane // 32 == k, jnp.where((lane & 31) == subl, 1.0, 0.0), r)
                    rh, rl = split(r)
                    ts.append(dot(lhs, jnp.concatenate([rh, rl, rh, rl], 0), NN))
                if k < 3:
                    n = 96 - lo
                    ln = lax.broadcasted_iota(jnp.int32, (n, 128), 1)
                    ls = []
                    for e in range(8):
                        g = e % 4
                        w = ws[e // 4]
                        w = pltpu.roll(w, (32 * (k - g)) % 128, axis=1) if g != k else w
                        w = jnp.where(lane // 32 == k, w, 0.0)
                        wh, wl = split(w)
                        wh = jnp.concatenate([wh] * 4, 0)
                        wl = jnp.concatenate([wl] * 4, 0)
                        xh, xl = split(xs[e][lo + 32 :, :])
                        ls.append(
                            dot(
                                jnp.concatenate([xh, xl, xh], 1),
                                jnp.concatenate([wh, wh, wl], 1),
                                NT,
                            )
                        )
                    us = []
                    for e in range(8):
                        lh = ls[e].astype(BF).astype(F32)
                        lhs = jnp.where(ln < 64, lh, ls[e] - lh).astype(BF)
                        th, tl = split(ts[e])
                        us.append(dot(lhs, jnp.concatenate([th, tl, th, tl], 0), NN))
                for e in range(8):
                    c = cs[e]
                    xw[c, lo : lo + 32, :] = jnp.where(lane < lo + 32, ts[e], 0.0)
                    if k < 3:
                        rest = xs[e][lo + 32 :, :]
                        xw[c, lo + 32 :, :] = jnp.where(ln // 32 == k, 0.0, rest) - us[e]
                return 0

            lax.fori_loop(0, 2, apply, 0)


def window(first, nb, c):
    ci, cj = c // 4, c % 4
    idx = nb[ci, pl.ds(cj, 1), :]
    gx = idx >> 12
    gy = (idx >> 7) & 31
    w = (gx - (first[0] + ci) + 2) * 5 + (gy - (first[1] + cj) + 2)
    return ci, cj, w, idx & 127


def factor_kernel(first, length, nb, geo, g_out, w3_out, xw, wp, mid, cc, tt, l32s):
    count = 16
    lane8 = lax.broadcasted_iota(jnp.int32, (8, 128), 1)
    sub8 = lax.broadcasted_iota(jnp.int32, (8, 128), 0)
    scale = math.sqrt(3.0) / length[0]
    eye = (
        lax.broadcasted_iota(jnp.int32, (128, 128), 0)
        == lax.broadcasted_iota(jnp.int32, (128, 128), 1)
    )

    def covariance(c, _):
        ci, cj, w, member = window(first, nb, c)
        parts = []
        for h in range(2):
            wb = jnp.broadcast_to(w[:, 128 * h : 128 * h + 128], (8, 128))
            mb = jnp.broadcast_to(member[:, 128 * h : 128 * h + 128], (8, 128))
            acc = jnp.zeros((8, 128), F32)
            for wi in range(5):
                for wj in range(5):
                    if wi == 2 and wj == 2:
                        continue
                    shift = jnp.where(
                        sub8 == 0, float(wi - 2), jnp.where(sub8 == 1, float(wj - 2), 0.0)
                    )
                    t = lane_take(geo[ci + wi, cj + wj], mb) + shift
                    acc = jnp.where(wb == wi * 5 + wj, t, acc)
            parts.append(acc)
        parts.append(geo[ci + 2, cj + 2])
        pts = jnp.concatenate(parts, 1)
        cols = jnp.transpose(pts * scale)
        rows = pts * scale

        def block(a, b):
            dx = cols[128 * a : 128 * a + 128, 0:1] - rows[0:1, 128 * b : 128 * b + 128]
            dy = cols[128 * a : 128 * a + 128, 1:2] - rows[1:2, 128 * b : 128 * b + 128]
            s2 = dx * dx + dy * dy
            s = s2 * lax.rsqrt(jnp.maximum(s2, 1e-30))
            k = (1.0 + s) * jnp.exp(-s)
            if a == b:
                k = k + jnp.where(eye, pts[2:3, 128 * b : 128 * b + 128], 0.0)
            return k

        xw[c] = block(0, 0)
        cc[c, :128, :] = block(1, 0)
        cc[c, 128:, :] = block(2, 0)
        mid[c] = block(1, 1)
        tt[c, :, :128] = block(2, 1)
        tt[c, :, 128:] = block(2, 2)
        return 0

    lax.fori_loop(0, count, covariance, 0)
    def level1(q, _):
        cs = [4 * q + e for e in range(4)]
        w1 = [xw[c] for c in cs]
        p = [mm_nt(cc[c], w) for c, w in zip(cs, w1)]
        u = [mm_nt(a, a) for a in p]
        v = [mm_nn(a, w) for a, w in zip(p, w1)]
        for e, c in enumerate(cs):
            cc[c] = v[e]
            xw[c] = mid[c] - u[e][:128, :128]
            tt[c] = tt[c] - u[e][128:, :]
        return 0

    def level2(q, _):
        cs = [4 * q + e for e in range(4)]
        w2 = [xw[c] for c in cs]
        l32 = [mm_nt(tt[c, :, :128], w) for c, w in zip(cs, w2)]
        u = [mm_nt(a, a) for a in l32]
        v = [mm_nn(a, w) for a, w in zip(l32, w2)]
        for e, c in enumerate(cs):
            l32s[c] = v[e]
            xw[c] = tt[c, :, 128:] - u[e]
        return 0

    def level(b, _):
        inv_chol(xw, wp, count)

        @pl.when(b == 0)
        def _():
            lax.fori_loop(0, count // 4, level1, 0)

        @pl.when(b == 1)
        def _():
            lax.fori_loop(0, count // 4, level2, 0)

        return 0

    lax.fori_loop(0, 3, level, 0)

    def last(q, _):
        cs = [4 * q + e for e in range(4)]
        w3 = [xw[c] for c in cs]
        q2 = [l32s[c] for c in cs]
        q1 = [cc[c, 128:, :] - mm_nn(b, cc[c, :128, :]) for c, b in zip(cs, q2)]
        gb = [
            mm_nn(w, jnp.concatenate([a, b], 1)).astype(BF)
            for w, a, b in zip(w3, q1, q2)
        ]
        for e, c in enumerate(cs):
            w3_out[c] = w3[e]
            g_out[c] = gb[e]
        return 0

    lax.fori_loop(0, count // 4, last, 0)


VM = pl.BlockSpec(memory_space=pltpu.VMEM)
SM = pl.BlockSpec(memory_space=pltpu.SMEM)


def factor(first, length, nb, geo):
    return pl.pallas_call(
        factor_kernel,
        out_shape=(
            jax.ShapeDtypeStruct((16, 128, 256), BF),
            jax.ShapeDtypeStruct((16, 128, 128), F32),
        ),
        in_specs=[SM, SM, VM, VM],
        out_specs=(VM, VM),
        scratch_shapes=[
            pltpu.VMEM((16, 128, 128), F32),
            pltpu.VMEM((4, 32, 128), F32),
            pltpu.VMEM((16, 128, 128), F32),
            pltpu.VMEM((16, 256, 128), F32),
            pltpu.VMEM((16, 128, 256), F32),
            pltpu.VMEM((16, 128, 128), F32),
        ],
        compiler_params=pltpu.CompilerParams(vmem_limit_bytes=20 << 20),
        name="factor",
    )(first, length, nb, geo)


def whiten_kernel(first, nb, north, upper, lower, south, g, w3, own, white, weights, term, tab, acc, lhs):
    ci = pl.program_id(0)

    @pl.when(ci == 0)
    def _():
        tab[0:2] = north[...]
        tab[2:4] = upper[...]
        tab[4:6] = lower[...]
        tab[6:8] = south[...]
        for wi in range(5):
            for cj, q in ((0, 5), (1, 0), (2, 7), (3, 2)):
                lhs[wi, 128 * cj : 128 * cj + 128, 128 * q : 128 * q + 128] = jnp.zeros((128, 128), BF)

    point = lax.broadcasted_iota(jnp.int32, (128, 256), 0)
    for cj in range(4):
        _, _, w, member = window(first, nb, 4 * ci + cj)
        here = point == jnp.broadcast_to(member, (128, 256))
        odd = jnp.broadcast_to(w & 1, (128, 256)) == 1
        pick = jnp.concatenate(
            [
                jnp.where(here & ~odd, 1.0, 0.0).astype(BF),
                jnp.where(here & odd, 1.0, 0.0).astype(BF),
            ],
            0,
        )
        gf = g[cj].astype(F32)
        pair = w >> 1
        for p in range(13):
            s = dot(jnp.where(pair == p, gf, 0.0).astype(BF), pick, NT).astype(BF)
            for h in range(2):
                wi, wj = divmod(2 * p + h, 5)
                if wi < 5:
                    at = 128 * (cj + wj)
                    lhs[wi, 128 * cj : 128 * cj + 128, at : at + 128] = s[:, 128 * h : 128 * h + 128]
        acc[128 * cj : 128 * cj + 128, :] = mm_nt(w3[cj], own[0, :, 128 * cj : 128 * cj + 128])

    for wi in range(5):
        row = tab.at[ci + wi]
        both = dot(lhs[wi, :, 256:768], row[:, 256:768], NT)
        left = dot(lhs[wi, :256, :256], row[:, :256], NT)
        right = dot(lhs[wi, 256:, 768:], row[:, 768:], NT)
        acc[...] = acc[...] - both - jnp.concatenate([left, right], 0)
    weights[...] = acc[...].astype(BF)
    eye = (
        lax.broadcasted_iota(jnp.int32, (128, 128), 0)
        == lax.broadcasted_iota(jnp.int32, (128, 128), 1)
    )
    for cj in range(4):
        out = acc[128 * cj : 128 * cj + 128, :]
        white[cj] = out
        diag = jnp.sum(jnp.where(eye, w3[cj], 0.0), axis=0, keepdims=True)
        total = 0.5 * jnp.sum(out * out) - 256.0 * jnp.sum(jnp.log(diag))
        value = -total / 32768.0 - 0.5 * math.log(2.0 * math.pi)
        term[0, cj : cj + 1, :] = jnp.full((1, 128), value, F32)


def whiten(first, nb, pieces, g, w3, own):
    def whole(a):
        nd = a.ndim
        return pl.BlockSpec(a.shape, lambda s: (0,) * nd, pipeline_mode=pl.Buffered(1))

    return pl.pallas_call(
        whiten_kernel,
        grid=(4,),
        out_shape=(
            jax.ShapeDtypeStruct((16, 128, 256), F32),
            jax.ShapeDtypeStruct((2048, 256), BF),
            jax.ShapeDtypeStruct((4, 8, 128), F32),
        ),
        in_specs=[SM, whole(nb)]
        + [whole(p) for p in pieces]
        + [
            pl.BlockSpec((4, 128, 256), lambda s: (s, 0, 0)),
            pl.BlockSpec((4, 128, 128), lambda s: (s, 0, 0)),
            pl.BlockSpec((1, 256, 512), lambda s: (s, 0, 0)),
        ],
        out_specs=(
            pl.BlockSpec((4, 128, 256), lambda s: (s, 0, 0)),
            pl.BlockSpec((512, 256), lambda s: (s, 0)),
            pl.BlockSpec((1, 8, 128), lambda s: (s, 0, 0)),
        ),
        scratch_shapes=[pltpu.VMEM((8, 256, 1024), BF), pltpu.VMEM((512, 256), F32),
            pltpu.VMEM((5, 512, 1024), BF)],
        compiler_params=pltpu.CompilerParams(vmem_limit_bytes=24 << 20),
        name="whiten",
    )(first, nb, *pieces, g, w3, own)


LN2 = math.log(2.0)
TB = 1024
FAR = 1


def pieces3(x):
    a = x.astype(BF).astype(F32)
    r = x - a
    b = r.astype(BF).astype(F32)
    return a, b, r - b


def cross_kernel(loops, scale, tgt, pts, w, acc_in, out, rhs, total):
    def form(x, y, left):
        q = x * x + y * y
        qs = pieces3(q)
        ones = jnp.ones_like(x)
        xs, ys = pieces3(x), pieces3(y)
        m = -2.0 if left else 1.0
        rows = []
        for a, b in ((0, 0), (0, 1), (1, 0), (0, 2), (1, 1), (2, 0)):
            k = a if left else b
            rows += [xs[k] * m, ys[k] * m]
        rows += (list(qs) + [ones] * 3) if left else ([ones] * 3 + list(qs))
        rows += [jnp.zeros_like(x)] * 14
        return jnp.concatenate(rows, 0).astype(BF)

    @pl.when(pl.program_id(0) == 0)
    def _():
        rhs[...] = form(pts[0:1, :] * scale[0], pts[1:2, :] * scale[0], False)

    lhs = form(tgt[0, 0:1, :] * scale[0], tgt[0, 1:2, :] * scale[0], True)
    def chunk(at, acc):
        s2 = jnp.maximum(dot(lhs, rhs[:, pl.ds(at, 256)], TN), 1e-30)
        s = s2 * lax.rsqrt(s2)
        k = (1.0 + s * LN2) * jnp.exp2(-s)
        return acc + dot(k.astype(BF), w[pl.ds(at, 256), :], NN)

    acc = acc_in[...] if acc_in is not None else jnp.zeros((TB, 256), F32)
    per = 8 // loops
    if loops == 1:
        for e in range(8):
            acc = chunk(256 * e, acc)
        out[...] = acc.astype(out.dtype)
        return
    total[...] = acc

    def some(b, _):
        acc = total[...]
        for e in range(per):
            acc = chunk(pl.multiple_of((b * per + e) * 256, 256), acc)
        total[...] = acc
        return 0

    lax.fori_loop(0, loops, some, 0)
    out[...] = total[...].astype(out.dtype)


def cross(scale, tgt, pts, w, dtype, acc=None, skip=0, name="cross", loops=1):
    n = tgt.shape[0]
    if acc is None:
        kernel = lambda s, t, p, w, o, r, m: cross_kernel(loops, s, t, p, w, None, o, r, m)
    else:
        kernel = lambda *refs: cross_kernel(loops, *refs)
    return pl.pallas_call(
        kernel,
        grid=(n,),
        out_shape=jax.ShapeDtypeStruct((n * TB, 256), dtype),
        in_specs=[
            pl.BlockSpec(memory_space=pltpu.SMEM),
            pl.BlockSpec((1, 2, TB), lambda s: (s, 0, 0)),
            pl.BlockSpec((2, 2048), lambda s: (0, 0)),
            pl.BlockSpec((2048, 256), lambda s: (0, 0)),
        ]
        + ([] if acc is None else [pl.BlockSpec((TB, 256), lambda s: (skip + s, 0))]),
        out_specs=pl.BlockSpec((TB, 256), lambda s: (s, 0)),
        scratch_shapes=[pltpu.VMEM((32, 2048), BF), pltpu.VMEM((TB, 256), F32)],
        compiler_params=pltpu.CompilerParams(vmem_limit_bytes=24 << 20),
        name=name,
    )(scale, tgt, pts, w, *([] if acc is None else [acc]))


def sort_kernel(tile, spots, out, slot):
    t = tile[...]
    named = lax.broadcasted_iota(jnp.int32, (16, 512), 0) == jnp.broadcast_to(t, (16, 512))
    hot = jnp.where(named, 1.0, 0.0)
    before = lax.broadcasted_iota(jnp.int32, (512, 512), 0) < lax.broadcasted_iota(
        jnp.int32, (512, 512), 1
    )
    counts = dot(hot.astype(BF), jnp.where(before, 1.0, 0.0).astype(BF), NN)
    rank = jnp.sum(counts * hot, axis=0, keepdims=True).astype(jnp.int32)
    slot[...] = t * 64 + rank
    at = lax.broadcasted_iota(jnp.int32, (128, 512), 0) & 63
    place = jnp.where(at == jnp.broadcast_to(rank, (128, 512)), 1.0, 0.0).astype(BF)
    moved = []
    for i in range(2):
        parts = [hot * p for p in pieces3(spots[i : i + 1, :])]
        m = dot(jnp.concatenate(parts, 0).astype(BF), place, NT)
        moved.append(m[:16] + m[16:32] + m[32:48])
    lane = lax.broadcasted_iota(jnp.int32, (16, 128), 1)
    row = jnp.where(lane < 64, moved[0], moved[1])
    for g in range(16):
        out[g] = jnp.broadcast_to(row[g : g + 1, :], (8, 128))


def sort_targets(tile, spots):
    return pl.pallas_call(
        sort_kernel,
        out_shape=(
            jax.ShapeDtypeStruct((16, 8, 128), F32),
            jax.ShapeDtypeStruct((1, 512), jnp.int32),
        ),
        in_specs=[VM, VM],
        out_specs=(VM, VM),
        compiler_params=pltpu.CompilerParams(vmem_limit_bytes=8 << 20),
        name="sort_targets",
    )(tile, spots)


def sides(low, high, axis):
    count = lax.axis_size(axis)
    forward = [(i, i + 1) for i in range(count - 1)]
    backward = [(b, a) for a, b in forward]
    return lax.ppermute(high, axis, forward), lax.ppermute(low, axis, backward)


def body(values, offsets, nugget, neighbours, length_scale, target_tile, target_spots):
    row = lax.axis_index("rows")
    col = lax.axis_index("cols")
    length = length_scale[0]
    first = jnp.stack([row * 4, col * 4]).astype(jnp.int32)

    geo = jnp.concatenate(
        [offsets.transpose(1, 2, 0, 3), nugget[:, :, None, :], jnp.zeros((4, 4, 5, 128), F32)], 2
    )
    w, e = sides(geo, geo, "cols")
    partner_geo = jnp.where(col % 2 == 0, e, w)
    geo = jnp.concatenate([w[:, 2:], geo, e[:, :2]], 1)
    upper, lower = geo[:2], geo[2:]
    target_spots, upper, lower = lax.optimization_barrier((target_spots, upper, lower))
    north, south = sides(upper, lower, "rows")

    own = values.transpose(1, 0, 2, 3).reshape(4, 256, 512)
    mid = own.astype(BF)
    w, e = sides(mid[:, :, :256], mid[:, :, 256:], "cols")

    everyone, slot = sort_targets(target_tile.reshape(1, 512), target_spots)
    everyone = everyone.reshape(128, 1, 128)
    spots = lax.all_to_all(everyone, ("rows", "cols"), split_axis=0, concat_axis=0, tiled=True)
    first, w, e, north, south, spots, own = lax.optimization_barrier(
        (first, w, e, north, south, spots, own)
    )
    spots = spots.reshape(16, 8, 2, 64).transpose(1, 2, 0, 3).reshape(4, 2, 2, 1024)
    band, half = col // 2, col % 2
    spots = lax.dynamic_index_in_dim(spots, half, 1, keepdims=False)
    spots = jnp.take(spots, (band + jnp.array([2, 1, 3, 0], jnp.int32)) % 4, axis=0)
    mid_y = (band * 8 + 4).astype(F32)
    tgt = jnp.stack([spots[:, 0] * 4.0 - 2.0, spots[:, 1] * 32.0 - mid_y], 1)
    tgt = tgt.reshape(4, 2, 1024 // TB, TB).transpose(0, 2, 1, 3).reshape(-1, 2, TB)
    px = offsets[0] + (jnp.arange(4, dtype=F32) - 2.0)[:, None, None]
    py = offsets[1] + (jnp.arange(4, dtype=F32) - 4.0 + 4.0 * half.astype(F32))[None, :, None]
    pts = jnp.stack([px.reshape(-1), py.reshape(-1)])
    partner = [(c, c ^ 1) for c in range(8)]
    px = partner_geo[:, :, 0] + (jnp.arange(4, dtype=F32) - 2.0)[:, None, None]
    py = partner_geo[:, :, 1] + (jnp.arange(4, dtype=F32) - 4.0 * half.astype(F32))[None, :, None]
    pts2 = jnp.stack([px.reshape(-1), py.reshape(-1)])

    geo = jnp.concatenate([north, geo, south], 0)
    upper = jnp.concatenate([w[:2], mid[:2], e[:2]], 2)
    lower = jnp.concatenate([w[2:], mid[2:], e[2:]], 2)
    n, s = sides(upper, lower, "rows")
    around = [n, upper, lower, s]
    g, w3 = factor(first, length_scale, neighbours, geo)
    white, weights, term = whiten(first, neighbours, around, g, w3, own)
    scale = jnp.stack([math.sqrt(3.0) / LN2 / length])
    weights2 = lax.ppermute(weights, "cols", partner)
    near = cross(scale, tgt, pts, weights, F32, name="cross_near")
    per = 1024 // TB
    parts = []
    for i, k in enumerate((2, 1, 3)):
        part = cross(
            scale, tgt[per * i : per * i + per], pts2, weights2, BF, near, per * i, "cross_far", FAR
        )
        parts.append(lax.ppermute(part, "cols", [(c, (c + 2 * k) % 8) for c in range(8)]))
    here = cross(scale, tgt[3 * per :], pts2, weights2, F32, near, 3 * per, "cross_here", 2)
    predicted = here + (parts[0].astype(F32) + parts[1].astype(F32) + parts[2].astype(F32))
    predicted = (predicted * (1.0 / 128.0)).astype(BF)
    returned = lax.all_to_all(
        predicted.reshape(16, 64, 256), "rows", split_axis=0, concat_axis=0, tiled=True
    )
    predictions = returned.reshape(-1, 256)[slot.reshape(512)].astype(F32)
    return (white.reshape(4, 4, 128, 256), term[:, :4, 0], predictions)


def solution(mesh):
    return jax.shard_map(
        body,
        mesh=mesh,
        in_specs=(
            P(None, "rows", "cols", None),
            P(None, "rows", "cols", None),
            P("rows", "cols", None),
            P("rows", "cols", None),
            P(),
            P(("rows", "cols"), None),
            P(None, ("rows", "cols")),
        ),
        out_specs=(P("rows", "cols", None, None), P("rows", "cols"), P(("rows", "cols"), None)),
        check_vma=False,
    )
```

```python
import math

import jax
import jax.numpy as jnp

from jax import lax
from jax.experimental import pallas as pl
from jax.experimental.pallas import tpu as pltpu
from jax.sharding import PartitionSpec as P

F32 = jnp.float32
BF = jnp.bfloat16
NN = (((1,), (0,)), ((), ()))
NT = (((1,), (1,)), ((), ()))
TN = (((0,), (0,)), ((), ()))


def split(x):
    hi = x.astype(BF)
    return hi, (x - hi.astype(F32)).astype(BF)


def dot(a, b, dims):
    return lax.dot_general(a, b, dims, preferred_element_type=F32)


def mm_nt(a, b):
    ah, al = split(a)
    bh, bl = split(b)
    return dot(jnp.concatenate([ah, ah, al], 1), jnp.concatenate([bh, bl, bh], 1), NT)


def mm_nn(a, b):
    ah, al = split(a)
    bh, bl = split(b)
    return dot(jnp.concatenate([ah, ah, al], 1), jnp.concatenate([bh, bl, bh], 0), NN)


def lane_take(x, idx):
    return jnp.take_along_axis(x, idx, axis=1, mode="promise_in_bounds")


def recip(p):
    r = pl.reciprocal(p, approx=True)
    return r * (2.0 - p * r)


def leaf_factor(leaf, lane, sub):
    base = lane & 96
    col = lane & 31
    x = [list(p) for p in leaf]
    ones = jnp.ones((8, 128), F32)
    piv = [[[ones, jnp.zeros((8, 128), F32), ones] for _ in range(4)] for _ in range(4)]

    def spread_row(t, s):
        return jnp.broadcast_to(t[s : s + 1, :], (8, 128))

    for j in range(0, 32, 2):
        v0, s0 = divmod(j, 8)
        first, second = base + j, base + j + 1
        unit0 = jnp.where(col == j, 1.0, 0.0)
        unit1 = jnp.where(col == j + 1, 1.0, 0.0)
        below = sub > s0 + 1
        here = (sub == s0) | (sub == s0 + 1)
        for p in range(4):
            c0 = [lane_take(x[p][v], first) for v in range(v0, 4)]
            c1 = [lane_take(x[p][v], second) for v in range(v0, 4)]
            a, b, d = spread_row(c0[0], s0), spread_row(c0[0], s0 + 1), spread_row(c1[0], s0 + 1)
            r = recip(a * d - b * b)
            r0 = spread_row(x[p][v0], s0) + unit0
            r1 = spread_row(x[p][v0], s0 + 1) + unit1
            w0 = d * r0 - b * r1
            w1 = a * r1 - b * r0
            for i, new in enumerate((a, b, d)):
                piv[p][v0][i] = jnp.where(here, new, piv[p][v0][i])
            for v in range(v0, 4):
                if v == v0 and s0 == 6:
                    continue
                t = c0[v - v0] * w0 + c1[v - v0] * w1
                if v == v0:
                    t = jnp.where(below, t, 0.0)
                x[p][v] = x[p][v] - t * r
    odd = (sub & 1) == 1
    out = []
    for p in range(4):
        o = []
        for v in range(4):
            a, b, d = piv[p][v]
            f = jnp.where(odd, b * recip(a), 0.0)
            e = jnp.where(odd, d - b * f, a)
            q = lax.rsqrt(e)
            q = q * (1.5 - 0.5 * e * q * q)
            r_i = sub + 8 * v
            n = jnp.where(col < (r_i & 30), x[p][v], jnp.where(col == r_i, 1.0, 0.0))
            o.append(q * (n - f * pltpu.roll(n, 1, axis=0)))
        out.append(o)
    return out


def inv_chol(xw, wp, count):
    lane8 = lax.broadcasted_iota(jnp.int32, (8, 128), 1)
    sub8 = lax.broadcasted_iota(jnp.int32, (8, 128), 0)
    lane = lax.broadcasted_iota(jnp.int32, (32, 128), 1)
    subl = lax.broadcasted_iota(jnp.int32, (32, 128), 0)
    for k in range(4):
        lo = 32 * k
        for base in range(0, count, 16):
            leaf = []
            for p in range(4):
                tiles = []
                for v in range(4):
                    acc = None
                    for g in range(4):
                        t = xw[base + 4 * p + g, lo + 8 * v : lo + 8 * v + 8, :]
                        t = pltpu.roll(t, (32 * (g - k)) % 128, axis=1) if g != k else t
                        acc = t if acc is None else jnp.where(lane8 // 32 == g, t, acc)
                    tiles.append(acc)
                leaf.append(tiles)
            inv = leaf_factor(leaf, lane8, sub8)
            for p in range(4):
                for v in range(4):
                    wp[p, 8 * v : 8 * v + 8, :] = inv[p][v]

            def apply(q, _):
                cs = [base + 8 * q + e for e in range(8)]
                xs = [xw[c] for c in cs]
                ws = [wp[2 * q], wp[2 * q + 1]]
                ts = []
                for e in range(8):
                    g = e % 4
                    gi = 32 * g + (lane8 & 31)
                    w = ws[e // 4]
                    wr = jnp.concatenate(
                        [lane_take(w[8 * v : 8 * v + 8], gi) for v in range(4)], 0
                    )
                    wh = wr.astype(BF).astype(F32)
                    lhs = jnp.where(lane < 64, wh, wr - wh).astype(BF)
                    r = xs[e][lo : lo + 32, :]
                    r = jnp.where(lane // 32 == k, jnp.where((lane & 31) == subl, 1.0, 0.0), r)
                    rh, rl = split(r)
                    ts.append(dot(lhs, jnp.concatenate([rh, rl, rh, rl], 0), NN))
                if k < 3:
                    n = 96 - lo
                    ln = lax.broadcasted_iota(jnp.int32, (n, 128), 1)
                    ls = []
                    for e in range(8):
                        g = e % 4
                        w = ws[e // 4]
                        w = pltpu.roll(w, (32 * (k - g)) % 128, axis=1) if g != k else w
                        w = jnp.where(lane // 32 == k, w, 0.0)
                        wh, wl = split(w)
                        wh = jnp.concatenate([wh] * 4, 0)
                        wl = jnp.concatenate([wl] * 4, 0)
                        xh, xl = split(xs[e][lo + 32 :, :])
                        ls.append(
                            dot(
                                jnp.concatenate([xh, xl, xh], 1),
                                jnp.concatenate([wh, wh, wl], 1),
                                NT,
                            )
                        )
                    us = []
                    for e in range(8):
                        lh = ls[e].astype(BF).astype(F32)
                        lhs = jnp.where(ln < 64, lh, ls[e] - lh).astype(BF)
                        th, tl = split(ts[e])
                        us.append(dot(lhs, jnp.concatenate([th, tl, th, tl], 0), NN))
                for e in range(8):
                    c = cs[e]
                    xw[c, lo : lo + 32, :] = jnp.where(lane < lo + 32, ts[e], 0.0)
                    if k < 3:
                        rest = xs[e][lo + 32 :, :]
                        xw[c, lo + 32 :, :] = jnp.where(ln // 32 == k, 0.0, rest) - us[e]
                return 0

            lax.fori_loop(0, 2, apply, 0)


def window(first, nb, c):
    ci, cj = c // 4, c % 4
    idx = nb[ci, pl.ds(cj, 1), :]
    gx = idx >> 12
    gy = (idx >> 7) & 31
    w = (gx - (first[0] + ci) + 2) * 5 + (gy - (first[1] + cj) + 2)
    return ci, cj, w, idx & 127


def factor_kernel(first, length, nb, geo, g_out, w3_out, xw, wp, mid, cc, tt, l32s):
    count = 16
    lane8 = lax.broadcasted_iota(jnp.int32, (8, 128), 1)
    sub8 = lax.broadcasted_iota(jnp.int32, (8, 128), 0)
    scale = math.sqrt(3.0) / length[0]
    eye = (
        lax.broadcasted_iota(jnp.int32, (128, 128), 0)
        == lax.broadcasted_iota(jnp.int32, (128, 128), 1)
    )

    def covariance(c, _):
        ci, cj, w, member = window(first, nb, c)
        parts = []
        for h in range(2):
            wb = jnp.broadcast_to(w[:, 128 * h : 128 * h + 128], (8, 128))
            mb = jnp.broadcast_to(member[:, 128 * h : 128 * h + 128], (8, 128))
            acc = jnp.zeros((8, 128), F32)
            for wi in range(5):
                for wj in range(5):
                    if wi == 2 and wj == 2:
                        continue
                    shift = jnp.where(
                        sub8 == 0, float(wi - 2), jnp.where(sub8 == 1, float(wj - 2), 0.0)
                    )
                    t = lane_take(geo[ci + wi, cj + wj], mb) + shift
                    acc = jnp.where(wb == wi * 5 + wj, t, acc)
            parts.append(acc)
        parts.append(geo[ci + 2, cj + 2])
        pts = jnp.concatenate(parts, 1)
        cols = jnp.transpose(pts * scale)
        rows = pts * scale

        def block(a, b):
            dx = cols[128 * a : 128 * a + 128, 0:1] - rows[0:1, 128 * b : 128 * b + 128]
            dy = cols[128 * a : 128 * a + 128, 1:2] - rows[1:2, 128 * b : 128 * b + 128]
            s2 = dx * dx + dy * dy
            s = s2 * lax.rsqrt(jnp.maximum(s2, 1e-30))
            k = (1.0 + s) * jnp.exp(-s)
            if a == b:
                k = k + jnp.where(eye, pts[2:3, 128 * b : 128 * b + 128], 0.0)
            return k

        xw[c] = block(0, 0)
        cc[c, :128, :] = block(1, 0)
        cc[c, 128:, :] = block(2, 0)
        mid[c] = block(1, 1)
        tt[c, :, :128] = block(2, 1)
        tt[c, :, 128:] = block(2, 2)
        return 0

    lax.fori_loop(0, count, covariance, 0)
    def level1(q, _):
        cs = [4 * q + e for e in range(4)]
        w1 = [xw[c] for c in cs]
        p = [mm_nt(cc[c], w) for c, w in zip(cs, w1)]
        u = [mm_nt(a, a) for a in p]
        v = [mm_nn(a, w) for a, w in zip(p, w1)]
        for e, c in enumerate(cs):
            cc[c] = v[e]
            xw[c] = mid[c] - u[e][:128, :128]
            tt[c] = tt[c] - u[e][128:, :]
        return 0

    def level2(q, _):
        cs = [4 * q + e for e in range(4)]
        w2 = [xw[c] for c in cs]
        l32 = [mm_nt(tt[c, :, :128], w) for c, w in zip(cs, w2)]
        u = [mm_nt(a, a) for a in l32]
        v = [mm_nn(a, w) for a, w in zip(l32, w2)]
        for e, c in enumerate(cs):
            l32s[c] = v[e]
            xw[c] = tt[c, :, 128:] - u[e]
        return 0

    def level(b, _):
        inv_chol(xw, wp, count)

        @pl.when(b == 0)
        def _():
            lax.fori_loop(0, count // 4, level1, 0)

        @pl.when(b == 1)
        def _():
            lax.fori_loop(0, count // 4, level2, 0)

        return 0

    lax.fori_loop(0, 3, level, 0)

    def last(q, _):
        cs = [4 * q + e for e in range(4)]
        w3 = [xw[c] for c in cs]
        q2 = [l32s[c] for c in cs]
        q1 = [cc[c, 128:, :] - mm_nn(b, cc[c, :128, :]) for c, b in zip(cs, q2)]
        gb = [
            mm_nn(w, jnp.concatenate([a, b], 1)).astype(BF)
            for w, a, b in zip(w3, q1, q2)
        ]
        for e, c in enumerate(cs):
            w3_out[c] = w3[e]
            g_out[c] = gb[e]
        return 0

    lax.fori_loop(0, count // 4, last, 0)


VM = pl.BlockSpec(memory_space=pltpu.VMEM)
SM = pl.BlockSpec(memory_space=pltpu.SMEM)


def factor(first, length, nb, geo):
    return pl.pallas_call(
        factor_kernel,
        out_shape=(
            jax.ShapeDtypeStruct((16, 128, 256), BF),
            jax.ShapeDtypeStruct((16, 128, 128), F32),
        ),
        in_specs=[SM, SM, VM, VM],
        out_specs=(VM, VM),
        scratch_shapes=[
            pltpu.VMEM((16, 128, 128), F32),
            pltpu.VMEM((4, 32, 128), F32),
            pltpu.VMEM((16, 128, 128), F32),
            pltpu.VMEM((16, 256, 128), F32),
            pltpu.VMEM((16, 128, 256), F32),
            pltpu.VMEM((16, 128, 128), F32),
        ],
        compiler_params=pltpu.CompilerParams(vmem_limit_bytes=20 << 20),
        name="factor",
    )(first, length, nb, geo)


def whiten_kernel(first, nb, north, upper, lower, south, g, w3, own, white, weights, term, tab, acc, lhs):
    ci = pl.program_id(0)

    @pl.when(ci == 0)
    def _():
        tab[0:2] = north[...]
        tab[2:4] = upper[...]
        tab[4:6] = lower[...]
        tab[6:8] = south[...]
        for wi in range(5):
            for cj, q in ((0, 5), (1, 0), (2, 7), (3, 2)):
                lhs[wi, 128 * cj : 128 * cj + 128, 128 * q : 128 * q + 128] = jnp.zeros((128, 128), BF)

    point = lax.broadcasted_iota(jnp.int32, (128, 256), 0)
    for cj in range(4):
        _, _, w, member = window(first, nb, 4 * ci + cj)
        here = point == jnp.broadcast_to(member, (128, 256))
        odd = jnp.broadcast_to(w & 1, (128, 256)) == 1
        pick = jnp.concatenate(
            [
                jnp.where(here & ~odd, 1.0, 0.0).astype(BF),
                jnp.where(here & odd, 1.0, 0.0).astype(BF),
            ],
            0,
        )
        gf = g[cj].astype(F32)
        pair = w >> 1
        for p in range(13):
            s = dot(jnp.where(pair == p, gf, 0.0).astype(BF), pick, NT).astype(BF)
            for h in range(2):
                wi, wj = divmod(2 * p + h, 5)
                if wi < 5:
                    at = 128 * (cj + wj)
                    lhs[wi, 128 * cj : 128 * cj + 128, at : at + 128] = s[:, 128 * h : 128 * h + 128]
        acc[128 * cj : 128 * cj + 128, :] = mm_nt(w3[cj], own[0, :, 128 * cj : 128 * cj + 128])

    for wi in range(5):
        row = tab.at[ci + wi]
        both = dot(lhs[wi, :, 256:768], row[:, 256:768], NT)
        left = dot(lhs[wi, :256, :256], row[:, :256], NT)
        right = dot(lhs[wi, 256:, 768:], row[:, 768:], NT)
        acc[...] = acc[...] - both - jnp.concatenate([left, right], 0)
    weights[...] = acc[...].astype(BF)
    eye = (
        lax.broadcasted_iota(jnp.int32, (128, 128), 0)
        == lax.broadcasted_iota(jnp.int32, (128, 128), 1)
    )
    for cj in range(4):
        out = acc[128 * cj : 128 * cj + 128, :]
        white[cj] = out
        diag = jnp.sum(jnp.where(eye, w3[cj], 0.0), axis=0, keepdims=True)
        total = 0.5 * jnp.sum(out * out) - 256.0 * jnp.sum(jnp.log(diag))
        value = -total / 32768.0 - 0.5 * math.log(2.0 * math.pi)
        term[0, cj : cj + 1, :] = jnp.full((1, 128), value, F32)


def whiten(first, nb, pieces, g, w3, own):
    def whole(a):
        nd = a.ndim
        return pl.BlockSpec(a.shape, lambda s: (0,) * nd, pipeline_mode=pl.Buffered(1))

    return pl.pallas_call(
        whiten_kernel,
        grid=(4,),
        out_shape=(
            jax.ShapeDtypeStruct((16, 128, 256), F32),
            jax.ShapeDtypeStruct((2048, 256), BF),
            jax.ShapeDtypeStruct((4, 8, 128), F32),
        ),
        in_specs=[SM, whole(nb)]
        + [whole(p) for p in pieces]
        + [
            pl.BlockSpec((4, 128, 256), lambda s: (s, 0, 0)),
            pl.BlockSpec((4, 128, 128), lambda s: (s, 0, 0)),
            pl.BlockSpec((1, 256, 512), lambda s: (s, 0, 0)),
        ],
        out_specs=(
            pl.BlockSpec((4, 128, 256), lambda s: (s, 0, 0)),
            pl.BlockSpec((512, 256), lambda s: (s, 0)),
            pl.BlockSpec((1, 8, 128), lambda s: (s, 0, 0)),
        ),
        scratch_shapes=[pltpu.VMEM((8, 256, 1024), BF), pltpu.VMEM((512, 256), F32),
            pltpu.VMEM((5, 512, 1024), BF)],
        compiler_params=pltpu.CompilerParams(vmem_limit_bytes=24 << 20),
        name="whiten",
    )(first, nb, *pieces, g, w3, own)


LN2 = math.log(2.0)
TB = 1024
FAR = 1


def pieces3(x):
    a = x.astype(BF).astype(F32)
    r = x - a
    b = r.astype(BF).astype(F32)
    return a, b, r - b


def cross_kernel(loops, scale, tgt, pts, w, acc_in, out, rhs, total):
    def form(x, y, left):
        q = x * x + y * y
        qs = pieces3(q)
        ones = jnp.ones_like(x)
        xs, ys = pieces3(x), pieces3(y)
        m = -2.0 if left else 1.0
        rows = []
        for a, b in ((0, 0), (0, 1), (1, 0), (0, 2), (1, 1), (2, 0)):
            k = a if left else b
            rows += [xs[k] * m, ys[k] * m]
        rows += (list(qs) + [ones] * 3) if left else ([ones] * 3 + list(qs))
        rows += [jnp.zeros_like(x)] * 14
        return jnp.concatenate(rows, 0).astype(BF)

    @pl.when(pl.program_id(0) == 0)
    def _():
        rhs[...] = form(pts[0:1, :] * scale[0], pts[1:2, :] * scale[0], False)

    lhs = form(tgt[0, 0:1, :] * scale[0], tgt[0, 1:2, :] * scale[0], True)
    def chunk(at, acc):
        s2 = jnp.maximum(dot(lhs, rhs[:, pl.ds(at, 256)], TN), 1e-30)
        s = s2 * lax.rsqrt(s2)
        k = (1.0 + s * LN2) * jnp.exp2(-s)
        return acc + dot(k.astype(BF), w[pl.ds(at, 256), :], NN)

    acc = acc_in[...] if acc_in is not None else jnp.zeros((TB, 256), F32)
    per = 8 // loops
    if loops == 1:
        for e in range(8):
            acc = chunk(256 * e, acc)
        out[...] = acc.astype(out.dtype)
        return
    total[...] = acc

    def some(b, _):
        acc = total[...]
        for e in range(per):
            acc = chunk(pl.multiple_of((b * per + e) * 256, 256), acc)
        total[...] = acc
        return 0

    lax.fori_loop(0, loops, some, 0)
    out[...] = total[...].astype(out.dtype)


def cross(scale, tgt, pts, w, dtype, acc=None, skip=0, name="cross", loops=1):
    n = tgt.shape[0]
    if acc is None:
        kernel = lambda s, t, p, w, o, r, m: cross_kernel(loops, s, t, p, w, None, o, r, m)
    else:
        kernel = lambda *refs: cross_kernel(loops, *refs)
    return pl.pallas_call(
        kernel,
        grid=(n,),
        out_shape=jax.ShapeDtypeStruct((n * TB, 256), dtype),
        in_specs=[
            pl.BlockSpec(memory_space=pltpu.SMEM),
            pl.BlockSpec((1, 2, TB), lambda s: (s, 0, 0)),
            pl.BlockSpec((2, 2048), lambda s: (0, 0)),
            pl.BlockSpec((2048, 256), lambda s: (0, 0)),
        ]
        + ([] if acc is None else [pl.BlockSpec((TB, 256), lambda s: (skip + s, 0))]),
        out_specs=pl.BlockSpec((TB, 256), lambda s: (s, 0)),
        scratch_shapes=[pltpu.VMEM((32, 2048), BF), pltpu.VMEM((TB, 256), F32)],
        compiler_params=pltpu.CompilerParams(vmem_limit_bytes=24 << 20),
        name=name,
    )(scale, tgt, pts, w, *([] if acc is None else [acc]))


def sort_kernel(tile, spots, out, slot):
    t = tile[...]
    named = lax.broadcasted_iota(jnp.int32, (16, 512), 0) == jnp.broadcast_to(t, (16, 512))
    hot = jnp.where(named, 1.0, 0.0)
    before = lax.broadcasted_iota(jnp.int32, (512, 512), 0) < lax.broadcasted_iota(
        jnp.int32, (512, 512), 1
    )
    counts = dot(hot.astype(BF), jnp.where(before, 1.0, 0.0).astype(BF), NN)
    rank = jnp.sum(counts * hot, axis=0, keepdims=True).astype(jnp.int32)
    slot[...] = t * 64 + rank
    at = lax.broadcasted_iota(jnp.int32, (128, 512), 0) & 63
    place = jnp.where(at == jnp.broadcast_to(rank, (128, 512)), 1.0, 0.0).astype(BF)
    moved = []
    for i in range(2):
        parts = [hot * p for p in pieces3(spots[i : i + 1, :])]
        m = dot(jnp.concatenate(parts, 0).astype(BF), place, NT)
        moved.append(m[:16] + m[16:32] + m[32:48])
    lane = lax.broadcasted_iota(jnp.int32, (16, 128), 1)
    row = jnp.where(lane < 64, moved[0], moved[1])
    for g in range(16):
        out[g] = jnp.broadcast_to(row[g : g + 1, :], (8, 128))


def sort_targets(tile, spots):
    return pl.pallas_call(
        sort_kernel,
        out_shape=(
            jax.ShapeDtypeStruct((16, 8, 128), F32),
            jax.ShapeDtypeStruct((1, 512), jnp.int32),
        ),
        in_specs=[VM, VM],
        out_specs=(VM, VM),
        compiler_params=pltpu.CompilerParams(vmem_limit_bytes=8 << 20),
        name="sort_targets",
    )(tile, spots)


def sides(low, high, axis):
    count = lax.axis_size(axis)
    forward = [(i, i + 1) for i in range(count - 1)]
    backward = [(b, a) for a, b in forward]
    return lax.ppermute(high, axis, forward), lax.ppermute(low, axis, backward)


def body(values, offsets, nugget, neighbours, length_scale, target_tile, target_spots):
    row = lax.axis_index("rows")
    col = lax.axis_index("cols")
    length = length_scale[0]
    first = jnp.stack([row * 4, col * 4]).astype(jnp.int32)

    geo = jnp.concatenate(
        [offsets.transpose(1, 2, 0, 3), nugget[:, :, None, :], jnp.zeros((4, 4, 5, 128), F32)], 2
    )
    w, e = sides(geo, geo, "cols")
    partner_geo = jnp.where(col % 2 == 0, e, w)
    geo = jnp.concatenate([w[:, 2:], geo, e[:, :2]], 1)
    upper, lower = geo[:2], geo[2:]
    target_spots, upper, lower = lax.optimization_barrier((target_spots, upper, lower))
    north, south = sides(upper, lower, "rows")

    own = values.transpose(1, 0, 2, 3).reshape(4, 256, 512)
    mid = own.astype(BF)
    w, e = sides(mid[:, :, :256], mid[:, :, 256:], "cols")

    everyone, slot = sort_targets(target_tile.reshape(1, 512), target_spots)
    everyone = everyone.reshape(128, 1, 128)
    spots = lax.all_to_all(everyone, ("rows", "cols"), split_axis=0, concat_axis=0, tiled=True)
    first, w, e, north, south, spots, own = lax.optimization_barrier(
        (first, w, e, north, south, spots, own)
    )
    spots = spots.reshape(16, 8, 2, 64).transpose(1, 2, 0, 3).reshape(4, 2, 2, 1024)
    band, half = col // 2, col % 2
    spots = lax.dynamic_index_in_dim(spots, half, 1, keepdims=False)
    spots = jnp.take(spots, (band + jnp.array([1, 2, 3, 0], jnp.int32)) % 4, axis=0)
    mid_y = (band * 8 + 4).astype(F32)
    tgt = jnp.stack([spots[:, 0] * 4.0 - 2.0, spots[:, 1] * 32.0 - mid_y], 1)
    tgt = tgt.reshape(4, 2, 1024 // TB, TB).transpose(0, 2, 1, 3).reshape(-1, 2, TB)
    px = offsets[0] + (jnp.arange(4, dtype=F32) - 2.0)[:, None, None]
    py = offsets[1] + (jnp.arange(4, dtype=F32) - 4.0 + 4.0 * half.astype(F32))[None, :, None]
    pts = jnp.stack([px.reshape(-1), py.reshape(-1)])
    partner = [(c, c ^ 1) for c in range(8)]
    px = partner_geo[:, :, 0] + (jnp.arange(4, dtype=F32) - 2.0)[:, None, None]
    py = partner_geo[:, :, 1] + (jnp.arange(4, dtype=F32) - 4.0 * half.astype(F32))[None, :, None]
    pts2 = jnp.stack([px.reshape(-1), py.reshape(-1)])

    geo = jnp.concatenate([north, geo, south], 0)
    upper = jnp.concatenate([w[:2], mid[:2], e[:2]], 2)
    lower = jnp.concatenate([w[2:], mid[2:], e[2:]], 2)
    n, s = sides(upper, lower, "rows")
    around = [n, upper, lower, s]
    g, w3 = factor(first, length_scale, neighbours, geo)
    white, weights, term = whiten(first, neighbours, around, g, w3, own)
    scale = jnp.stack([math.sqrt(3.0) / LN2 / length])
    weights2 = lax.ppermute(weights, "cols", partner)
    near = cross(scale, tgt, pts, weights, F32, name="cross_near")
    per = 1024 // TB
    parts = []
    for i, k in enumerate((1, 2, 3)):
        part = cross(
            scale, tgt[per * i : per * i + per], pts2, weights2, BF, near, per * i, "cross_far", FAR
        )
        parts.append(lax.ppermute(part, "cols", [(c, (c + 2 * k) % 8) for c in range(8)]))
    here = cross(scale, tgt[3 * per :], pts2, weights2, F32, near, 3 * per, "cross_here", 2)
    predicted = here + (parts[0].astype(F32) + parts[1].astype(F32) + parts[2].astype(F32))
    predicted = (predicted * (1.0 / 128.0)).astype(BF)
    returned = lax.all_to_all(
        predicted.reshape(16, 64, 256), "rows", split_axis=0, concat_axis=0, tiled=True
    )
    predictions = returned.reshape(-1, 256)[slot.reshape(512)].astype(F32)
    return (white.reshape(4, 4, 128, 256), term[:, :4, 0], predictions)


def solution(mesh):
    return jax.shard_map(
        body,
        mesh=mesh,
        in_specs=(
            P(None, "rows", "cols", None),
            P(None, "rows", "cols", None),
            P("rows", "cols", None),
            P("rows", "cols", None),
            P(),
            P(("rows", "cols"), None),
            P(None, ("rows", "cols")),
        ),
        out_specs=(P("rows", "cols", None, None), P("rows", "cols"), P(("rows", "cols"), None)),
        check_vma=False,
    )
```
